256 devices in a mesh: seq: 16 (over x, y_hi, core), fsdp: 16 (over y_lo, z).
Axes of the slice: x: 4, y: 4 (y_hi: 2, y_lo: 2; y = y_hi * 2 + y_lo), z: 8, core: 2. Of those that a mesh axis runs over, the one named last changes fastest.
Arguments:
- tokens: bfloat16 [16384, 4096], P('seq', 'fsdp'), may hold values from -6 to 6
- norm_gain: bfloat16 [4096], replicated, may hold values from 0.25 to 1.75
- in_weight: bfloat16 [3, 4096, 4096], P(None, 'seq', 'fsdp'), may hold values from -0.09375 to 0.09375
- short_filter: bfloat16 [7, 3, 4096], P(None, None, 'fsdp'), may hold values from -2 to 2
- medium_filter: bfloat16 [128, 4096], P(None, 'fsdp'), may hold values from -0.5 to 0.5
- out_weight: bfloat16 [4096, 4096], P(None, ('fsdp', 'seq')), may hold values from -0.375 to 0.375
- genome_lengths: int32 [4], replicated, may hold values from 1 to 8192, 16384 in all
- block_at_slot: int32 [64], replicated, may hold values from 0 to 63, each once
Outputs:
- layer_out: bfloat16 [16384, 4096], P('seq', 'fsdp')
The draws below stay inside these ranges and needn't reach their ends.
Inputs may be any that keep to these rules, and one draw needn't show every extreme that they name: `genome_lengths`: the lengths sum to 16384. `block_at_slot`: every block number appears exactly once.
All inputs are finite; a program needn't handle non-finite values.
Results may differ from the reference program's by a relative error of at most 0.0087.
Values may be sent and summed in bfloat16 or wider, within the bound.
No kernel may reach another device: no remote copies, remote signals or barrier semaphores. Data moves between devices by JAX's collectives and lax.ppermute only.
A program may use at most 64 MiB of HBM per device.

```python
import math
import jax
import jax.numpy as jnp
import numpy as np
from jax import lax

D = 4096
C = 4096
SHORT = 7
MED = 128
BLK = 256
G = 4
NBLK = 64
TOKENS = 16384


def strengthened(entries, key, source, target, shards_of, factor):
    owner, partner = [(jnp.arange(entries.shape[dim]) // (entries.shape[dim] // shards_of)).reshape([-1 if axis == dim else 1 for axis in range(entries.ndim)]) for dim in (source, target)]
    chosen = jax.random.permutation(key, shards_of)[partner]
    strong = (owner == chosen) | (owner == (partner + shards_of // 2) % shards_of)
    return jnp.where(strong, factor * entries, entries)


def steps_of(rng, extent, split, smallest, high):
    def one(dim, blocks):
        draws = jax.random.uniform(jax.random.fold_in(jax.random.fold_in(rng, 6), dim), (blocks,), jnp.float32, smallest / len(split), high / len(split))
        return jnp.repeat(jnp.exp(draws), extent[dim] // blocks).reshape((-1,) + (1,) * (len(extent) - dim - 1))

    loudness = one(*split[0])
    for cut in split[1:]:
        loudness = loudness * one(*cut)
    return loudness


def profile(count, total, limit, lean):
    portions = [(1 << 20) // math.isqrt(standing ** lean) + 1 for standing in range(2, count + 1)]
    spare, given = total - limit - (count - 1), [1] * (count - 1)
    while spare > 0:
        free = [i for i in range(count - 1) if given[i] < limit]
        mass, budget = sum([portions[i] for i in free]), spare
        for i in free:
            extra = min(limit - given[i], max(1, budget * portions[i] // mass), spare)
            given[i] = given[i] + extra
            spare = spare - extra
    return np.array([limit] + given)


def ragged_sizes(rng, amount, total, reach, slope):
    if amount == 2:
        one = jax.random.randint(rng, (), max(1, total - reach), min(reach, total - 1) + 1)
        return jnp.stack([one, total - one])
    lengths = jnp.asarray(profile(amount, total, reach, slope), jnp.int32)
    couples = (amount - 1) // 2
    giver, taker = lengths[1:1 + 2 * couples:2], lengths[2:2 + 2 * couples:2]
    room = jnp.minimum(giver - 1, reach - taker)
    passed = jax.random.randint(jax.random.fold_in(rng, 1), (couples,), 0, 1 << 20) % (room + 1)
    lengths = lengths.at[1:1 + 2 * couples:2].set(giver - passed).at[2:2 + 2 * couples:2].set(taker + passed)
    return lengths[jax.random.permutation(jax.random.fold_in(rng, 2), amount)]


def gaussian(own_key, dims, spread, reach, shards=(), kind=jnp.bfloat16):
    array = spread * jax.random.normal(own_key, dims, jnp.float32)
    if shards:
        array = array * steps_of(own_key, dims, shards, -0.22, 0.18)
    return jnp.clip(array, -reach, reach).astype(kind)


def bell_draw_with(stream_key, dims, spread, reach, cuts, heavy, kind=jnp.bfloat16):
    array = spread * jax.random.normal(stream_key, dims, jnp.float32)
    if cuts:
        array = array * steps_of(stream_key, dims, cuts, -0.22, 0.18)
    return jnp.clip(strengthened(array, jax.random.fold_in(stream_key, 3), *heavy), -reach, reach).astype(kind)


def setup_inputs(seed: int = 0) -> dict:
    splits = jax.random.split(jax.random.key(seed), 9)
    tokens = gaussian(splits[0], (TOKENS, D), 1.0, 6.0, ((0, 16), (1, 16)))
    norm_gain = jnp.clip(1.0 + 0.15 * jax.random.normal(splits[1], (D,), jnp.float32), 0.25, 1.75).astype(jnp.bfloat16)
    in_weight = gaussian(splits[2], (3, D, C), D ** -0.5, 0.09375, ((1, 16), (2, 16)))
    short_filter = gaussian(splits[3], (SHORT, 3, C), SHORT ** -0.5, 2.0, ((2, 16),))
    medium_filter = gaussian(splits[4], (MED, C), MED ** -0.5, 0.5, ((1, 16),))
    out_weight = bell_draw_with(splits[5], (C, D), C ** -0.5, 0.375, ((1, 256),), (0, 1, 256, 6.0))
    genome_lengths = ragged_sizes(splits[6], G, TOKENS, TOKENS // 2, 2).astype(jnp.int32)
    block_at_slot = jax.random.permutation(splits[7], NBLK).astype(jnp.int32)
    return {"tokens": tokens, "norm_gain": norm_gain, "in_weight": in_weight, "short_filter": short_filter, "medium_filter": medium_filter, "out_weight": out_weight, "genome_lengths": genome_lengths, "block_at_slot": block_at_slot}


epsilon = 1e-06

def segment_ids(position, boundaries):
    counted = lax.optimization_barrier(jnp.sum((boundaries <= position[..., None]).astype(jnp.int32), axis=-1))
    return jnp.where(position < 0, -1, counted).astype(jnp.int32)

def reference(tokens, norm_gain, in_weight, short_filter, medium_filter, out_weight, genome_lengths, block_at_slot):
    slot_ids = jnp.arange(NBLK, dtype=jnp.int32)
    inverse = jnp.zeros((NBLK,), jnp.int32).at[block_at_slot].set(slot_ids)
    ordered = jnp.take(tokens.reshape(NBLK, BLK, D), inverse, axis=0).reshape(TOKENS, D)
    values = ordered.astype(jnp.float32)
    rescale = lax.rsqrt(lax.optimization_barrier(jnp.mean(values * values, axis=1, keepdims=True)) + epsilon)
    normed = (values * rescale * norm_gain.astype(jnp.float32)).astype(jnp.bfloat16)
    projected = jnp.stack([jnp.dot(normed, in_weight[branch], preferred_element_type=jnp.float32) for branch in range(3)], axis=1).astype(jnp.bfloat16)
    boundaries = jnp.cumsum(genome_lengths).astype(jnp.int32)
    position = jnp.arange(TOKENS, dtype=jnp.int32)
    segment = segment_ids(position, boundaries)
    short_reach = SHORT - 1
    padded = jnp.concatenate([jnp.zeros((short_reach, 3, C), jnp.bfloat16), projected], axis=0)
    padded_seg = segment_ids(jnp.arange(-short_reach, TOKENS, dtype=jnp.int32), boundaries)
    mixed = jnp.zeros((TOKENS, 3, C), jnp.float32)
    for tap_index in range(SHORT):
        offset = short_reach - tap_index
        matches = (padded_seg[offset:offset + TOKENS] == segment).astype(jnp.float32)
        mixed = mixed + padded[offset:offset + TOKENS].astype(jnp.float32) * matches[:, None, None] * short_filter[tap_index].astype(jnp.float32)
    gating = mixed[:, 0, :]
    product = (mixed[:, 1, :] * mixed[:, 2, :]).astype(jnp.bfloat16)
    medium_reach = MED - 1
    padded_prod = jnp.concatenate([jnp.zeros((medium_reach, C), jnp.float32), product.astype(jnp.float32)], axis=0)
    long_seg = segment_ids(jnp.arange(-medium_reach, TOKENS, dtype=jnp.int32), boundaries)
    tap_weights = medium_filter.astype(jnp.float32)

    def add_tap(tap_index, accumulated):
        offset = (medium_reach - tap_index).astype(jnp.int32)
        window = lax.dynamic_slice_in_dim(padded_prod, offset, TOKENS, 0)
        matches = lax.dynamic_slice_in_dim(long_seg, offset, TOKENS, 0) == segment
        weights = lax.dynamic_slice_in_dim(tap_weights, tap_index.astype(jnp.int32), 1, 0)
        return accumulated + jnp.where(matches[:, None], window, 0.0) * weights
    filtered = lax.fori_loop(0, MED, add_tap, jnp.zeros((TOKENS, C), jnp.float32))
    gated = (gating * filtered).astype(jnp.bfloat16)
    branch_out = jnp.dot(gated, out_weight, preferred_element_type=jnp.float32)
    result = (values + branch_out).astype(jnp.bfloat16)
    return jnp.take(result.reshape(NBLK, BLK, D), block_at_slot, axis=0).reshape(TOKENS, D)
```

```python
import functools

import jax
import jax.numpy as jnp
from jax import lax
from jax.experimental import pallas as pl
from jax.experimental.pallas import tpu as pltpu
from jax.sharding import PartitionSpec as P


BLK = 256
SHORT = 7
MED = 128
LANES = 128
TAIL = 8
HALF = 512
PIECE = 256
D = 4096
HALO = MED + 3 * TAIL
AXES = ("seq", "fsdp")
epsilon = 1e-06
OFFSETS = (0, -1, 1, -2, 2, -3, 3)


def linear(x, y, z, core):
    return (x * 4 + (y // 2) * 2 + core) * 16 + (y % 2) * 8 + z


def permutation(move):
    pairs = []
    for x in range(4):
        for y in range(4):
            for z in range(8):
                for core in range(2):
                    pairs.append((linear(x, y, z, core), linear(*move(x, y, z, core))))
    return pairs


def send(value, move):
    return lax.ppermute(value, AXES, permutation(move))


def along_z(step):
    return lambda x, y, z, core: (x, y, (z + step) % 8, core)


def swap_y(x, y, z, core):
    return (x, y ^ 1, z, core)


def swap_core(x, y, z, core):
    return (x, y, z, core ^ 1)


def ring_z(chunk):
    right, left = chunk, chunk
    whole = {0: chunk}
    for step in range(1, 4):
        right, left = send(right, along_z(1)), send(left, along_z(-1))
        whole[-step], whole[step] = right, left
    last = (send(right[0], along_z(1)), send(left[1], along_z(-1)))
    return whole, last


def plane_groups(with_core):
    groups = []
    for z in range(8):
        every = [
            [linear(x, y, z, core) for x in range(4) for y in range(4)] for core in range(2)
        ]
        if with_core:
            groups.append(sorted(every[0] + every[1]))
        else:
            groups += every
    return groups


def full():
    return pl.BlockSpec(memory_space=pltpu.VMEM)


def scalars():
    return pl.BlockSpec(memory_space=pltpu.SMEM)


def project_kernel(owner_ref, core_ref, rescale_ref, w_ref, *refs):
    pieces, (out_ref, x_scratch, w_scratch) = refs[:18], refs[18:]
    core = core_ref[0]
    for group in range(2):
        mine = pieces[group * 9 : group * 9 + 9]
        rows = pl.ds(group * HALF, HALF)
        for t in range(16):
            piece = mine[t // 2][t % 2] if t < 14 else mine[t - 7][...]
            x_scratch[rows, t * PIECE : (t + 1) * PIECE] = piece
    for branch in range(3):
        for t in range(16):
            owner = owner_ref[t]
            chip = (owner // 2) * 2
            other = lax.rem(owner + core, 2)
            for part in range(2):
                w_scratch[
                    t * PIECE : (t + 1) * PIECE, part * LANES : (part + 1) * LANES
                ] = w_ref[chip + part, other, branch]

        def rows_step(i, carry):
            rows = pl.ds(pl.multiple_of(i * BLK, BLK), BLK)
            product = jnp.dot(
                x_scratch[rows, :], w_scratch[...], preferred_element_type=jnp.float32
            )
            out_ref[branch, i] = (product * rescale_ref[rows, :]).astype(jnp.bfloat16)
            return carry

        lax.fori_loop(0, 4, rows_step, 0)


def project(owner, core, rescale, weights, pieces):
    return pl.pallas_call(
        project_kernel,
        out_shape=jax.ShapeDtypeStruct((3, 4, BLK, 2 * LANES), jnp.bfloat16),
        in_specs=[scalars(), scalars()] + [full()] * 20,
        out_specs=full(),
        scratch_shapes=[
            pltpu.VMEM((2 * HALF, D), jnp.bfloat16),
            pltpu.VMEM((D, 2 * LANES), jnp.bfloat16),
        ],
        compiler_params=pltpu.CompilerParams(vmem_limit_bytes=48 << 20),
        cost_estimate=pl.CostEstimate(
            flops=2 * 1024 * D * 768, bytes_accessed=16 << 20, transcendentals=0
        ),
        name="project",
    )(owner, core, rescale, weights, *pieces)


def reach_of(start, rows, ends_ref):
    position = start + lax.broadcasted_iota(jnp.int32, (rows, LANES), 0)
    first = jnp.zeros((rows, LANES), jnp.int32)
    for g in range(3):
        end = ends_ref[g]
        first = jnp.maximum(first, jnp.where(position >= end, end, 0))
    return position - first


def short_mix(window_ref, reach, taps_ref, branch, rows):
    total = jnp.zeros((rows, LANES), jnp.float32)
    for j in range(SHORT):
        part = window_ref[TAIL - j : TAIL - j + rows, :]
        part = jnp.where(reach >= j, part, 0.0)
        total = total + part * taps_ref[j, branch : branch + 1, :].astype(jnp.float32)
    return total


def tail_kernel(start_ref, ends_ref, proj_ref, taps_ref, out_ref, window):
    start = start_ref[pl.program_id(0)] + BLK - MED
    reach = reach_of(start, MED, ends_ref)
    mixes = []
    for branch in (1, 2):
        window[...] = proj_ref[branch, 0, BLK - MED - TAIL :, :].astype(jnp.float32)
        mixes.append(short_mix(window, reach, taps_ref, branch, MED))
    out_ref[0, :MED, :] = (mixes[0] * mixes[1]).astype(jnp.bfloat16)
    for branch in range(3):
        at = MED + branch * TAIL
        out_ref[0, at : at + TAIL, :] = proj_ref[branch, 0, BLK - TAIL :, :]


def tails(starts, ends, proj, taps):
    return pl.pallas_call(
        tail_kernel,
        grid_spec=pltpu.PrefetchScalarGridSpec(
            num_scalar_prefetch=2,
            grid=(4, 2),
            in_specs=[
                pl.BlockSpec((3, 1, BLK, LANES), lambda i, c, *_: (0, i, 0, c)),
                pl.BlockSpec((SHORT, 3, LANES), lambda i, c, *_: (0, 0, c)),
            ],
            out_specs=pl.BlockSpec((1, HALO, LANES), lambda i, c, *_: (i, 0, c)),
            scratch_shapes=[pltpu.VMEM((MED + TAIL, LANES), jnp.float32)],
        ),
        out_shape=jax.ShapeDtypeStruct((4, HALO, 2 * LANES), jnp.bfloat16),
        name="tails",
    )(starts, ends, proj, taps)


def filter_kernel(
    source_ref, start_ref, ends_ref, proj_ref, halo_ref, taps_ref, medium_ref, out_ref,
    window, product, shifted, filtered,
):
    start = start_ref[pl.program_id(0)]
    reach = reach_of(start, BLK, ends_ref)
    mixes = []
    for branch in range(3):
        at = MED + branch * TAIL
        window[:TAIL, :] = halo_ref[0, at : at + TAIL, :].astype(jnp.float32)
        window[TAIL:, :] = proj_ref[branch, 0].astype(jnp.float32)
        mixes.append(short_mix(window, reach, taps_ref, branch, BLK))
    product[:MED, :] = halo_ref[0, :MED, :].astype(jnp.float32)
    product[MED:, :] = (mixes[1] * mixes[2]).astype(jnp.bfloat16).astype(jnp.float32)
    row = start - MED + lax.broadcasted_iota(jnp.int32, (MED + BLK, LANES), 0)
    filtered[...] = jnp.zeros((BLK, LANES), jnp.float32)
    for genome in range(4):
        low = 0 if genome == 0 else ends_ref[genome - 1]
        high = ends_ref[genome]

        @pl.when((low < start + BLK) & (high > start))
        def _():
            kept = jnp.where(row >= low, product[...], 0.0)
            shifted[0, TAIL:, :] = kept
            for s in range(1, TAIL):
                shifted[s, TAIL + s :, :] = kept[: MED + BLK - s, :]

            def step(turn, total):
                base = pl.multiple_of(TAIL + MED - turn * TAIL, TAIL)
                weights = medium_ref[pl.ds(pl.multiple_of(turn * TAIL, TAIL), TAIL), :]
                for s in range(TAIL):
                    part = shifted[s, pl.ds(base, BLK), :]
                    total = total + part * weights[s : s + 1, :]
                return total

            total = lax.fori_loop(
                0, MED // TAIL, step, jnp.zeros((BLK, LANES), jnp.float32)
            )
            here = row[MED:, :]
            filtered[...] = jnp.where((here >= low) & (here < high), total, filtered[...])

    out_ref[0] = (mixes[0] * filtered[...]).astype(jnp.bfloat16)


def filters(sources, starts, ends, proj, halos, taps, medium):
    return pl.pallas_call(
        filter_kernel,
        grid_spec=pltpu.PrefetchScalarGridSpec(
            num_scalar_prefetch=3,
            grid=(4, 2),
            in_specs=[
                pl.BlockSpec((3, 1, BLK, LANES), lambda i, c, *_: (0, i, 0, c)),
                pl.BlockSpec((1, HALO, LANES), lambda i, c, source, *_: (source[i], 0, c)),
                pl.BlockSpec((SHORT, 3, LANES), lambda i, c, *_: (0, 0, c)),
                pl.BlockSpec((MED, LANES), lambda i, c, *_: (0, c)),
            ],
            out_specs=pl.BlockSpec((1, BLK, LANES), lambda i, c, *_: (i, 0, c)),
            scratch_shapes=[
                pltpu.VMEM((BLK + TAIL, LANES), jnp.float32),
                pltpu.VMEM((BLK + MED, LANES), jnp.float32),
                pltpu.VMEM((TAIL, BLK + MED + TAIL, LANES), jnp.float32),
                pltpu.VMEM((BLK, LANES), jnp.float32),
            ],
        ),
        out_shape=jax.ShapeDtypeStruct((4, BLK, 2 * LANES), jnp.bfloat16),
        name="filters",
    )(sources, starts, ends, proj, halos, taps, medium)


def output_kernel(place_ref, x_ref, y_ref, w_ref, *refs):
    pieces, (mine_ref, theirs_ref) = refs[:9], refs[9:]
    z, core, y_low = place_ref[0], place_ref[1], place_ref[2]
    for side, (residual_ref, out_ref) in enumerate(((x_ref, mine_ref), (y_ref, theirs_ref))):
        column = lax.rem(y_low + side, 2)
        total = residual_ref[...].astype(jnp.float32)
        for t in range(16):
            if t < 14:
                offset, piece = OFFSETS[t // 2], pieces[t // 2][t % 2]
            else:
                offset, piece = 4, pieces[t - 7][...]
            chip = lax.rem(z + offset + 8, 8)
            other = lax.rem(core + t, 2)
            w = w_ref[:, column, chip, other].reshape(16 * 16, 2 * LANES)
            total = total + lax.dot_general(
                piece, w, (((1,), (1,)), ((), ())), preferred_element_type=jnp.float32
            )
        out_ref[...] = total.astype(jnp.bfloat16)


def output(place, residual, other_residual, weights, pieces):
    shape = jax.ShapeDtypeStruct((HALF, PIECE), jnp.bfloat16)
    return pl.pallas_call(
        output_kernel,
        out_shape=(shape, shape),
        in_specs=[scalars()] + [full()] * 12,
        out_specs=(full(), full()),
        compiler_params=pltpu.CompilerParams(vmem_limit_bytes=48 << 20),
        cost_estimate=pl.CostEstimate(
            flops=2 * HALF * D * HALF, bytes_accessed=10 << 20, transcendentals=0
        ),
        name="output",
    )(place, residual, other_residual, weights, *pieces)


def shards(
    tokens,
    norm_gain,
    in_weight,
    short_filter,
    medium_filter,
    out_weight,
    genome_lengths,
    block_at_slot,
):
    seq, fsdp = lax.axis_index("seq"), lax.axis_index("fsdp")
    core, y_low, z = seq % 2, fsdp // 8, fsdp % 8

    halves = in_weight.reshape(3, PIECE, 2, LANES)
    keep = jnp.where(core == 0, halves[:, :, 0], halves[:, :, 1])
    give = jnp.where(core == 0, halves[:, :, 1], halves[:, :, 0])
    pair = jnp.stack([keep, send(give, swap_core)])
    weights = lax.all_gather(pair, AXES, axis=0, axis_index_groups=plane_groups(False))

    rows = tokens.reshape(2, HALF, PIECE)
    mine = jnp.where(y_low == 0, rows[0], rows[1])
    residual = send(jnp.where(y_low == 0, rows[1], rows[0]), swap_y)
    whole, last = ring_z(jnp.stack([mine, residual]))
    gains = norm_gain.astype(jnp.float32).reshape(2, 8, PIECE)
    gains = jnp.where(y_low == 0, gains, gains[::-1])
    pieces, squares, owners = [], [], []
    for group in range(2):
        held = [whole[o] for o in OFFSETS] + list(last)
        if group == 1:
            held = [send(h, swap_core) for h in held]
        square = jnp.zeros((HALF, 1), jnp.float32)
        for i, h in enumerate(held):
            offset = OFFSETS[i] if i < 7 else 4
            gain = lax.dynamic_index_in_dim(gains, (z + offset) % 8, 1, keepdims=True)
            gain = gain if i < 7 else gain[i - 7]
            value = h.astype(jnp.float32)
            part = jnp.sum(value * value, axis=-1, keepdims=True)
            square = square + (part[0] + part[1] if i < 7 else part)
            pieces.append((value * gain).astype(jnp.bfloat16))
        squares.append(square)
    rescale = lax.rsqrt(jnp.concatenate(squares, axis=0) / D + epsilon)
    for t in range(16):
        offset = OFFSETS[t // 2] if t < 14 else 4
        owners.append(((y_low + t) % 2) * 8 + (z + offset) % 8)
    owner = jnp.stack(owners).astype(jnp.int32)
    proj = project(owner, core.reshape(1).astype(jnp.int32), rescale, weights, pieces)

    both = jnp.concatenate([short_filter.reshape(SHORT * 3, PIECE), medium_filter], axis=0)
    both = jnp.where(core == 0, both[:, :LANES], both[:, LANES:])
    theirs = send(both, swap_y)
    both = jnp.concatenate(
        [jnp.where(y_low == 0, both, theirs), jnp.where(y_low == 0, theirs, both)], axis=1
    )
    taps = both[: SHORT * 3].reshape(SHORT, 3, 2 * LANES)
    medium = both[SHORT * 3 :].astype(jnp.float32)

    slots = jnp.stack(
        [((seq ^ group) * 4 + y_low * 2 + i) for group in range(2) for i in range(2)]
    )
    all_slots = jnp.arange(block_at_slot.shape[0], dtype=jnp.int32)
    ids = jnp.sum(jnp.where(all_slots == slots[:, None], block_at_slot, 0), axis=1)
    previous = jnp.maximum(ids - 1, 0)
    before = jnp.sum(jnp.where(block_at_slot == previous[:, None], all_slots, 0), axis=1)
    owner_seq, part, index = before // 4, (before // 2) % 2, before % 2
    group = (owner_seq + core) % 2
    sources = (((owner_seq // 2) * 2 + part) * 4 + group * 2 + index).astype(jnp.int32)
    starts = (ids * BLK).astype(jnp.int32)
    ends = jnp.cumsum(genome_lengths).astype(jnp.int32)

    tail = tails(starts, ends, proj, taps)
    halos = lax.all_gather(tail, AXES, axis=0, tiled=True, axis_index_groups=plane_groups(False))
    gated = filters(sources, starts, ends, proj, halos, taps, medium)

    columns = out_weight.reshape(2, 8, 2, LANES, 16).transpose(1, 2, 4, 0, 3)
    columns = columns.reshape(8, 2, 16, 2 * LANES)
    columns = lax.all_gather(columns, AXES, axis=0, axis_index_groups=plane_groups(True))
    columns = columns.reshape(16, 2, 8, 2, 16, 2 * LANES)

    gated = gated.reshape(2, HALF, 2 * LANES)
    chunk = jnp.stack([gated[0], send(gated[1], swap_core)])
    whole, last = ring_z(chunk)
    place = jnp.stack([z, core, y_low]).astype(jnp.int32)
    ours, others = output(
        place, mine, residual, columns, [whole[o] for o in OFFSETS] + list(last)
    )
    others = send(others, swap_y)
    first = jnp.where(y_low == 0, ours, others)
    second = jnp.where(y_low == 0, others, ours)
    return jnp.concatenate([first, second], axis=0)


def solution(mesh):
    in_specs = (
        P("seq", "fsdp"),
        P(),
        P(None, "seq", "fsdp"),
        P(None, None, "fsdp"),
        P(None, "fsdp"),
        P(None, ("fsdp", "seq")),
        P(),
        P(),
    )
    out_specs = P("seq", "fsdp")
    return jax.shard_map(shards, mesh=mesh, in_specs=in_specs, out_specs=out_specs, check_vma=False)
```

```python
import functools

import jax
import jax.numpy as jnp
from jax import lax
from jax.experimental import pallas as pl
from jax.experimental.pallas import tpu as pltpu
from jax.sharding import PartitionSpec as P


BLK = 256
SHORT = 7
MED = 128
LANES = 128
TAIL = 8
HALF = 512
PIECE = 256
D = 4096
HALO = MED + 3 * TAIL
AXES = ("seq", "fsdp")
epsilon = 1e-06
OFFSETS = (0, -1, 1, -2, 2, -3, 3)


def linear(x, y, z, core):
    return (x * 4 + (y // 2) * 2 + core) * 16 + (y % 2) * 8 + z


def permutation(move):
    pairs = []
    for x in range(4):
        for y in range(4):
            for z in range(8):
                for core in range(2):
                    pairs.append((linear(x, y, z, core), linear(*move(x, y, z, core))))
    return pairs


def send(value, move):
    return lax.ppermute(value, AXES, permutation(move))


def along_z(step):
    return lambda x, y, z, core: (x, y, (z + step) % 8, core)


def along_x(step):
    return lambda x, y, z, core: ((x + step) % 4, y, z, core)


def along_y(step):
    return lambda x, y, z, core: (x, (y + step) % 4, z, core)


def swap_y(x, y, z, core):
    return (x, y ^ 1, z, core)


def swap_core(x, y, z, core):
    return (x, y, z, core ^ 1)


def ring_z(chunk):
    right, left = chunk, chunk
    whole = {0: chunk}
    for step in range(1, 4):
        right, left = send(right, along_z(1)), send(left, along_z(-1))
        whole[-step], whole[step] = right, left
    last = (send(right[0], along_z(1)), send(left[1], along_z(-1)))
    return whole, last


def plane_groups(with_core):
    groups = []
    for z in range(8):
        every = [
            [linear(x, y, z, core) for x in range(4) for y in range(4)] for core in range(2)
        ]
        if with_core:
            groups.append(sorted(every[0] + every[1]))
        else:
            groups += every
    return groups


def full():
    return pl.BlockSpec(memory_space=pltpu.VMEM)


def scalars():
    return pl.BlockSpec(memory_space=pltpu.SMEM)


def project_kernel(
    owner_ref, place_ref, kv_ref, q_ref, *refs
):
    pieces, (out_ref, x_scratch, s_scratch, w_scratch, total, sems) = refs[:18], refs[18:]
    x, y, core = place_ref[0], place_ref[1], place_ref[2]

    def copies(t):
        made = []
        for group in range(2):
            mine = pieces[group * 9 : group * 9 + 9]
            piece = mine[t // 2].at[t % 2] if t < 14 else mine[t - 7]
            made.append((
                piece.at[pl.ds(0, HALF)],
                x_scratch.at[pl.ds(group * HALF, HALF), pl.ds(t * PIECE, PIECE)],
            ))
            made.append((piece.at[pl.ds(HALF, TAIL)], s_scratch.at[group, t]))
        owner = owner_ref[t]
        other = lax.rem(owner + core, 2)
        for part in range(2):
            chip = (owner // 2) * 2 + part
            lanes = pl.ds(part * LANES, LANES)
            rows = pl.ds(t * PIECE, PIECE)
            dx, dy = lax.rem(chip // 4 - x + 4, 4), lax.rem(lax.rem(chip, 4) - y + 4, 4)
            made.append((q_ref.at[dy, dx, other], w_scratch.at[0, rows, lanes]))
            for branch in range(2):
                made.append((kv_ref.at[chip, other, branch], w_scratch.at[branch + 1, rows, lanes]))
        return [
            pltpu.make_async_copy(source, target, sems.at[t, i])
            for i, (source, target) in enumerate(made)
        ]

    for t in range(16):
        for copy in copies(t):
            copy.start()
    for part in range(2):
        for t in range(part * 8, part * 8 + 8):
            for copy in copies(t):
                copy.wait()
        depth = slice(part * D // 2, (part + 1) * D // 2)
        for branch in range(3):
            for group in range(2):
                rows = pl.ds(group * HALF, HALF)
                product = jnp.dot(
                    x_scratch[rows, depth], w_scratch[branch, depth, :],
                    preferred_element_type=jnp.float32,
                )
                if part == 0:
                    total[branch, rows, :] = product
                else:
                    total[branch, rows, :] += product
    for group in range(2):
        square = jnp.sum(s_scratch[group].astype(jnp.float32), axis=0)
        for i in range(2):
            row = square[i : i + 1] + square[i + 2 : i + 3] + square[i + 4 : i + 5]
            scale = lax.rsqrt(row / D + epsilon)
            scale = jnp.transpose(jnp.broadcast_to(scale, (LANES, PIECE)))
            scale = jnp.concatenate([scale, scale], axis=1)
            block = group * 2 + i
            for branch in range(3):
                value = total[branch, block * BLK : (block + 1) * BLK, :]
                out_ref[branch, block] = (value * scale).astype(jnp.bfloat16)


def project(owner, place, kv, q, pieces):
    return pl.pallas_call(
        project_kernel,
        out_shape=jax.ShapeDtypeStruct((3, 4, BLK, 2 * LANES), jnp.bfloat16),
        in_specs=[scalars(), scalars()] + [pl.BlockSpec(memory_space=pl.ANY)] * 20,
        out_specs=full(),
        scratch_shapes=[
            pltpu.VMEM((2 * HALF, D), jnp.bfloat16),
            pltpu.VMEM((2, 16, TAIL, PIECE), jnp.bfloat16),
            pltpu.VMEM((3, D, 2 * LANES), jnp.bfloat16),
            pltpu.VMEM((3, 2 * HALF, 2 * LANES), jnp.float32),
            pltpu.SemaphoreType.DMA((16, 10)),
        ],
        compiler_params=pltpu.CompilerParams(vmem_limit_bytes=32 << 20),
        cost_estimate=pl.CostEstimate(
            flops=2 * 1024 * D * 768, bytes_accessed=16 << 20, transcendentals=0
        ),
        name="project",
    )(owner, place, kv, q, *pieces)


def reach_of(start, rows, ends_ref):
    position = start + lax.broadcasted_iota(jnp.int32, (rows, LANES), 0)
    first = jnp.zeros((rows, LANES), jnp.int32)
    for g in range(3):
        end = ends_ref[g]
        first = jnp.maximum(first, jnp.where(position >= end, end, 0))
    return position - first


def split_by_genome(start, ends_ref):
    cut = False
    for g in range(3):
        cut = cut | ((ends_ref[g] > start) & (ends_ref[g] < start + BLK))
    return cut


def short_mix(window_ref, reach, taps_ref, branch, rows, lanes):
    total = jnp.zeros((rows, LANES), jnp.float32)
    for j in range(SHORT):
        part = window_ref[TAIL - j : TAIL - j + rows, :]
        if reach is not None:
            part = jnp.where(reach >= j, part, 0.0)
        total = total + part * taps_ref[j, branch : branch + 1, lanes].astype(jnp.float32)
    return total


def product_kernel(start_ref, ends_ref, proj_ref, taps_ref, out_ref, low_ref, high_ref, k, v):
    start = start_ref[pl.program_id(0)]
    cut = split_by_genome(start, ends_ref)
    for part, tail_ref in enumerate((low_ref, high_ref)):
        lanes = pl.ds(part * LANES, LANES)
        k[:TAIL, :] = jnp.zeros((TAIL, LANES), jnp.float32)
        v[:TAIL, :] = jnp.zeros((TAIL, LANES), jnp.float32)
        k[TAIL:, :] = proj_ref[1, 0, :, lanes].astype(jnp.float32)
        v[TAIL:, :] = proj_ref[2, 0, :, lanes].astype(jnp.float32)

        def store(reach):
            mixed = short_mix(k, reach, taps_ref, 1, BLK, lanes)
            product = mixed * short_mix(v, reach, taps_ref, 2, BLK, lanes)
            first = lax.broadcasted_iota(jnp.int32, (BLK, LANES), 0) >= SHORT - 1
            out_ref[0, :, lanes] = jnp.where(first, product, 0.0).astype(jnp.bfloat16)

        @pl.when(cut)
        def _():
            store(reach_of(start, BLK, ends_ref))

        @pl.when(jnp.logical_not(cut))
        def _():
            store(None)

        tail_ref[0, :MED, :] = out_ref[0, BLK - MED :, lanes]
        for branch in range(3):
            at = MED + branch * TAIL
            tail_ref[0, at : at + TAIL, :] = proj_ref[branch, 0, BLK - TAIL :, lanes]


def products(starts, ends, proj, taps):
    tail = jax.ShapeDtypeStruct((4, HALO, LANES), jnp.bfloat16)
    tail_spec = pl.BlockSpec((1, HALO, LANES), lambda i, *_: (i, 0, 0))
    return pl.pallas_call(
        product_kernel,
        grid_spec=pltpu.PrefetchScalarGridSpec(
            num_scalar_prefetch=2,
            grid=(4,),
            in_specs=[
                pl.BlockSpec((3, 1, BLK, 2 * LANES), lambda i, *_: (0, i, 0, 0)),
                pl.BlockSpec((SHORT, 3, 2 * LANES), lambda i, *_: (0, 0, 0)),
            ],
            out_specs=(
                pl.BlockSpec((1, BLK, 2 * LANES), lambda i, *_: (i, 0, 0)), tail_spec, tail_spec,
            ),
            scratch_shapes=[pltpu.VMEM((BLK + TAIL, LANES), jnp.float32)] * 2,
        ),
        out_shape=(jax.ShapeDtypeStruct((4, BLK, 2 * LANES), jnp.bfloat16), tail, tail),
        cost_estimate=pl.CostEstimate(
            flops=60 << 20, bytes_accessed=4 << 20, transcendentals=0
        ),
        name="products",
    )(starts, ends, proj, taps)


def taps_of(shifted, medium_ref, lanes, base, first, last, rows):
    def step(turn, total):
        at = pl.multiple_of(base - turn * TAIL, TAIL)
        weights = medium_ref[pl.ds(pl.multiple_of(turn * TAIL, TAIL), TAIL), lanes]
        for s in range(TAIL):
            total = total + shifted[s, pl.ds(at, rows), :] * weights[s : s + 1, :]
        return total

    return lax.fori_loop(first, last, step, jnp.zeros((rows, LANES), jnp.float32))


GROUP = 64


def inner_kernel(start_ref, ends_ref, product_ref, medium_ref, out_ref, shifted):
    start = start_ref[pl.program_id(0)]
    row = start + lax.broadcasted_iota(jnp.int32, (BLK, LANES), 0)
    cut = split_by_genome(start, ends_ref)

    for part in range(2):
        lanes = pl.ds(part * LANES, LANES)

        def run(low, high):
            value = product_ref[0, :, lanes].astype(jnp.float32)
            if low is not None:
                value = jnp.where(row >= low, value, 0.0)
            for s in range(TAIL):
                shifted[s, : GROUP + TAIL, :] = jnp.zeros((GROUP + TAIL, LANES), jnp.float32)
                shifted[s, GROUP + s : GROUP + BLK, :] = value[: BLK - s, :]
            for r in range(BLK // GROUP):
                last = min(MED // TAIL, (r + 1) * GROUP // TAIL)
                total = taps_of(
                    shifted, medium_ref, lanes, GROUP + r * GROUP, 0, last, GROUP
                )
                rows = pl.ds(r * GROUP, GROUP)
                if low is not None:
                    here = row[r * GROUP : (r + 1) * GROUP]
                    total = jnp.where((here >= low) & (here < high), total, out_ref[0, rows, lanes])
                out_ref[0, rows, lanes] = total

        @pl.when(jnp.logical_not(cut))
        def _():
            run(None, None)

        @pl.when(cut)
        def _():
            def genome(g, carry):
                low = jnp.where(g == 0, 0, ends_ref[jnp.maximum(g - 1, 0)])
                high = ends_ref[g]

                @pl.when((low < start + BLK) & (high > start))
                def _():
                    run(low, high)

                return carry

            lax.fori_loop(0, 4, genome, 0)


def inner(starts, ends, product, medium):
    return pl.pallas_call(
        inner_kernel,
        grid_spec=pltpu.PrefetchScalarGridSpec(
            num_scalar_prefetch=2,
            grid=(4,),
            in_specs=[
                pl.BlockSpec((1, BLK, 2 * LANES), lambda i, *_: (i, 0, 0)),
                pl.BlockSpec((MED, 2 * LANES), lambda i, *_: (0, 0)),
            ],
            out_specs=pl.BlockSpec((1, BLK, 2 * LANES), lambda i, *_: (i, 0, 0)),
            scratch_shapes=[pltpu.VMEM((TAIL, GROUP + BLK, LANES), jnp.float32)],
        ),
        out_shape=jax.ShapeDtypeStruct((4, BLK, 2 * LANES), jnp.float32),
        cost_estimate=pl.CostEstimate(
            flops=2 * 1024 * 256 * 128, bytes_accessed=2 << 20, transcendentals=0
        ),
        name="inner",
    )(starts, ends, product, medium)


def route_kernel(table_ref, *refs):
    ins, outs, every = refs[:8], refs[8:16], refs[16]
    for way in range(2):
        for d in range(4):
            every[d * 4 : (d + 1) * 4] = ins[way * 4 + d][...]
        for d in range(4):
            for j in range(4):
                outs[way * 4 + d][j] = every[table_ref[way, d, j]]


def route(table, ins):
    return pl.pallas_call(
        route_kernel,
        out_shape=(jax.ShapeDtypeStruct((4, HALO, LANES), jnp.bfloat16),) * 8,
        in_specs=[scalars()] + [full()] * 8,
        out_specs=(full(),) * 8,
        scratch_shapes=[pltpu.VMEM((16, HALO, LANES), jnp.bfloat16)],
        cost_estimate=pl.CostEstimate(flops=1 << 10, bytes_accessed=4 << 20, transcendentals=0),
        name="route",
    )(table, *ins)


def edge_kernel(
    start_ref, ends_ref, pick_ref, proj_ref, partial_ref, taps_ref, medium_ref, *refs
):
    halos, (out_ref, halo, window, small, prior, shifted, filtered) = refs[:8], refs[8:]
    block = pl.program_id(0)
    start = start_ref[block]
    cut = split_by_genome(start, ends_ref)
    near = MED + TAIL
    reach8 = reach_of(start, TAIL, ends_ref)
    row = start - MED + lax.broadcasted_iota(jnp.int32, (near, LANES), 0)
    out_row = start + lax.broadcasted_iota(jnp.int32, (near, LANES), 0)
    for part in range(2):
        lanes = pl.ds(part * LANES, LANES)
        for m in range(4):

            @pl.when(pick_ref[part, block] == m)
            def _(m=m):
                halo[...] = halos[part * 4 + m][0].astype(jnp.float32)

        mixes = []
        for branch in (1, 2):
            at = MED + branch * TAIL
            small[:TAIL, :] = halo[at : at + TAIL, :]
            small[TAIL:, :] = proj_ref[branch, 0, : 2 * TAIL, lanes][:TAIL].astype(jnp.float32)
            mixes.append(short_mix(small, reach8, taps_ref, branch, TAIL, lanes))
        first = lax.broadcasted_iota(jnp.int32, (TAIL, LANES), 0) < SHORT - 1
        early = (mixes[0] * mixes[1]).astype(jnp.bfloat16).astype(jnp.float32)
        prior[:MED, :] = halo[:MED, :]
        prior[MED:, :] = jnp.where(first, early, 0.0)
        filtered[...] = partial_ref[0, :, lanes]

        def genome(g, carry):
            low = jnp.where(g == 0, 0, ends_ref[jnp.maximum(g - 1, 0)])
            high = ends_ref[g]

            @pl.when((low < start + near) & (high > start))
            def _():
                value = jnp.where(row >= low, prior[...], 0.0)
                for s in range(TAIL):
                    shifted[s, TAIL : TAIL + TAIL, :] = jnp.zeros((TAIL, LANES), jnp.float32)
                    shifted[s, near + TAIL :, :] = jnp.zeros((GROUP, LANES), jnp.float32)
                    shifted[s, TAIL + s : TAIL + s + near, :] = value
                for r, (at, rows, begin) in enumerate(
                    ((0, GROUP, 0), (GROUP, GROUP, 7), (2 * GROUP, TAIL, 15))
                ):
                    total = taps_of(
                        shifted, medium_ref, lanes, TAIL + MED + at, begin, MED // TAIL, rows
                    )
                    here = out_row[at : at + rows]
                    total = jnp.where((here >= low) & (here < high), total, 0.0)
                    filtered[at : at + rows, :] += total

            return carry

        lax.fori_loop(0, 4, genome, 0)
        window[:TAIL, :] = halo[MED : MED + TAIL, :]
        window[TAIL:, :] = proj_ref[0, 0, :, lanes].astype(jnp.float32)

        @pl.when(cut)
        def _():
            mixed = short_mix(window, reach_of(start, BLK, ends_ref), taps_ref, 0, BLK, lanes)
            out_ref[0, :, lanes] = (mixed * filtered[...]).astype(jnp.bfloat16)

        @pl.when(jnp.logical_not(cut))
        def _():
            head = short_mix(window, reach8, taps_ref, 0, TAIL, lanes)
            mixed = short_mix(window, None, taps_ref, 0, BLK, lanes)
            mixed = jnp.concatenate([head, mixed[TAIL:]], axis=0)
            out_ref[0, :, lanes] = (mixed * filtered[...]).astype(jnp.bfloat16)


def edges(starts, ends, picks, proj, partial, taps, medium, halos):
    return pl.pallas_call(
        edge_kernel,
        grid_spec=pltpu.PrefetchScalarGridSpec(
            num_scalar_prefetch=3,
            grid=(4,),
            in_specs=[
                pl.BlockSpec((3, 1, BLK, 2 * LANES), lambda i, *_: (0, i, 0, 0)),
                pl.BlockSpec((1, BLK, 2 * LANES), lambda i, *_: (i, 0, 0)),
                pl.BlockSpec((SHORT, 3, 2 * LANES), lambda i, *_: (0, 0, 0)),
                pl.BlockSpec((MED, 2 * LANES), lambda i, *_: (0, 0)),
            ]
            + [pl.BlockSpec((1, HALO, LANES), lambda i, *_: (i, 0, 0))] * 8,
            out_specs=pl.BlockSpec((1, BLK, 2 * LANES), lambda i, *_: (i, 0, 0)),
            scratch_shapes=[
                pltpu.VMEM((HALO, LANES), jnp.float32),
                pltpu.VMEM((BLK + TAIL, LANES), jnp.float32),
                pltpu.VMEM((2 * TAIL, LANES), jnp.float32),
                pltpu.VMEM((MED + TAIL, LANES), jnp.float32),
                pltpu.VMEM((TAIL, MED + 2 * TAIL + GROUP, LANES), jnp.float32),
                pltpu.VMEM((BLK, LANES), jnp.float32),
            ],
        ),
        out_shape=jax.ShapeDtypeStruct((4, BLK, 2 * LANES), jnp.bfloat16),
        cost_estimate=pl.CostEstimate(
            flops=2 * 1024 * 256 * 64, bytes_accessed=5 << 20, transcendentals=0
        ),
        name="edges",
    )(starts, ends, picks, proj, partial, taps, medium, *halos)


def output_kernel(place_ref, x_ref, y_ref, w_ref, *refs):
    pieces, (mine_ref, theirs_ref) = refs[:9], refs[9:]
    z, core, y_low = place_ref[0], place_ref[1], place_ref[2]
    for side, (residual_ref, out_ref) in enumerate(((x_ref, mine_ref), (y_ref, theirs_ref))):
        column = lax.rem(y_low + side, 2)
        total = residual_ref[...].astype(jnp.float32)
        for t in range(16):
            if t < 14:
                offset, piece = OFFSETS[t // 2], pieces[t // 2][t % 2]
            else:
                offset, piece = 4, pieces[t - 7][...]
            chip = lax.rem(z + offset + 8, 8)
            other = lax.rem(core + t, 2)
            w = w_ref[:, column, chip, other].reshape(16 * 16, 2 * LANES)
            total = total + lax.dot_general(
                piece, w, (((1,), (1,)), ((), ())), preferred_element_type=jnp.float32
            )
        out_ref[...] = total.astype(jnp.bfloat16)


def output(place, residual, other_residual, weights, pieces):
    shape = jax.ShapeDtypeStruct((HALF, PIECE), jnp.bfloat16)
    return pl.pallas_call(
        output_kernel,
        out_shape=(shape, shape),
        in_specs=[scalars()] + [full()] * 12,
        out_specs=(full(), full()),
        compiler_params=pltpu.CompilerParams(vmem_limit_bytes=48 << 20),
        cost_estimate=pl.CostEstimate(
            flops=2 * HALF * D * HALF, bytes_accessed=10 << 20, transcendentals=0
        ),
        name="output",
    )(place, residual, other_residual, weights, *pieces)


def shards(
    tokens,
    norm_gain,
    in_weight,
    short_filter,
    medium_filter,
    out_weight,
    genome_lengths,
    block_at_slot,
):
    seq, fsdp = lax.axis_index("seq"), lax.axis_index("fsdp")
    x, core, y_low, z = seq // 4, seq % 2, fsdp // 8, fsdp % 8
    y = ((seq // 2) % 2) * 2 + y_low

    values = tokens.astype(jnp.float32)
    gain = lax.dynamic_index_in_dim(norm_gain.reshape(16, 1, PIECE), fsdp, 0, keepdims=False)
    scaled = (values * gain.astype(jnp.float32)).astype(jnp.bfloat16)
    square = jnp.sum(values * values, axis=1)
    parts = []
    for _ in range(3):
        part = lax.reduce_precision(square, exponent_bits=8, mantissa_bits=7)
        parts.append(part.astype(jnp.bfloat16).reshape(2, 2, PIECE))
        square = square - part
    parts.append(jnp.zeros((2, 2, PIECE), jnp.bfloat16))
    packed = jnp.concatenate([scaled.reshape(2, HALF, PIECE)] + parts, axis=1)
    mine = jnp.where(y_low == 0, packed[0], packed[1])
    theirs = send(jnp.where(y_low == 0, packed[1], packed[0]), swap_y)
    whole, last = ring_z(jnp.stack([mine, theirs]))
    pieces = [whole[o] for o in OFFSETS] + list(last)
    pieces = pieces + [send(p, swap_core) for p in pieces]

    halves = in_weight.reshape(3, PIECE, 2, LANES)
    keep = jnp.where(core == 0, halves[:, :, 0], halves[:, :, 1])
    give = jnp.where(core == 0, halves[:, :, 1], halves[:, :, 0])
    pair = jnp.stack([keep, send(give, swap_core)])
    kv = lax.all_gather(pair[:, 1:], AXES, axis=0, axis_index_groups=plane_groups(False))
    q = pair[:, 0]
    q = jnp.stack([q] + [send(q, along_x(-d)) for d in range(1, 4)])
    q = jnp.stack([q] + [send(q, along_y(-d)) for d in range(1, 4)])

    owners = []
    for t in range(16):
        offset = OFFSETS[t // 2] if t < 14 else 4
        owners.append(((y_low + t) % 2) * 8 + (z + offset) % 8)
    owner = jnp.stack(owners).astype(jnp.int32)
    place = jnp.stack([x, y, core]).astype(jnp.int32)
    proj = project(owner, place, kv, q, pieces)

    both = jnp.concatenate([short_filter.reshape(SHORT * 3, PIECE), medium_filter], axis=0)
    both = jnp.where(core == 0, both[:, :LANES], both[:, LANES:])
    theirs = send(both, swap_y)
    both = jnp.concatenate(
        [jnp.where(y_low == 0, both, theirs), jnp.where(y_low == 0, theirs, both)], axis=1
    )
    taps = both[: SHORT * 3].reshape(SHORT, 3, 2 * LANES)
    medium = both[SHORT * 3 :].astype(jnp.float32)

    way = jnp.arange(2, dtype=jnp.int32).reshape(2, 1, 1, 1)
    ahead = jnp.arange(4, dtype=jnp.int32).reshape(1, 4, 1, 1)
    group = jnp.arange(2, dtype=jnp.int32).reshape(1, 1, 2, 1)
    index = jnp.arange(2, dtype=jnp.int32).reshape(1, 1, 1, 2)
    to_x, to_y = (x + way * ahead) % 4, (y + (1 - way) * ahead) % 4
    slots = (to_x * 4 + (to_y // 2) * 2 + (core + group) % 2) * 4 + (to_y % 2) * 2 + index
    slots = slots.reshape(32)
    all_slots = jnp.arange(block_at_slot.shape[0], dtype=jnp.int32)
    ids = jnp.sum(jnp.where(all_slots == slots[:, None], block_at_slot, 0), axis=1)
    previous = jnp.maximum(ids - 1, 0)
    before = jnp.sum(jnp.where(block_at_slot == previous[:, None], all_slots, 0), axis=1)
    before = before.reshape(2, 4, 4)
    from_x, from_y = before // 16, ((before // 8) % 2) * 2 + (before // 2) % 2
    local = ((before // 4 + core) % 2) * 2 + before % 2
    dx, dy = (from_x - x) % 4, (from_y - y) % 4
    table = jnp.stack(
        [jnp.where(dy[0] == 0, dx[0] * 4, 0) + local[0],
         jnp.where(dx[1] == 0, dy[1] * 4, 0) + local[1]]
    ).astype(jnp.int32)
    picks = jnp.stack([dy[0, 0], dx[1, 0]]).astype(jnp.int32)
    starts = (ids[:4] * BLK).astype(jnp.int32)
    ends = jnp.cumsum(genome_lengths).astype(jnp.int32)

    product, low, high = products(starts, ends, proj, taps)
    rows_x = [low] + [send(low, along_x(-d)) for d in range(1, 4)]
    rows_y = [high] + [send(high, along_y(-d)) for d in range(1, 4)]
    partial = inner(starts, ends, product, medium)
    routed = route(table, rows_x + rows_y)
    halos = [routed[0]] + [send(routed[4 - d], along_y(4 - d)) for d in range(1, 4)]
    halos += [routed[4]] + [send(routed[8 - d], along_x(4 - d)) for d in range(1, 4)]
    gated = edges(starts, ends, picks, proj, partial, taps, medium, halos)

    columns = out_weight.reshape(2, 8, 2, LANES, 16).transpose(1, 2, 4, 0, 3)
    columns = columns.reshape(8, 2, 16, 2 * LANES)
    columns = lax.all_gather(columns, AXES, axis=0, axis_index_groups=plane_groups(True))
    columns = columns.reshape(16, 2, 8, 2, 16, 2 * LANES)

    rows = tokens.reshape(2, HALF, PIECE)
    mine = jnp.where(y_low == 0, rows[0], rows[1])
    residual = send(jnp.where(y_low == 0, rows[1], rows[0]), swap_y)
    gated = gated.reshape(2, HALF, 2 * LANES)
    chunk = jnp.stack([gated[0], send(gated[1], swap_core)])
    whole, last = ring_z(chunk)
    place = jnp.stack([z, core, y_low]).astype(jnp.int32)
    ours, others = output(
        place, mine, residual, columns, [whole[o] for o in OFFSETS] + list(last)
    )
    others = send(others, swap_y)
    first = jnp.where(y_low == 0, ours, others)
    second = jnp.where(y_low == 0, others, ours)
    return jnp.concatenate([first, second], axis=0)


def solution(mesh):
    in_specs = (
        P("seq", "fsdp"),
        P(),
        P(None, "seq", "fsdp"),
        P(None, None, "fsdp"),
        P(None, "fsdp"),
        P(None, ("fsdp", "seq")),
        P(),
        P(),
    )
    out_specs = P("seq", "fsdp")
    return jax.shard_map(shards, mesh=mesh, in_specs=in_specs, out_specs=out_specs, check_vma=False)
```

```python
import functools

import jax
import jax.numpy as jnp
from jax import lax
from jax.experimental import pallas as pl
from jax.experimental.pallas import tpu as pltpu
from jax.sharding import PartitionSpec as P


BLK = 256
SHORT = 7
MED = 128
LANES = 128
TAIL = 8
HALF = 512
PIECE = 256
D = 4096
HALO = MED + 3 * TAIL
AXES = ("seq", "fsdp")
epsilon = 1e-06
OFFSETS = (0, -1, 1, -2, 2, -3, 3, 4)


def linear(x, y, z, core):
    return (x * 4 + (y // 2) * 2 + core) * 16 + (y % 2) * 8 + z


def permutation(move):
    pairs = []
    for x in range(4):
        for y in range(4):
            for z in range(8):
                for core in range(2):
                    pairs.append((linear(x, y, z, core), linear(*move(x, y, z, core))))
    return pairs


def send(value, move):
    return lax.ppermute(value, AXES, permutation(move))


def along_z(step):
    return lambda x, y, z, core: (x, y, (z + step) % 8, core)


def along_x(step):
    return lambda x, y, z, core: ((x + step) % 4, y, z, core)


def along_y(step):
    return lambda x, y, z, core: (x, (y + step) % 4, z, core)


def swap_y(x, y, z, core):
    return (x, y ^ 1, z, core)


def swap_core(x, y, z, core):
    return (x, y, z, core ^ 1)


def ring_z(chunk, way):
    there, back = chunk, chunk
    found = {0: chunk}
    for step in range(1, 5):
        there = send(there, along_z(way))
        found[-way * step if step < 4 else 4] = there
        if step < 4:
            back = send(back, along_z(-way))
            found[way * step] = back
    return [found[o] for o in OFFSETS]


def axis_of(chunk, along):
    return [chunk] + [send(chunk, along(-d)) for d in range(1, 4)]


def anywhere():
    return pl.BlockSpec(memory_space=pl.ANY)


def full():
    return pl.BlockSpec(memory_space=pltpu.VMEM)


def scalars():
    return pl.BlockSpec(memory_space=pltpu.SMEM)


def project_kernel(where_ref, place_ref, *refs):
    weights, pieces = refs[:8], refs[8:40]
    out_ref, x_scratch, s_scratch, w_scratch, total, x_sems, s_sems, w_sems = refs[40:]
    x, y, core = place_ref[0], place_ref[1], place_ref[2]
    started = []
    for group in range(2):
        for t in range(16):
            piece = pieces[group * 16 + t]
            target = x_scratch.at[pl.ds(group * HALF, HALF), pl.ds(t * PIECE, PIECE)]
            started.append(
                pltpu.make_async_copy(piece.at[pl.ds(0, HALF)], target, x_sems.at[group, t])
            )
            target = s_scratch.at[group, t]
            started.append(
                pltpu.make_async_copy(piece.at[pl.ds(HALF, TAIL)], target, s_sems.at[group, t])
            )
    for other in range(2):
        for a in range(4):
            for b in range(4):
                dx, dy = (b, a) if other == 0 else (a, b)
                to_x, to_y = lax.rem(x + dx, 4), lax.rem(y + dy, 4)
                owner = to_x * 4 + (to_y // 2) * 2 + lax.rem(core + other, 2)
                rows = pl.ds(pl.multiple_of(where_ref[owner] * PIECE, PIECE), PIECE)
                lanes = pl.ds(pl.multiple_of(lax.rem(to_y, 2) * LANES, LANES), LANES)
                started.append(
                    pltpu.make_async_copy(
                        weights[other * 4 + a].at[b],
                        w_scratch.at[:, rows, lanes],
                        w_sems.at[other, a, b],
                    )
                )
    for copy in started:
        copy.start()
    for copy in started:
        copy.wait()

    def step(i, carry):
        branch, group = i // 2, lax.rem(i, 2)
        rows = pl.ds(pl.multiple_of(group * HALF, HALF), HALF)
        total[branch, rows, :] = jnp.dot(
            x_scratch[rows, :], w_scratch[branch], preferred_element_type=jnp.float32
        )
        return carry

    lax.fori_loop(0, 6, step, 0)
    for group in range(2):
        square = jnp.sum(s_scratch[group].astype(jnp.float32), axis=0)
        for i in range(2):
            row = square[i : i + 1] + square[i + 2 : i + 3] + square[i + 4 : i + 5]
            scale = lax.rsqrt(row / D + epsilon)
            scale = jnp.transpose(jnp.broadcast_to(scale, (LANES, PIECE)))
            scale = jnp.concatenate([scale, scale], axis=1)
            block = group * 2 + i
            for branch in range(3):
                value = total[branch, block * BLK : (block + 1) * BLK, :]
                out_ref[branch, block] = (value * scale).astype(jnp.bfloat16)


def project(where, place, weights, pieces):
    return pl.pallas_call(
        project_kernel,
        out_shape=jax.ShapeDtypeStruct((3, 4, BLK, 2 * LANES), jnp.bfloat16),
        in_specs=[scalars(), scalars()] + [anywhere()] * 40,
        out_specs=full(),
        scratch_shapes=[
            pltpu.VMEM((2 * HALF, D), jnp.bfloat16),
            pltpu.VMEM((2, 16, TAIL, PIECE), jnp.bfloat16),
            pltpu.VMEM((3, D, 2 * LANES), jnp.bfloat16),
            pltpu.VMEM((3, 2 * HALF, 2 * LANES), jnp.float32),
            pltpu.SemaphoreType.DMA((2, 16)),
            pltpu.SemaphoreType.DMA((2, 16)),
            pltpu.SemaphoreType.DMA((2, 4, 4)),
        ],
        compiler_params=pltpu.CompilerParams(vmem_limit_bytes=32 << 20),
        cost_estimate=pl.CostEstimate(
            flops=2 * 1024 * D * 768, bytes_accessed=16 << 20, transcendentals=0
        ),
        name="project",
    )(where, place, *weights, *pieces)


def reach_of(start, rows, ends_ref):
    position = start + lax.broadcasted_iota(jnp.int32, (rows, LANES), 0)
    first = jnp.zeros((rows, LANES), jnp.int32)
    for g in range(3):
        end = ends_ref[g]
        first = jnp.maximum(first, jnp.where(position >= end, end, 0))
    return position - first


def split_by_genome(start, ends_ref):
    cut = False
    for g in range(3):
        cut = cut | ((ends_ref[g] > start) & (ends_ref[g] < start + BLK))
    return cut


def short_mix(window_ref, reach, taps_ref, branch, rows, lanes):
    total = jnp.zeros((rows, LANES), jnp.float32)
    for j in range(SHORT):
        part = window_ref[TAIL - j : TAIL - j + rows, :]
        if reach is not None:
            part = jnp.where(reach >= j, part, 0.0)
        total = total + part * taps_ref[j, branch : branch + 1, lanes].astype(jnp.float32)
    return total


def product_kernel(start_ref, ends_ref, proj_ref, taps_ref, out_ref, low_ref, high_ref, k, v):
    start = start_ref[pl.program_id(0)]
    cut = split_by_genome(start, ends_ref)
    for part, tail_ref in enumerate((low_ref, high_ref)):
        lanes = pl.ds(part * LANES, LANES)
        k[:TAIL, :] = jnp.zeros((TAIL, LANES), jnp.float32)
        v[:TAIL, :] = jnp.zeros((TAIL, LANES), jnp.float32)
        k[TAIL:, :] = proj_ref[1, 0, :, lanes].astype(jnp.float32)
        v[TAIL:, :] = proj_ref[2, 0, :, lanes].astype(jnp.float32)

        def store(reach):
            mixed = short_mix(k, reach, taps_ref, 1, BLK, lanes)
            product = mixed * short_mix(v, reach, taps_ref, 2, BLK, lanes)
            first = lax.broadcasted_iota(jnp.int32, (BLK, LANES), 0) >= SHORT - 1
            out_ref[0, :, lanes] = jnp.where(first, product, 0.0).astype(jnp.bfloat16)

        @pl.when(cut)
        def _():
            store(reach_of(start, BLK, ends_ref))

        @pl.when(jnp.logical_not(cut))
        def _():
            store(None)

        tail_ref[0, :MED, :] = out_ref[0, BLK - MED :, lanes]
        for branch in range(3):
            at = MED + branch * TAIL
            tail_ref[0, at : at + TAIL, :] = proj_ref[branch, 0, BLK - TAIL :, lanes]


def products(starts, ends, proj, taps):
    tail = jax.ShapeDtypeStruct((4, HALO, LANES), jnp.bfloat16)
    tail_spec = pl.BlockSpec((1, HALO, LANES), lambda i, *_: (i, 0, 0))
    return pl.pallas_call(
        product_kernel,
        grid_spec=pltpu.PrefetchScalarGridSpec(
            num_scalar_prefetch=2,
            grid=(4,),
            in_specs=[
                pl.BlockSpec((3, 1, BLK, 2 * LANES), lambda i, *_: (0, i, 0, 0)),
                pl.BlockSpec((SHORT, 3, 2 * LANES), lambda i, *_: (0, 0, 0)),
            ],
            out_specs=(
                pl.BlockSpec((1, BLK, 2 * LANES), lambda i, *_: (i, 0, 0)), tail_spec, tail_spec,
            ),
            scratch_shapes=[pltpu.VMEM((BLK + TAIL, LANES), jnp.float32)] * 2,
        ),
        out_shape=(jax.ShapeDtypeStruct((4, BLK, 2 * LANES), jnp.bfloat16), tail, tail),
        cost_estimate=pl.CostEstimate(
            flops=60 << 20, bytes_accessed=4 << 20, transcendentals=0
        ),
        name="products",
    )(starts, ends, proj, taps)


def taps_of(shifted, medium_ref, lanes, base, first, last, rows):
    def step(turn, total):
        at = pl.multiple_of(base - turn * TAIL, TAIL)
        weights = medium_ref[pl.ds(pl.multiple_of(turn * TAIL, TAIL), TAIL), lanes]
        for s in range(TAIL):
            total = total + shifted[s, pl.ds(at, rows), :] * weights[s : s + 1, :]
        return total

    return lax.fori_loop(first, last, step, jnp.zeros((rows, LANES), jnp.float32))


GROUP = 64


def inner_kernel(index, start_ref, ends_ref, product_ref, medium_ref, out_ref, shifted):
    start = start_ref[pl.program_id(0) * 2 + index]
    row = start + lax.broadcasted_iota(jnp.int32, (BLK, LANES), 0)
    cut = split_by_genome(start, ends_ref)

    for part in range(2):
        lanes = pl.ds(part * LANES, LANES)

        def run(low, high):
            value = product_ref[0, :, lanes].astype(jnp.float32)
            if low is not None:
                value = jnp.where(row >= low, value, 0.0)
            for s in range(TAIL):
                shifted[s, : GROUP + TAIL, :] = jnp.zeros((GROUP + TAIL, LANES), jnp.float32)
                shifted[s, GROUP + s : GROUP + BLK, :] = value[: BLK - s, :]
            for r in range(BLK // GROUP):
                last = min(MED // TAIL, (r + 1) * GROUP // TAIL)
                total = taps_of(
                    shifted, medium_ref, lanes, GROUP + r * GROUP, 0, last, GROUP
                )
                rows = pl.ds(r * GROUP, GROUP)
                if low is not None:
                    here = row[r * GROUP : (r + 1) * GROUP]
                    total = jnp.where((here >= low) & (here < high), total, out_ref[0, rows, lanes])
                out_ref[0, rows, lanes] = total

        @pl.when(jnp.logical_not(cut))
        def _():
            run(None, None)

        @pl.when(cut)
        def _():
            def genome(g, carry):
                low = jnp.where(g == 0, 0, ends_ref[jnp.maximum(g - 1, 0)])
                high = ends_ref[g]

                @pl.when((low < start + BLK) & (high > start))
                def _():
                    run(low, high)

                return carry

            lax.fori_loop(0, 4, genome, 0)


def inner(index, starts, ends, product, medium):
    return pl.pallas_call(
        functools.partial(inner_kernel, index),
        grid_spec=pltpu.PrefetchScalarGridSpec(
            num_scalar_prefetch=2,
            grid=(2,),
            in_specs=[
                pl.BlockSpec((1, BLK, 2 * LANES), lambda i, *_: (i * 2 + index, 0, 0)),
                pl.BlockSpec((MED, 2 * LANES), lambda i, *_: (0, 0)),
            ],
            out_specs=pl.BlockSpec((1, BLK, 2 * LANES), lambda i, *_: (i, 0, 0)),
            scratch_shapes=[pltpu.VMEM((TAIL, GROUP + BLK, LANES), jnp.float32)],
        ),
        out_shape=jax.ShapeDtypeStruct((2, BLK, 2 * LANES), jnp.float32),
        cost_estimate=pl.CostEstimate(
            flops=1024 * 256 * 128, bytes_accessed=1 << 20, transcendentals=0
        ),
        name="inner",
    )(starts, ends, product, medium)


def route_kernel(table_ref, *refs):
    ins, outs, every = refs[:8], refs[8:16], refs[16]
    for way in range(2):
        for d in range(4):
            every[d * 4 : (d + 1) * 4] = ins[way * 4 + d][...]
        for d in range(4):
            for j in range(4):
                outs[way * 4 + d][j] = every[table_ref[way, d, j]]


def route(table, ins):
    return pl.pallas_call(
        route_kernel,
        out_shape=(jax.ShapeDtypeStruct((4, HALO, LANES), jnp.bfloat16),) * 8,
        in_specs=[scalars()] + [full()] * 8,
        out_specs=(full(),) * 8,
        scratch_shapes=[pltpu.VMEM((16, HALO, LANES), jnp.bfloat16)],
        cost_estimate=pl.CostEstimate(flops=1 << 10, bytes_accessed=4 << 20, transcendentals=0),
        name="route",
    )(table, *ins)


def edge_kernel(
    index, start_ref, ends_ref, pick_ref, proj_ref, partial_ref, taps_ref, medium_ref, *refs
):
    halos, (out_ref, halo, window, small, prior, shifted, filtered) = refs[:8], refs[8:]
    block = pl.program_id(0) * 2 + index
    start = start_ref[block]
    cut = split_by_genome(start, ends_ref)
    near = MED + TAIL
    reach8 = reach_of(start, TAIL, ends_ref)
    row = start - MED + lax.broadcasted_iota(jnp.int32, (near, LANES), 0)
    out_row = start + lax.broadcasted_iota(jnp.int32, (near, LANES), 0)
    for part in range(2):
        lanes = pl.ds(part * LANES, LANES)
        for m in range(4):

            @pl.when(pick_ref[part, block] == m)
            def _(m=m):
                halo[...] = halos[part * 4 + m][0].astype(jnp.float32)

        mixes = []
        for branch in (1, 2):
            at = MED + branch * TAIL
            small[:TAIL, :] = halo[at : at + TAIL, :]
            small[TAIL:, :] = proj_ref[branch, 0, : 2 * TAIL, lanes][:TAIL].astype(jnp.float32)
            mixes.append(short_mix(small, reach8, taps_ref, branch, TAIL, lanes))
        first = lax.broadcasted_iota(jnp.int32, (TAIL, LANES), 0) < SHORT - 1
        early = (mixes[0] * mixes[1]).astype(jnp.bfloat16).astype(jnp.float32)
        prior[:MED, :] = halo[:MED, :]
        prior[MED:, :] = jnp.where(first, early, 0.0)
        filtered[...] = partial_ref[0, :, lanes]

        def genome(g, carry):
            low = jnp.where(g == 0, 0, ends_ref[jnp.maximum(g - 1, 0)])
            high = ends_ref[g]

            @pl.when((low < start + near) & (high > start))
            def _():
                value = jnp.where(row >= low, prior[...], 0.0)
                for s in range(TAIL):
                    shifted[s, TAIL : TAIL + TAIL, :] = jnp.zeros((TAIL, LANES), jnp.float32)
                    shifted[s, near + TAIL :, :] = jnp.zeros((GROUP, LANES), jnp.float32)
                    shifted[s, TAIL + s : TAIL + s + near, :] = value
                for r, (at, rows, begin) in enumerate(
                    ((0, GROUP, 0), (GROUP, GROUP, 7), (2 * GROUP, TAIL, 15))
                ):
                    total = taps_of(
                        shifted, medium_ref, lanes, TAIL + MED + at, begin, MED // TAIL, rows
                    )
                    here = out_row[at : at + rows]
                    total = jnp.where((here >= low) & (here < high), total, 0.0)
                    filtered[at : at + rows, :] += total

            return carry

        lax.fori_loop(0, 4, genome, 0)
        window[:TAIL, :] = halo[MED : MED + TAIL, :]
        window[TAIL:, :] = proj_ref[0, 0, :, lanes].astype(jnp.float32)

        @pl.when(cut)
        def _():
            mixed = short_mix(window, reach_of(start, BLK, ends_ref), taps_ref, 0, BLK, lanes)
            out_ref[0, :, lanes] = (mixed * filtered[...]).astype(jnp.bfloat16)

        @pl.when(jnp.logical_not(cut))
        def _():
            head = short_mix(window, reach8, taps_ref, 0, TAIL, lanes)
            mixed = short_mix(window, None, taps_ref, 0, BLK, lanes)
            mixed = jnp.concatenate([head, mixed[TAIL:]], axis=0)
            out_ref[0, :, lanes] = (mixed * filtered[...]).astype(jnp.bfloat16)


def edges(index, starts, ends, picks, proj, partial, taps, medium, halos):
    return pl.pallas_call(
        functools.partial(edge_kernel, index),
        grid_spec=pltpu.PrefetchScalarGridSpec(
            num_scalar_prefetch=3,
            grid=(2,),
            in_specs=[
                pl.BlockSpec((3, 1, BLK, 2 * LANES), lambda i, *_: (0, i * 2 + index, 0, 0)),
                pl.BlockSpec((1, BLK, 2 * LANES), lambda i, *_: (i, 0, 0)),
                pl.BlockSpec((SHORT, 3, 2 * LANES), lambda i, *_: (0, 0, 0)),
                pl.BlockSpec((MED, 2 * LANES), lambda i, *_: (0, 0)),
            ]
            + [pl.BlockSpec((1, HALO, LANES), lambda i, *_: (i * 2 + index, 0, 0))] * 8,
            out_specs=pl.BlockSpec((1, BLK, 2 * LANES), lambda i, *_: (i, 0, 0)),
            scratch_shapes=[
                pltpu.VMEM((HALO, LANES), jnp.float32),
                pltpu.VMEM((BLK + TAIL, LANES), jnp.float32),
                pltpu.VMEM((2 * TAIL, LANES), jnp.float32),
                pltpu.VMEM((MED + TAIL, LANES), jnp.float32),
                pltpu.VMEM((TAIL, MED + 2 * TAIL + GROUP, LANES), jnp.float32),
                pltpu.VMEM((BLK, LANES), jnp.float32),
            ],
        ),
        out_shape=jax.ShapeDtypeStruct((2, BLK, 2 * LANES), jnp.bfloat16),
        cost_estimate=pl.CostEstimate(
            flops=1024 * 256 * 64, bytes_accessed=3 << 20, transcendentals=0
        ),
        name="edges",
    )(starts, ends, picks, proj, partial, taps, medium, *halos)


def assemble_kernel(place_ref, *refs):
    columns, out_ref, sems = refs[:8], refs[8], refs[9]
    x, y, core = place_ref[0], place_ref[1], place_ref[2]
    started = []
    for other in range(2):
        for dy in range(4):
            for dx in range(4):
                to_x, to_y = lax.rem(x + dx, 4), lax.rem(y + dy, 4)
                owner = to_x * 4 + (to_y // 2) * 2 + lax.rem(core + other, 2)
                rows = pl.ds(pl.multiple_of(owner * 16, 16), 16)
                started.append(
                    pltpu.make_async_copy(
                        columns[other * 4 + dy].at[dx],
                        out_ref.at[lax.rem(to_y, 2), rows],
                        sems.at[other, dy, dx],
                    )
                )
    for copy in started:
        copy.start()
    for copy in started:
        copy.wait()


def assemble(place, columns):
    return pl.pallas_call(
        assemble_kernel,
        out_shape=jax.ShapeDtypeStruct((2, PIECE, D), jnp.bfloat16),
        in_specs=[scalars()] + [anywhere()] * 8,
        out_specs=full(),
        scratch_shapes=[pltpu.SemaphoreType.DMA((2, 4, 4))],
        cost_estimate=pl.CostEstimate(flops=1 << 10, bytes_accessed=8 << 20, transcendentals=0),
        name="assemble",
    )(place, *columns)


def output_kernel(place_ref, x_ref, y_ref, w_ref, *refs):
    pieces, (mine_ref, theirs_ref, scratch, sems) = refs[:8], refs[8:]
    core, y_low, z = place_ref[2], place_ref[3], place_ref[4]
    started = []
    for t, offset in enumerate(OFFSETS):
        for q in range(2):
            channel = lax.rem(z + offset + 8, 8) * 2 + lax.rem(core + q, 2)
            lanes = pl.ds(pl.multiple_of(channel * PIECE, PIECE), PIECE)
            started.append(
                pltpu.make_async_copy(pieces[t].at[q], scratch.at[:, lanes], sems.at[t, q])
            )
    for copy in started:
        copy.start()
    for copy in started:
        copy.wait()
    for side, (residual_ref, out_ref) in enumerate(((x_ref, mine_ref), (y_ref, theirs_ref))):
        summed = lax.dot_general(
            scratch[...], w_ref[lax.rem(y_low + side, 2)], (((1,), (1,)), ((), ())),
            preferred_element_type=jnp.float32,
        )
        out_ref[...] = (residual_ref[...].astype(jnp.float32) + summed).astype(jnp.bfloat16)


def output(place, residual, other_residual, weights, pieces):
    shape = jax.ShapeDtypeStruct((BLK, PIECE), jnp.bfloat16)
    return pl.pallas_call(
        output_kernel,
        out_shape=(shape, shape),
        in_specs=[scalars()] + [full()] * 3 + [anywhere()] * 8,
        out_specs=(full(), full()),
        scratch_shapes=[
            pltpu.VMEM((BLK, D), jnp.bfloat16), pltpu.SemaphoreType.DMA((8, 2)),
        ],
        compiler_params=pltpu.CompilerParams(vmem_limit_bytes=32 << 20),
        cost_estimate=pl.CostEstimate(
            flops=2 * BLK * D * HALF, bytes_accessed=6 << 20, transcendentals=0
        ),
        name="output",
    )(place, residual, other_residual, weights, *pieces)


def shards(
    tokens,
    norm_gain,
    in_weight,
    short_filter,
    medium_filter,
    out_weight,
    genome_lengths,
    block_at_slot,
):
    seq, fsdp = lax.axis_index("seq"), lax.axis_index("fsdp")
    x, core, y_low, z = seq // 4, seq % 2, fsdp // 8, fsdp % 8
    y = ((seq // 2) % 2) * 2 + y_low

    values = tokens.astype(jnp.float32)
    gain = lax.dynamic_index_in_dim(norm_gain.reshape(16, 1, PIECE), fsdp, 0, keepdims=False)
    scaled = (values * gain.astype(jnp.float32)).astype(jnp.bfloat16)
    square = jnp.sum(values * values, axis=1)
    parts = []
    for _ in range(3):
        part = lax.reduce_precision(square, exponent_bits=8, mantissa_bits=7)
        parts.append(part.astype(jnp.bfloat16).reshape(2, 2, PIECE))
        square = square - part
    parts.append(jnp.zeros((2, 2, PIECE), jnp.bfloat16))
    packed = jnp.concatenate([scaled.reshape(2, HALF, PIECE)] + parts, axis=1)
    mine = jnp.where(y_low == 0, packed[0], packed[1])
    theirs = send(jnp.where(y_low == 0, packed[1], packed[0]), swap_y)
    rings = (ring_z(mine, 1), ring_z(theirs, -1))
    pieces = [rings[t % 2][t // 2] for t in range(16)]
    pieces = pieces + [send(p, swap_core) for p in pieces]

    halves = in_weight.reshape(3, PIECE, 2, LANES)
    keep = jnp.where(core == 0, halves[:, :, 0], halves[:, :, 1])
    give = jnp.where(core == 0, halves[:, :, 1], halves[:, :, 0])
    other = send(give, swap_core)
    weights = axis_of(jnp.stack(axis_of(keep, along_x)), along_y)
    weights += axis_of(jnp.stack(axis_of(other, along_y)), along_x)

    owners = [((y_low + t) % 2) * 8 + (z + OFFSETS[t // 2]) % 8 for t in range(16)]
    owner = jnp.stack(owners).astype(jnp.int32)
    turn = jnp.arange(16, dtype=jnp.int32)
    where = jnp.sum(jnp.where(owner == turn[:, None], turn, 0), axis=1).astype(jnp.int32)
    place = jnp.stack([x, y, core, y_low, z]).astype(jnp.int32)
    proj = project(where, place, weights, pieces)

    both = jnp.concatenate([short_filter.reshape(SHORT * 3, PIECE), medium_filter], axis=0)
    both = jnp.where(core == 0, both[:, :LANES], both[:, LANES:])
    theirs = send(both, swap_y)
    both = jnp.concatenate(
        [jnp.where(y_low == 0, both, theirs), jnp.where(y_low == 0, theirs, both)], axis=1
    )
    taps = both[: SHORT * 3].reshape(SHORT, 3, 2 * LANES)
    medium = both[SHORT * 3 :].astype(jnp.float32)

    way = jnp.arange(2, dtype=jnp.int32).reshape(2, 1, 1, 1)
    ahead = jnp.arange(4, dtype=jnp.int32).reshape(1, 4, 1, 1)
    group = jnp.arange(2, dtype=jnp.int32).reshape(1, 1, 2, 1)
    index = jnp.arange(2, dtype=jnp.int32).reshape(1, 1, 1, 2)
    to_x, to_y = (x + way * ahead) % 4, (y + (1 - way) * ahead) % 4
    slots = (to_x * 4 + (to_y // 2) * 2 + (core + group) % 2) * 4 + (to_y % 2) * 2 + index
    slots = slots.reshape(32)
    all_slots = jnp.arange(block_at_slot.shape[0], dtype=jnp.int32)
    ids = jnp.sum(jnp.where(all_slots == slots[:, None], block_at_slot, 0), axis=1)
    previous = jnp.maximum(ids - 1, 0)
    before = jnp.sum(jnp.where(block_at_slot == previous[:, None], all_slots, 0), axis=1)
    before = before.reshape(2, 4, 4)
    from_x, from_y = before // 16, ((before // 8) % 2) * 2 + (before // 2) % 2
    local = ((before // 4 + core) % 2) * 2 + before % 2
    dx, dy = (from_x - x) % 4, (from_y - y) % 4
    table = jnp.stack(
        [jnp.where(dy[0] == 0, dx[0] * 4, 0) + local[0],
         jnp.where(dx[1] == 0, dy[1] * 4, 0) + local[1]]
    ).astype(jnp.int32)
    picks = jnp.stack([dy[0, 0], dx[1, 0]]).astype(jnp.int32)
    starts = (ids[:4] * BLK).astype(jnp.int32)
    ends = jnp.cumsum(genome_lengths).astype(jnp.int32)

    product, low, high = products(starts, ends, proj, taps)
    rows_x, rows_y = axis_of(low, along_x), axis_of(high, along_y)
    partials = [inner(i, starts, ends, product, medium) for i in range(2)]
    routed = route(table, rows_x + rows_y)
    halos = [routed[0]] + [send(routed[4 - d], along_y(4 - d)) for d in range(1, 4)]
    halos += [routed[4]] + [send(routed[8 - d], along_x(4 - d)) for d in range(1, 4)]

    columns = out_weight.reshape(2, 8, 2, LANES, 16).transpose(4, 1, 2, 0, 3).reshape(16, D)
    columns = jnp.stack(axis_of(columns, along_x))
    rows = tokens.reshape(2, 2, BLK, PIECE)
    residual = send(jnp.where(y_low == 0, rows[1], rows[0]), swap_y)
    mine = jnp.where(y_low == 0, rows[0], rows[1])
    chunks = []
    for i in range(2):
        gated = edges(i, starts, ends, picks, proj, partials[i], taps, medium, halos)
        if i == 0:
            gated, columns = lax.optimization_barrier((gated, columns))
        chunks.append(jnp.stack([gated[0], send(gated[1], swap_core)]))
    rings = [ring_z(chunks[0], 1), ring_z(chunks[1], -1)]
    columns = axis_of(columns, along_y)
    columns = assemble(place, columns + [send(c, swap_core) for c in columns])
    ours, theirs = [], []
    for i in range(2):
        here, there = output(place, mine[i], residual[i], columns, rings[i])
        ours.append(here)
        theirs.append(send(there, swap_y))
    ours, theirs = jnp.concatenate(ours), jnp.concatenate(theirs)
    first = jnp.where(y_low == 0, ours, theirs)
    second = jnp.where(y_low == 0, theirs, ours)
    return jnp.concatenate([first, second], axis=0)


def solution(mesh):
    in_specs = (
        P("seq", "fsdp"),
        P(),
        P(None, "seq", "fsdp"),
        P(None, None, "fsdp"),
        P(None, "fsdp"),
        P(None, ("fsdp", "seq")),
        P(),
        P(),
    )
    out_specs = P("seq", "fsdp")
    return jax.shard_map(shards, mesh=mesh, in_specs=in_specs, out_specs=out_specs, check_vma=False)
```

```python
import functools

import jax
import jax.numpy as jnp
from jax import lax
from jax.experimental import pallas as pl
from jax.experimental.pallas import tpu as pltpu
from jax.sharding import PartitionSpec as P


BLK = 256
SHORT = 7
MED = 128
LANES = 128
TAIL = 8
HALF = 512
PIECE = 256
D = 4096
HALO = MED + 3 * TAIL
AXES = ("seq", "fsdp")
epsilon = 1e-06


def linear(x, y, z, core):
    return (x * 4 + (y // 2) * 2 + core) * 16 + (y % 2) * 8 + z


def permutation(move):
    pairs = []
    for x in range(4):
        for y in range(4):
            for z in range(8):
                for core in range(2):
                    pairs.append((linear(x, y, z, core), linear(*move(x, y, z, core))))
    return pairs


def send(value, move):
    return lax.ppermute(value, AXES, permutation(move))


def along_x(step):
    return lambda x, y, z, core: ((x + step) % 4, y, z, core)


def along_y(step):
    return lambda x, y, z, core: (x, (y + step) % 4, z, core)


def swap_y(x, y, z, core):
    return (x, y ^ 1, z, core)


def swap_core(x, y, z, core):
    return (x, y, z, core ^ 1)


def gather_line(value):
    groups = [
        [linear(x, y, z, core) for z in range(8) for core in range(2)]
        for x in range(4)
        for y in range(4)
    ]
    return lax.all_gather(value, AXES, axis=0, axis_index_groups=groups)


def axis_of(chunk, along):
    return [chunk] + [send(chunk, along(-d)) for d in range(1, 4)]


def anywhere():
    return pl.BlockSpec(memory_space=pl.ANY)


def full():
    return pl.BlockSpec(memory_space=pltpu.VMEM)


def scalars():
    return pl.BlockSpec(memory_space=pltpu.SMEM)


def project_kernel(place_ref, line_ref, *refs):
    weights = refs[:8]
    out_ref, x_scratch, s_scratch, w_scratch, total, x_sems, s_sems, w_sems = refs[8:]
    x, y, core, y_low = place_ref[0], place_ref[1], place_ref[2], place_ref[3]

    def copies(i):
        made = []
        z, group = i // 2, lax.rem(i, 2)
        source = z * 2 + lax.rem(core + group, 2)
        rows = pl.ds(pl.multiple_of(group * HALF, HALF), HALF)
        for p in range(2):
            lanes = pl.ds(pl.multiple_of((z * 2 + p) * PIECE, PIECE), PIECE)
            made.append(
                pltpu.make_async_copy(
                    line_ref.at[source, p, pl.ds(0, HALF)], x_scratch.at[rows, lanes], x_sems.at[p, i]
                )
            )
            made.append(
                pltpu.make_async_copy(
                    line_ref.at[source, p, pl.ds(HALF, TAIL)], s_scratch.at[group, z * 2 + p],
                    s_sems.at[p, i],
                )
            )
        return made

    def start(i, carry):
        for copy in copies(i):
            copy.start()
        return carry

    def finish(i, carry):
        for copy in copies(i):
            copy.wait()
        return carry

    started = []
    for other in range(2):
        for a in range(4):
            for b in range(4):
                dx, dy = (b, a) if other == 0 else (a, b)
                to_x, to_y = lax.rem(x + dx, 4), lax.rem(y + dy, 4)
                owner = to_x * 4 + (to_y // 2) * 2 + lax.rem(core + other, 2)
                turn = lax.rem(owner, 8) * 2 + lax.rem(owner // 8 + y_low, 2)
                rows = pl.ds(pl.multiple_of(turn * PIECE, PIECE), PIECE)
                lanes = pl.ds(pl.multiple_of(lax.rem(to_y, 2) * LANES, LANES), LANES)
                started.append(
                    pltpu.make_async_copy(
                        weights[other * 4 + a].at[b],
                        w_scratch.at[:, rows, lanes],
                        w_sems.at[other, a, b],
                    )
                )
    lax.fori_loop(0, 16, start, 0)
    for copy in started:
        copy.start()
    lax.fori_loop(0, 16, finish, 0)
    for copy in started:
        copy.wait()

    def step(i, carry):
        branch, group = i // 2, lax.rem(i, 2)
        rows = pl.ds(pl.multiple_of(group * HALF, HALF), HALF)
        total[branch, rows, :] = jnp.dot(
            x_scratch[rows, :], w_scratch[branch], preferred_element_type=jnp.float32
        )
        return carry

    lax.fori_loop(0, 6, step, 0)
    for group in range(2):
        square = jnp.sum(s_scratch[group].astype(jnp.float32), axis=0)
        for i in range(2):
            row = square[i : i + 1] + square[i + 2 : i + 3] + square[i + 4 : i + 5]
            scale = lax.rsqrt(row / D + epsilon)
            scale = jnp.transpose(jnp.broadcast_to(scale, (LANES, PIECE)))
            scale = jnp.concatenate([scale, scale], axis=1)
            block = group * 2 + i

            def write(branch, carry, block=block, scale=scale):
                value = total[branch, block * BLK : (block + 1) * BLK, :]
                out_ref[branch, block] = (value * scale).astype(jnp.bfloat16)
                return carry

            lax.fori_loop(0, 3, write, 0)


def project(place, line, weights):
    return pl.pallas_call(
        project_kernel,
        out_shape=jax.ShapeDtypeStruct((3, 4, BLK, 2 * LANES), jnp.bfloat16),
        in_specs=[scalars()] + [anywhere()] * 9,
        out_specs=full(),
        scratch_shapes=[
            pltpu.VMEM((2 * HALF, D), jnp.bfloat16),
            pltpu.VMEM((2, 16, TAIL, PIECE), jnp.bfloat16),
            pltpu.VMEM((3, D, 2 * LANES), jnp.bfloat16),
            pltpu.VMEM((3, 2 * HALF, 2 * LANES), jnp.float32),
            pltpu.SemaphoreType.DMA((2, 16)),
            pltpu.SemaphoreType.DMA((2, 16)),
            pltpu.SemaphoreType.DMA((2, 4, 4)),
        ],
        compiler_params=pltpu.CompilerParams(vmem_limit_bytes=32 << 20),
        cost_estimate=pl.CostEstimate(
            flops=2 * 1024 * D * 768, bytes_accessed=16 << 20, transcendentals=0
        ),
        name="project",
    )(place, line, *weights)


def reach_of(start, rows, ends_ref):
    position = start + lax.broadcasted_iota(jnp.int32, (rows, LANES), 0)
    first = jnp.zeros((rows, LANES), jnp.int32)
    for g in range(3):
        end = ends_ref[g]
        first = jnp.maximum(first, jnp.where(position >= end, end, 0))
    return position - first


def split_by_genome(start, ends_ref):
    cut = False
    for g in range(3):
        cut = cut | ((ends_ref[g] > start) & (ends_ref[g] < start + BLK))
    return cut


def short_mix(window_ref, reach, taps_ref, branch, rows, lanes):
    total = jnp.zeros((rows, LANES), jnp.float32)
    for j in range(SHORT):
        part = window_ref[TAIL - j : TAIL - j + rows, :]
        if reach is not None:
            part = jnp.where(reach >= j, part, 0.0)
        total = total + part * taps_ref[j, branch : branch + 1, lanes].astype(jnp.float32)
    return total


def product_kernel(start_ref, ends_ref, proj_ref, taps_ref, out_ref, low_ref, high_ref, k, v):
    start = start_ref[pl.program_id(0)]
    cut = split_by_genome(start, ends_ref)
    for part, tail_ref in enumerate((low_ref, high_ref)):
        lanes = pl.ds(part * LANES, LANES)
        k[:TAIL, :] = jnp.zeros((TAIL, LANES), jnp.float32)
        v[:TAIL, :] = jnp.zeros((TAIL, LANES), jnp.float32)
        k[TAIL:, :] = proj_ref[1, 0, :, lanes].astype(jnp.float32)
        v[TAIL:, :] = proj_ref[2, 0, :, lanes].astype(jnp.float32)

        def store(reach):
            mixed = short_mix(k, reach, taps_ref, 1, BLK, lanes)
            product = mixed * short_mix(v, reach, taps_ref, 2, BLK, lanes)
            first = lax.broadcasted_iota(jnp.int32, (BLK, LANES), 0) >= SHORT - 1
            out_ref[0, :, lanes] = jnp.where(first, product, 0.0).astype(jnp.bfloat16)

        @pl.when(cut)
        def _():
            store(reach_of(start, BLK, ends_ref))

        @pl.when(jnp.logical_not(cut))
        def _():
            store(None)

        tail_ref[0, :MED, :] = out_ref[0, BLK - MED :, lanes]
        for branch in range(3):
            at = MED + branch * TAIL
            tail_ref[0, at : at + TAIL, :] = proj_ref[branch, 0, BLK - TAIL :, lanes]


def products(starts, ends, proj, taps):
    tail = jax.ShapeDtypeStruct((4, HALO, LANES), jnp.bfloat16)
    tail_spec = pl.BlockSpec((1, HALO, LANES), lambda i, *_: (i, 0, 0))
    return pl.pallas_call(
        product_kernel,
        grid_spec=pltpu.PrefetchScalarGridSpec(
            num_scalar_prefetch=2,
            grid=(4,),
            in_specs=[
                pl.BlockSpec((3, 1, BLK, 2 * LANES), lambda i, *_: (0, i, 0, 0)),
                pl.BlockSpec((SHORT, 3, 2 * LANES), lambda i, *_: (0, 0, 0)),
            ],
            out_specs=(
                pl.BlockSpec((1, BLK, 2 * LANES), lambda i, *_: (i, 0, 0)), tail_spec, tail_spec,
            ),
            scratch_shapes=[pltpu.VMEM((BLK + TAIL, LANES), jnp.float32)] * 2,
        ),
        out_shape=(jax.ShapeDtypeStruct((4, BLK, 2 * LANES), jnp.bfloat16), tail, tail),
        cost_estimate=pl.CostEstimate(
            flops=60 << 20, bytes_accessed=4 << 20, transcendentals=0
        ),
        name="products",
    )(starts, ends, proj, taps)


def taps_of(shifted, medium_ref, lanes, base, first, last, rows):
    def step(turn, total):
        at = pl.multiple_of(base - turn * TAIL, TAIL)
        weights = medium_ref[pl.ds(pl.multiple_of(turn * TAIL, TAIL), TAIL), lanes]
        for s in range(TAIL):
            total = total + shifted[s, pl.ds(at, rows), :] * weights[s : s + 1, :]
        return total

    return lax.fori_loop(first, last, step, jnp.zeros((rows, LANES), jnp.float32))


GROUP = 64


def inner_kernel(index, start_ref, ends_ref, product_ref, medium_ref, out_ref, shifted):
    start = start_ref[index * 2 + pl.program_id(0)]
    row = start + lax.broadcasted_iota(jnp.int32, (BLK, LANES), 0)
    cut = split_by_genome(start, ends_ref)

    for part in range(2):
        lanes = pl.ds(part * LANES, LANES)

        def run(low, high):
            value = product_ref[0, :, lanes].astype(jnp.float32)
            if low is not None:
                value = jnp.where(row >= low, value, 0.0)
            for s in range(TAIL):
                shifted[s, : GROUP + TAIL, :] = jnp.zeros((GROUP + TAIL, LANES), jnp.float32)
                shifted[s, GROUP + s : GROUP + BLK, :] = value[: BLK - s, :]
            for r in range(BLK // GROUP):
                last = min(MED // TAIL, (r + 1) * GROUP // TAIL)
                total = taps_of(
                    shifted, medium_ref, lanes, GROUP + r * GROUP, 0, last, GROUP
                )
                rows = pl.ds(r * GROUP, GROUP)
                if low is not None:
                    here = row[r * GROUP : (r + 1) * GROUP]
                    total = jnp.where((here >= low) & (here < high), total, out_ref[0, rows, lanes])
                out_ref[0, rows, lanes] = total

        @pl.when(jnp.logical_not(cut))
        def _():
            run(None, None)

        @pl.when(cut)
        def _():
            def genome(g, carry):
                low = jnp.where(g == 0, 0, ends_ref[jnp.maximum(g - 1, 0)])
                high = ends_ref[g]

                @pl.when((low < start + BLK) & (high > start))
                def _():
                    run(low, high)

                return carry

            lax.fori_loop(0, 4, genome, 0)


def inner(index, starts, ends, product, medium):
    return pl.pallas_call(
        functools.partial(inner_kernel, index),
        grid_spec=pltpu.PrefetchScalarGridSpec(
            num_scalar_prefetch=2,
            grid=(2,),
            in_specs=[
                pl.BlockSpec((1, BLK, 2 * LANES), lambda i, *_: (index * 2 + i, 0, 0)),
                pl.BlockSpec((MED, 2 * LANES), lambda i, *_: (0, 0)),
            ],
            out_specs=pl.BlockSpec((1, BLK, 2 * LANES), lambda i, *_: (i, 0, 0)),
            scratch_shapes=[pltpu.VMEM((TAIL, GROUP + BLK, LANES), jnp.float32)],
        ),
        out_shape=jax.ShapeDtypeStruct((2, BLK, 2 * LANES), jnp.float32),
        cost_estimate=pl.CostEstimate(
            flops=1024 * 256 * 128, bytes_accessed=1 << 20, transcendentals=0
        ),
        name="inner",
    )(starts, ends, product, medium)


def route_kernel(table_ref, *refs):
    ins, outs, every = refs[:8], refs[8:16], refs[16]
    for way in range(2):
        for d in range(4):
            every[d * 4 : (d + 1) * 4] = ins[way * 4 + d][...]
        for d in range(4):
            for j in range(4):
                outs[way * 4 + d][j] = every[table_ref[way, d, j]]


def route(table, ins):
    return pl.pallas_call(
        route_kernel,
        out_shape=(jax.ShapeDtypeStruct((4, HALO, LANES), jnp.bfloat16),) * 8,
        in_specs=[scalars()] + [full()] * 8,
        out_specs=(full(),) * 8,
        scratch_shapes=[pltpu.VMEM((16, HALO, LANES), jnp.bfloat16)],
        cost_estimate=pl.CostEstimate(flops=1 << 10, bytes_accessed=4 << 20, transcendentals=0),
        name="route",
    )(table, *ins)


def edge_kernel(
    start_ref, ends_ref, pick_ref, proj_ref, early_ref, late_ref, taps_ref, medium_ref, *refs
):
    halos, (out_ref, halo, window, small, prior, shifted, filtered) = refs[:8], refs[8:]
    block = pl.program_id(0)
    start = start_ref[block]
    cut = split_by_genome(start, ends_ref)
    near = MED + TAIL
    reach8 = reach_of(start, TAIL, ends_ref)
    row = start - MED + lax.broadcasted_iota(jnp.int32, (near, LANES), 0)
    out_row = start + lax.broadcasted_iota(jnp.int32, (near, LANES), 0)
    for part in range(2):
        lanes = pl.ds(part * LANES, LANES)
        for m in range(4):

            @pl.when(pick_ref[part, block] == m)
            def _(m=m):
                halo[...] = halos[part * 4 + m][0].astype(jnp.float32)

        mixes = []
        for branch in (1, 2):
            at = MED + branch * TAIL
            small[:TAIL, :] = halo[at : at + TAIL, :]
            small[TAIL:, :] = proj_ref[branch, 0, : 2 * TAIL, lanes][:TAIL].astype(jnp.float32)
            mixes.append(short_mix(small, reach8, taps_ref, branch, TAIL, lanes))
        first = lax.broadcasted_iota(jnp.int32, (TAIL, LANES), 0) < SHORT - 1
        early = (mixes[0] * mixes[1]).astype(jnp.bfloat16).astype(jnp.float32)
        prior[:MED, :] = halo[:MED, :]
        prior[MED:, :] = jnp.where(first, early, 0.0)

        @pl.when(block < 2)
        def _():
            filtered[...] = early_ref[0, :, lanes]

        @pl.when(block >= 2)
        def _():
            filtered[...] = late_ref[0, :, lanes]

        def genome(g, carry):
            low = jnp.where(g == 0, 0, ends_ref[jnp.maximum(g - 1, 0)])
            high = ends_ref[g]

            @pl.when((low < start + near) & (high > start))
            def _():
                value = jnp.where(row >= low, prior[...], 0.0)
                for s in range(TAIL):
                    shifted[s, TAIL : TAIL + TAIL, :] = jnp.zeros((TAIL, LANES), jnp.float32)
                    shifted[s, near + TAIL :, :] = jnp.zeros((GROUP, LANES), jnp.float32)
                    shifted[s, TAIL + s : TAIL + s + near, :] = value
                for r, (at, rows, begin) in enumerate(
                    ((0, GROUP, 0), (GROUP, GROUP, 7), (2 * GROUP, TAIL, 15))
                ):
                    total = taps_of(
                        shifted, medium_ref, lanes, TAIL + MED + at, begin, MED // TAIL, rows
                    )
                    here = out_row[at : at + rows]
                    total = jnp.where((here >= low) & (here < high), total, 0.0)
                    filtered[at : at + rows, :] += total

            return carry

        lax.fori_loop(0, 4, genome, 0)
        window[:TAIL, :] = halo[MED : MED + TAIL, :]
        window[TAIL:, :] = proj_ref[0, 0, :, lanes].astype(jnp.float32)

        @pl.when(cut)
        def _():
            mixed = short_mix(window, reach_of(start, BLK, ends_ref), taps_ref, 0, BLK, lanes)
            out_ref[0, :, lanes] = (mixed * filtered[...]).astype(jnp.bfloat16)

        @pl.when(jnp.logical_not(cut))
        def _():
            head = short_mix(window, reach8, taps_ref, 0, TAIL, lanes)
            mixed = short_mix(window, None, taps_ref, 0, BLK, lanes)
            mixed = jnp.concatenate([head, mixed[TAIL:]], axis=0)
            out_ref[0, :, lanes] = (mixed * filtered[...]).astype(jnp.bfloat16)


def edges(starts, ends, picks, proj, partials, taps, medium, halos):
    return pl.pallas_call(
        edge_kernel,
        grid_spec=pltpu.PrefetchScalarGridSpec(
            num_scalar_prefetch=3,
            grid=(4,),
            in_specs=[
                pl.BlockSpec((3, 1, BLK, 2 * LANES), lambda i, *_: (0, i, 0, 0)),
                pl.BlockSpec((1, BLK, 2 * LANES), lambda i, *_: (jnp.minimum(i, 1), 0, 0)),
                pl.BlockSpec((1, BLK, 2 * LANES), lambda i, *_: (jnp.maximum(i - 2, 0), 0, 0)),
                pl.BlockSpec((SHORT, 3, 2 * LANES), lambda i, *_: (0, 0, 0)),
                pl.BlockSpec((MED, 2 * LANES), lambda i, *_: (0, 0)),
            ]
            + [pl.BlockSpec((1, HALO, LANES), lambda i, *_: (i, 0, 0))] * 8,
            out_specs=pl.BlockSpec((1, BLK, 2 * LANES), lambda i, *_: (i, 0, 0)),
            scratch_shapes=[
                pltpu.VMEM((HALO, LANES), jnp.float32),
                pltpu.VMEM((BLK + TAIL, LANES), jnp.float32),
                pltpu.VMEM((2 * TAIL, LANES), jnp.float32),
                pltpu.VMEM((MED + TAIL, LANES), jnp.float32),
                pltpu.VMEM((TAIL, MED + 2 * TAIL + GROUP, LANES), jnp.float32),
                pltpu.VMEM((BLK, LANES), jnp.float32),
            ],
        ),
        out_shape=jax.ShapeDtypeStruct((4, BLK, 2 * LANES), jnp.bfloat16),
        cost_estimate=pl.CostEstimate(
            flops=1024 * 256 * 64, bytes_accessed=3 << 20, transcendentals=0
        ),
        name="edges",
    )(starts, ends, picks, proj, *partials, taps, medium, *halos)


def assemble_kernel(place_ref, own_ref, other_ref, out_ref, sems):
    x, y, core = place_ref[0], place_ref[1], place_ref[2]
    started = []
    for other, ref in enumerate((own_ref, other_ref)):
        for dy in range(4):
            for dx in range(4):
                to_x, to_y = lax.rem(x + dx, 4), lax.rem(y + dy, 4)
                owner = to_x * 4 + (to_y // 2) * 2 + lax.rem(core + other, 2)
                rows = pl.ds(pl.multiple_of(owner * 16, 16), 16)
                started.append(
                    pltpu.make_async_copy(
                        ref.at[dy, dx], out_ref.at[lax.rem(to_y, 2), rows], sems.at[other, dy, dx]
                    )
                )
    for copy in started:
        copy.start()
    for copy in started:
        copy.wait()


def assemble(place, own, other):
    return pl.pallas_call(
        assemble_kernel,
        out_shape=jax.ShapeDtypeStruct((2, PIECE, D), jnp.bfloat16),
        in_specs=[scalars()] + [anywhere()] * 2,
        out_specs=full(),
        scratch_shapes=[pltpu.SemaphoreType.DMA((2, 4, 4))],
        cost_estimate=pl.CostEstimate(flops=1 << 10, bytes_accessed=8 << 20, transcendentals=0),
        name="assemble",
    )(place, own, other)


def output_kernel(side, place_ref, residual_ref, w_ref, gated_ref, out_ref, scratch, total, sems):
    core, y_low = place_ref[2], place_ref[3]
    started = []
    for z in range(8):
        for owner in range(2):
            lanes = pl.ds((z * 2 + owner) * PIECE, PIECE)
            source = gated_ref.at[z * 2 + owner, lax.rem(core + owner, 2)]
            started.append(
                pltpu.make_async_copy(source, scratch.at[:, lanes], sems.at[z, owner])
            )
    for copy in started:
        copy.start()
    for copy in started:
        copy.wait()
    column = lax.rem(y_low + side, 2)
    total[...] = residual_ref[...].astype(jnp.float32)

    def step(i, carry):
        lanes = pl.ds(pl.multiple_of(i * 1024, 1024), 1024)
        total[...] += lax.dot_general(
            scratch[:, lanes], w_ref[column, :, lanes], (((1,), (1,)), ((), ())),
            preferred_element_type=jnp.float32,
        )
        return carry

    lax.fori_loop(0, 4, step, 0)
    out_ref[...] = total[...].astype(jnp.bfloat16)


def output(side, place, residual, weights, gated):
    return pl.pallas_call(
        functools.partial(output_kernel, side),
        out_shape=jax.ShapeDtypeStruct((HALF, PIECE), jnp.bfloat16),
        in_specs=[scalars()] + [full()] * 2 + [anywhere()],
        out_specs=full(),
        scratch_shapes=[
            pltpu.VMEM((HALF, D), jnp.bfloat16),
            pltpu.VMEM((HALF, PIECE), jnp.float32),
            pltpu.SemaphoreType.DMA((8, 2)),
        ],
        compiler_params=pltpu.CompilerParams(vmem_limit_bytes=32 << 20),
        cost_estimate=pl.CostEstimate(
            flops=2 * HALF * D * PIECE, bytes_accessed=6 << 20, transcendentals=0
        ),
        name="output",
    )(place, residual, weights, gated)


def shards(
    tokens,
    norm_gain,
    in_weight,
    short_filter,
    medium_filter,
    out_weight,
    genome_lengths,
    block_at_slot,
):
    seq, fsdp = lax.axis_index("seq"), lax.axis_index("fsdp")
    x, core, y_low, z = seq // 4, seq % 2, fsdp // 8, fsdp % 8
    y = ((seq // 2) % 2) * 2 + y_low

    values = tokens.astype(jnp.float32)
    gain = lax.dynamic_index_in_dim(norm_gain.reshape(16, 1, PIECE), fsdp, 0, keepdims=False)
    scaled = (values * gain.astype(jnp.float32)).astype(jnp.bfloat16)
    square = jnp.sum(values * values, axis=1)
    parts = []
    for _ in range(3):
        part = lax.reduce_precision(square, exponent_bits=8, mantissa_bits=7)
        parts.append(part.astype(jnp.bfloat16).reshape(2, 2, PIECE))
        square = square - part
    parts.append(jnp.zeros((2, 2, PIECE), jnp.bfloat16))
    packed = jnp.concatenate([scaled.reshape(2, HALF, PIECE)] + parts, axis=1)
    mine = jnp.where(y_low == 0, packed[0], packed[1])
    theirs = send(jnp.where(y_low == 0, packed[1], packed[0]), swap_y)
    line = gather_line(jnp.stack([mine, theirs]))

    halves = in_weight.reshape(3, PIECE, 2, LANES)
    keep = jnp.where(core == 0, halves[:, :, 0], halves[:, :, 1])
    give = jnp.where(core == 0, halves[:, :, 1], halves[:, :, 0])
    other = send(give, swap_core)
    weights = axis_of(jnp.stack(axis_of(keep, along_x)), along_y)
    weights += axis_of(jnp.stack(axis_of(other, along_y)), along_x)

    place = jnp.stack([x, y, core, y_low, z]).astype(jnp.int32)

    columns = out_weight.reshape(2, 8, 2, LANES, 16).transpose(4, 1, 2, 0, 3).reshape(16, D)
    columns = jnp.stack(axis_of(columns, along_x))
    place, columns = lax.optimization_barrier((place, columns))
    proj = project(place, line, weights)

    both = jnp.concatenate([short_filter.reshape(SHORT * 3, PIECE), medium_filter], axis=0)
    both = jnp.where(core == 0, both[:, :LANES], both[:, LANES:])
    theirs = send(both, swap_y)
    both = jnp.concatenate(
        [jnp.where(y_low == 0, both, theirs), jnp.where(y_low == 0, theirs, both)], axis=1
    )
    taps = both[: SHORT * 3].reshape(SHORT, 3, 2 * LANES)
    medium = both[SHORT * 3 :].astype(jnp.float32)

    way = jnp.arange(2, dtype=jnp.int32).reshape(2, 1, 1, 1)
    ahead = jnp.arange(4, dtype=jnp.int32).reshape(1, 4, 1, 1)
    group = jnp.arange(2, dtype=jnp.int32).reshape(1, 1, 2, 1)
    index = jnp.arange(2, dtype=jnp.int32).reshape(1, 1, 1, 2)
    to_x, to_y = (x + way * ahead) % 4, (y + (1 - way) * ahead) % 4
    slots = (to_x * 4 + (to_y // 2) * 2 + (core + group) % 2) * 4 + (to_y % 2) * 2 + index
    slots = slots.reshape(32)
    all_slots = jnp.arange(block_at_slot.shape[0], dtype=jnp.int32)
    ids = jnp.sum(jnp.where(all_slots == slots[:, None], block_at_slot, 0), axis=1)
    previous = jnp.maximum(ids - 1, 0)
    before = jnp.sum(jnp.where(block_at_slot == previous[:, None], all_slots, 0), axis=1)
    before = before.reshape(2, 4, 4)
    from_x, from_y = before // 16, ((before // 8) % 2) * 2 + (before // 2) % 2
    local = ((before // 4 + core) % 2) * 2 + before % 2
    dx, dy = (from_x - x) % 4, (from_y - y) % 4
    table = jnp.stack(
        [jnp.where(dy[0] == 0, dx[0] * 4, 0) + local[0],
         jnp.where(dx[1] == 0, dy[1] * 4, 0) + local[1]]
    ).astype(jnp.int32)
    picks = jnp.stack([dy[0, 0], dx[1, 0]]).astype(jnp.int32)
    starts = (ids[:4] * BLK).astype(jnp.int32)
    ends = jnp.cumsum(genome_lengths).astype(jnp.int32)

    product, low, high = products(starts, ends, proj, taps)
    rows_x, rows_y = axis_of(low, along_x), axis_of(high, along_y)
    partials = [inner(i, starts, ends, product, medium) for i in range(2)]
    table, partials[0] = lax.optimization_barrier((table, partials[0]))
    routed = route(table, rows_x + rows_y)
    halos = [routed[0]] + [send(routed[4 - d], along_y(4 - d)) for d in range(1, 4)]
    halos += [routed[4]] + [send(routed[8 - d], along_x(4 - d)) for d in range(1, 4)]

    rows = tokens.reshape(2, HALF, PIECE)
    residual = send(jnp.where(y_low == 0, rows[1], rows[0]), swap_y)
    mine = jnp.where(y_low == 0, rows[0], rows[1])
    gated = edges(starts, ends, picks, proj, partials, taps, medium, halos)
    columns = lax.optimization_barrier((columns, gated))[0]
    gathered = gather_line(gated.reshape(2, HALF, 2 * LANES))
    columns = jnp.stack(axis_of(columns, along_y))
    columns = assemble(place, columns, send(columns, swap_core))
    theirs = output(1, place, residual, columns, gathered)
    place, theirs = lax.optimization_barrier((place, theirs))
    theirs = send(theirs, swap_y)
    ours = output(0, place, mine, columns, gathered)
    first = jnp.where(y_low == 0, ours, theirs)
    second = jnp.where(y_low == 0, theirs, ours)
    return jnp.concatenate([first, second], axis=0)


def solution(mesh):
    in_specs = (
        P("seq", "fsdp"),
        P(),
        P(None, "seq", "fsdp"),
        P(None, None, "fsdp"),
        P(None, "fsdp"),
        P(None, ("fsdp", "seq")),
        P(),
        P(),
    )
    out_specs = P("seq", "fsdp")
    return jax.shard_map(shards, mesh=mesh, in_specs=in_specs, out_specs=out_specs, check_vma=False)
```

```python
import functools

import jax
import jax.numpy as jnp
from jax import lax
from jax.experimental import pallas as pl
from jax.experimental.pallas import tpu as pltpu
from jax.sharding import PartitionSpec as P


BLK = 256
SHORT = 7
MED = 128
LANES = 128
TAIL = 8
HALF = 512
PIECE = 256
D = 4096
HALO = MED + 3 * TAIL
AXES = ("seq", "fsdp")
epsilon = 1e-06


def linear(x, y, z, core):
    return (x * 4 + (y // 2) * 2 + core) * 16 + (y % 2) * 8 + z


def permutation(move):
    pairs = []
    for x in range(4):
        for y in range(4):
            for z in range(8):
                for core in range(2):
                    pairs.append((linear(x, y, z, core), linear(*move(x, y, z, core))))
    return pairs


def send(value, move):
    return lax.ppermute(value, AXES, permutation(move))


def along_x(step):
    return lambda x, y, z, core: ((x + step) % 4, y, z, core)


def along_y(step):
    return lambda x, y, z, core: (x, (y + step) % 4, z, core)


def swap_y(x, y, z, core):
    return (x, y ^ 1, z, core)


def swap_core(x, y, z, core):
    return (x, y, z, core ^ 1)


def gather_line(value):
    groups = [
        [linear(x, y, z, core) for z in range(8) for core in range(2)]
        for x in range(4)
        for y in range(4)
    ]
    return lax.all_gather(value, AXES, axis=0, axis_index_groups=groups)


def axis_of(chunk, along):
    return [chunk] + [send(chunk, along(-d)) for d in range(1, 4)]


def anywhere():
    return pl.BlockSpec(memory_space=pltpu.HBM)


def full():
    return pl.BlockSpec(memory_space=pltpu.VMEM)


def scalars():
    return pl.BlockSpec(memory_space=pltpu.SMEM)


def project_kernel(place_ref, line_ref, *refs):
    weights = refs[:8]
    out_ref, x_scratch, s_scratch, w_scratch, total, x_sems, s_sems, w_sems = refs[8:]
    x, y, core, y_low = place_ref[0], place_ref[1], place_ref[2], place_ref[3]

    def copies(i):
        made = []
        z, group = i // 2, lax.rem(i, 2)
        source = z * 2 + lax.rem(core + group, 2)
        rows = pl.ds(pl.multiple_of(group * HALF, HALF), HALF)
        for p in range(2):
            lanes = pl.ds(pl.multiple_of((z * 2 + p) * PIECE, PIECE), PIECE)
            made.append(
                pltpu.make_async_copy(
                    line_ref.at[source, p, pl.ds(0, HALF)], x_scratch.at[rows, lanes], x_sems.at[p, i]
                )
            )
            made.append(
                pltpu.make_async_copy(
                    line_ref.at[source, p, pl.ds(HALF, TAIL)], s_scratch.at[group, z * 2 + p],
                    s_sems.at[p, i],
                )
            )
        return made

    def start(i, carry):
        for copy in copies(i):
            copy.start()
        return carry

    def finish(i, carry):
        for copy in copies(i):
            copy.wait()
        return carry

    started = []
    for other in range(2):
        for a in range(4):
            for b in range(4):
                dx, dy = (b, a) if other == 0 else (a, b)
                to_x, to_y = lax.rem(x + dx, 4), lax.rem(y + dy, 4)
                owner = to_x * 4 + (to_y // 2) * 2 + lax.rem(core + other, 2)
                turn = lax.rem(owner, 8) * 2 + lax.rem(owner // 8 + y_low, 2)
                rows = pl.ds(pl.multiple_of(turn * PIECE, PIECE), PIECE)
                lanes = pl.ds(pl.multiple_of(lax.rem(to_y, 2) * LANES, LANES), LANES)
                started.append(
                    pltpu.make_async_copy(
                        weights[other * 4 + a].at[b],
                        w_scratch.at[:, rows, lanes],
                        w_sems.at[other, a, b],
                    )
                )
    for copy in started:
        copy.start()
    lax.fori_loop(0, 16, start, 0)
    for copy in started:
        copy.wait()

    def half(part, carry):
        lax.fori_loop(part * 8, part * 8 + 8, finish, 0)
        depth = pl.ds(pl.multiple_of(part * (D // 2), D // 2), D // 2)

        def step(i, carry):
            branch, group = i // 2, lax.rem(i, 2)
            rows = pl.ds(pl.multiple_of(group * HALF, HALF), HALF)
            product = jnp.dot(
                x_scratch[rows, depth], w_scratch[branch, depth, :],
                preferred_element_type=jnp.float32,
            )

            @pl.when(part == 0)
            def _():
                total[branch, rows, :] = product

            @pl.when(part == 1)
            def _():
                total[branch, rows, :] += product

            return carry

        return lax.fori_loop(0, 6, step, carry)

    lax.fori_loop(0, 2, half, 0)
    for group in range(2):
        square = jnp.sum(s_scratch[group].astype(jnp.float32), axis=0)
        for i in range(2):
            row = square[i : i + 1] + square[i + 2 : i + 3] + square[i + 4 : i + 5]
            scale = lax.rsqrt(row / D + epsilon)
            scale = jnp.transpose(jnp.broadcast_to(scale, (LANES, PIECE)))
            scale = jnp.concatenate([scale, scale], axis=1)
            block = group * 2 + i

            def write(branch, carry, block=block, scale=scale):
                value = total[branch, block * BLK : (block + 1) * BLK, :]
                out_ref[branch, block] = (value * scale).astype(jnp.bfloat16)
                return carry

            lax.fori_loop(0, 3, write, 0)


def project(place, line, weights):
    return pl.pallas_call(
        project_kernel,
        out_shape=jax.ShapeDtypeStruct((3, 4, BLK, 2 * LANES), jnp.bfloat16),
        in_specs=[scalars()] + [anywhere()] * 9,
        out_specs=full(),
        scratch_shapes=[
            pltpu.VMEM((2 * HALF, D), jnp.bfloat16),
            pltpu.VMEM((2, 16, TAIL, PIECE), jnp.bfloat16),
            pltpu.VMEM((3, D, 2 * LANES), jnp.bfloat16),
            pltpu.VMEM((3, 2 * HALF, 2 * LANES), jnp.float32),
            pltpu.SemaphoreType.DMA((2, 16)),
            pltpu.SemaphoreType.DMA((2, 16)),
            pltpu.SemaphoreType.DMA((2, 4, 4)),
        ],
        compiler_params=pltpu.CompilerParams(vmem_limit_bytes=32 << 20),
        cost_estimate=pl.CostEstimate(
            flops=2 * 1024 * D * 768, bytes_accessed=16 << 20, transcendentals=0
        ),
        name="project",
    )(place, line, *weights)


def reach_of(start, rows, ends_ref):
    position = start + lax.broadcasted_iota(jnp.int32, (rows, LANES), 0)
    first = jnp.zeros((rows, LANES), jnp.int32)
    for g in range(3):
        end = ends_ref[g]
        first = jnp.maximum(first, jnp.where(position >= end, end, 0))
    return position - first


def split_by_genome(start, ends_ref):
    cut = False
    for g in range(3):
        cut = cut | ((ends_ref[g] > start) & (ends_ref[g] < start + BLK))
    return cut


def short_mix(window_ref, reach, taps_ref, branch, rows, lanes):
    total = jnp.zeros((rows, LANES), jnp.float32)
    for j in range(SHORT):
        part = window_ref[TAIL - j : TAIL - j + rows, :]
        if reach is not None:
            part = jnp.where(reach >= j, part, 0.0)
        total = total + part * taps_ref[j, branch : branch + 1, lanes].astype(jnp.float32)
    return total


def product_kernel(start_ref, ends_ref, proj_ref, taps_ref, out_ref, tail_ref, k, v):
    start = start_ref[pl.program_id(0)]
    cut = split_by_genome(start, ends_ref)
    for part in range(2):
        lanes = pl.ds(part * LANES, LANES)
        k[:TAIL, :] = jnp.zeros((TAIL, LANES), jnp.float32)
        v[:TAIL, :] = jnp.zeros((TAIL, LANES), jnp.float32)
        k[TAIL:, :] = proj_ref[1, 0, :, lanes].astype(jnp.float32)
        v[TAIL:, :] = proj_ref[2, 0, :, lanes].astype(jnp.float32)

        def store(reach):
            mixed = short_mix(k, reach, taps_ref, 1, BLK, lanes)
            product = mixed * short_mix(v, reach, taps_ref, 2, BLK, lanes)
            first = lax.broadcasted_iota(jnp.int32, (BLK, LANES), 0) >= SHORT - 1
            out_ref[0, :, lanes] = jnp.where(first, product, 0.0).astype(jnp.bfloat16)

        @pl.when(cut)
        def _():
            store(reach_of(start, BLK, ends_ref))

        @pl.when(jnp.logical_not(cut))
        def _():
            store(None)

        tail_ref[0, :MED, lanes] = out_ref[0, BLK - MED :, lanes]
        for branch in range(3):
            at = MED + branch * TAIL
            tail_ref[0, at : at + TAIL, lanes] = proj_ref[branch, 0, BLK - TAIL :, lanes]


def products(starts, ends, proj, taps):
    tail = jax.ShapeDtypeStruct((4, HALO, 2 * LANES), jnp.bfloat16)
    tail_spec = pl.BlockSpec((1, HALO, 2 * LANES), lambda i, *_: (i, 0, 0))
    return pl.pallas_call(
        product_kernel,
        grid_spec=pltpu.PrefetchScalarGridSpec(
            num_scalar_prefetch=2,
            grid=(4,),
            in_specs=[
                pl.BlockSpec((3, 1, BLK, 2 * LANES), lambda i, *_: (0, i, 0, 0)),
                pl.BlockSpec((SHORT, 3, 2 * LANES), lambda i, *_: (0, 0, 0)),
            ],
            out_specs=(
                pl.BlockSpec((1, BLK, 2 * LANES), lambda i, *_: (i, 0, 0)), tail_spec,
            ),
            scratch_shapes=[pltpu.VMEM((BLK + TAIL, LANES), jnp.float32)] * 2,
        ),
        out_shape=(jax.ShapeDtypeStruct((4, BLK, 2 * LANES), jnp.bfloat16), tail),
        cost_estimate=pl.CostEstimate(
            flops=60 << 20, bytes_accessed=4 << 20, transcendentals=0
        ),
        name="products",
    )(starts, ends, proj, taps)


def taps_of(shifted, medium_ref, lanes, base, first, last, rows):
    def step(turn, total):
        at = pl.multiple_of(base - turn * TAIL, TAIL)
        weights = medium_ref[pl.ds(pl.multiple_of(turn * TAIL, TAIL), TAIL), lanes]
        for s in range(TAIL):
            total = total + shifted[s, pl.ds(at, rows), :] * weights[s : s + 1, :]
        return total

    return lax.fori_loop(first, last, step, jnp.zeros((rows, LANES), jnp.float32))


GROUP = 64


def inner_kernel(index, start_ref, ends_ref, product_ref, medium_ref, out_ref, shifted):
    start = start_ref[index * 2 + pl.program_id(0)]
    row = start + lax.broadcasted_iota(jnp.int32, (BLK, LANES), 0)
    cut = split_by_genome(start, ends_ref)

    for part in range(2):
        lanes = pl.ds(part * LANES, LANES)

        def run(low, high):
            value = product_ref[0, :, lanes].astype(jnp.float32)
            if low is not None:
                value = jnp.where(row >= low, value, 0.0)
            for s in range(TAIL):
                shifted[s, : GROUP + TAIL, :] = jnp.zeros((GROUP + TAIL, LANES), jnp.float32)
                shifted[s, GROUP + s : GROUP + BLK, :] = value[: BLK - s, :]
            for r in range(BLK // GROUP):
                last = min(MED // TAIL, (r + 1) * GROUP // TAIL)
                total = taps_of(
                    shifted, medium_ref, lanes, GROUP + r * GROUP, 0, last, GROUP
                )
                rows = pl.ds(r * GROUP, GROUP)
                if low is not None:
                    here = row[r * GROUP : (r + 1) * GROUP]
                    total = jnp.where((here >= low) & (here < high), total, out_ref[0, rows, lanes])
                out_ref[0, rows, lanes] = total

        @pl.when(jnp.logical_not(cut))
        def _():
            run(None, None)

        @pl.when(cut)
        def _():
            def genome(g, carry):
                low = jnp.where(g == 0, 0, ends_ref[jnp.maximum(g - 1, 0)])
                high = ends_ref[g]

                @pl.when((low < start + BLK) & (high > start))
                def _():
                    run(low, high)

                return carry

            lax.fori_loop(0, 4, genome, 0)


def inner(index, starts, ends, product, medium):
    return pl.pallas_call(
        functools.partial(inner_kernel, index),
        grid_spec=pltpu.PrefetchScalarGridSpec(
            num_scalar_prefetch=2,
            grid=(2,),
            in_specs=[
                pl.BlockSpec((1, BLK, 2 * LANES), lambda i, *_: (index * 2 + i, 0, 0)),
                pl.BlockSpec((MED, 2 * LANES), lambda i, *_: (0, 0)),
            ],
            out_specs=pl.BlockSpec((1, BLK, 2 * LANES), lambda i, *_: (i, 0, 0)),
            scratch_shapes=[pltpu.VMEM((TAIL, GROUP + BLK, LANES), jnp.float32)],
        ),
        out_shape=jax.ShapeDtypeStruct((2, BLK, 2 * LANES), jnp.float32),
        cost_estimate=pl.CostEstimate(
            flops=1024 * 256 * 128, bytes_accessed=1 << 20, transcendentals=0
        ),
        name="inner",
    )(starts, ends, product, medium)


def route_kernel(table_ref, *refs):
    ins, outs, every = refs[:4], refs[4:8], refs[8]
    for d in range(4):
        every[d * 4 : (d + 1) * 4] = ins[d][...]
    for d in range(4):
        for j in range(4):
            outs[d][j] = every[table_ref[d, j]]


def route(table, ins):
    return pl.pallas_call(
        route_kernel,
        out_shape=(jax.ShapeDtypeStruct((4, HALO, 2 * LANES), jnp.bfloat16),) * 4,
        in_specs=[scalars()] + [full()] * 4,
        out_specs=(full(),) * 4,
        scratch_shapes=[pltpu.VMEM((16, HALO, 2 * LANES), jnp.bfloat16)],
        cost_estimate=pl.CostEstimate(flops=1 << 10, bytes_accessed=4 << 20, transcendentals=0),
        name="route",
    )(table, *ins)


def edge_kernel(
    start_ref, ends_ref, pick_ref, proj_ref, early_ref, late_ref, taps_ref, medium_ref, *refs
):
    halos, (out_ref, halo, window, small, prior, shifted, filtered) = refs[:4], refs[4:]
    block = pl.program_id(0)
    start = start_ref[block]
    cut = split_by_genome(start, ends_ref)
    near = MED + TAIL
    reach8 = reach_of(start, TAIL, ends_ref)
    row = start - MED + lax.broadcasted_iota(jnp.int32, (near, LANES), 0)
    out_row = start + lax.broadcasted_iota(jnp.int32, (near, LANES), 0)
    for part in range(2):
        lanes = pl.ds(part * LANES, LANES)
        for m in range(4):

            @pl.when(pick_ref[block] == m)
            def _(m=m):
                halo[...] = halos[m][0, :, lanes].astype(jnp.float32)

        mixes = []
        for branch in (1, 2):
            at = MED + branch * TAIL
            small[:TAIL, :] = halo[at : at + TAIL, :]
            small[TAIL:, :] = proj_ref[branch, 0, : 2 * TAIL, lanes][:TAIL].astype(jnp.float32)
            mixes.append(short_mix(small, reach8, taps_ref, branch, TAIL, lanes))
        first = lax.broadcasted_iota(jnp.int32, (TAIL, LANES), 0) < SHORT - 1
        early = (mixes[0] * mixes[1]).astype(jnp.bfloat16).astype(jnp.float32)
        prior[:MED, :] = halo[:MED, :]
        prior[MED:, :] = jnp.where(first, early, 0.0)

        @pl.when(block < 2)
        def _():
            filtered[...] = early_ref[0, :, lanes]

        @pl.when(block >= 2)
        def _():
            filtered[...] = late_ref[0, :, lanes]

        def genome(g, carry):
            low = jnp.where(g == 0, 0, ends_ref[jnp.maximum(g - 1, 0)])
            high = ends_ref[g]

            @pl.when((low < start + near) & (high > start))
            def _():
                value = jnp.where(row >= low, prior[...], 0.0)
                for s in range(TAIL):
                    shifted[s, TAIL : TAIL + TAIL, :] = jnp.zeros((TAIL, LANES), jnp.float32)
                    shifted[s, near + TAIL :, :] = jnp.zeros((GROUP, LANES), jnp.float32)
                    shifted[s, TAIL + s : TAIL + s + near, :] = value
                for at, rows, begin in ((0, GROUP, 0), (GROUP, GROUP, 7), (2 * GROUP, TAIL, 15)):
                    total = taps_of(
                        shifted, medium_ref, lanes, TAIL + MED + at, begin, MED // TAIL, rows
                    )
                    here = out_row[at : at + rows]
                    total = jnp.where((here >= low) & (here < high), total, 0.0)
                    filtered[at : at + rows, :] += total

            return carry

        lax.fori_loop(0, 4, genome, 0)
        window[:TAIL, :] = halo[MED : MED + TAIL, :]
        window[TAIL:, :] = proj_ref[0, 0, :, lanes].astype(jnp.float32)

        @pl.when(cut)
        def _():
            mixed = short_mix(window, reach_of(start, BLK, ends_ref), taps_ref, 0, BLK, lanes)
            out_ref[0, :, lanes] = (mixed * filtered[...]).astype(jnp.bfloat16)

        @pl.when(jnp.logical_not(cut))
        def _():
            head = short_mix(window, reach8, taps_ref, 0, TAIL, lanes)
            mixed = short_mix(window, None, taps_ref, 0, BLK, lanes)
            mixed = jnp.concatenate([head, mixed[TAIL:]], axis=0)
            out_ref[0, :, lanes] = (mixed * filtered[...]).astype(jnp.bfloat16)


def edges(starts, ends, picks, proj, partials, taps, medium, halos):
    return pl.pallas_call(
        edge_kernel,
        grid_spec=pltpu.PrefetchScalarGridSpec(
            num_scalar_prefetch=3,
            grid=(4,),
            in_specs=[
                pl.BlockSpec((3, 1, BLK, 2 * LANES), lambda i, *_: (0, i, 0, 0)),
                pl.BlockSpec((1, BLK, 2 * LANES), lambda i, *_: (jnp.minimum(i, 1), 0, 0)),
                pl.BlockSpec((1, BLK, 2 * LANES), lambda i, *_: (jnp.maximum(i - 2, 0), 0, 0)),
                pl.BlockSpec((SHORT, 3, 2 * LANES), lambda i, *_: (0, 0, 0)),
                pl.BlockSpec((MED, 2 * LANES), lambda i, *_: (0, 0)),
            ]
            + [pl.BlockSpec((1, HALO, 2 * LANES), lambda i, *_: (i, 0, 0))] * 4,
            out_specs=pl.BlockSpec((1, BLK, 2 * LANES), lambda i, *_: (i, 0, 0)),
            scratch_shapes=[
                pltpu.VMEM((HALO, LANES), jnp.float32),
                pltpu.VMEM((BLK + TAIL, LANES), jnp.float32),
                pltpu.VMEM((2 * TAIL, LANES), jnp.float32),
                pltpu.VMEM((MED + TAIL, LANES), jnp.float32),
                pltpu.VMEM((TAIL, MED + 2 * TAIL + GROUP, LANES), jnp.float32),
                pltpu.VMEM((BLK, LANES), jnp.float32),
            ],
        ),
        out_shape=jax.ShapeDtypeStruct((4, BLK, 2 * LANES), jnp.bfloat16),
        cost_estimate=pl.CostEstimate(
            flops=1024 * 256 * 64, bytes_accessed=3 << 20, transcendentals=0
        ),
        name="edges",
    )(starts, ends, picks, proj, *partials, taps, medium, *halos)


def assemble_kernel(place_ref, own_ref, other_ref, out_ref, sems):
    x, y, core = place_ref[0], place_ref[1], place_ref[2]
    started = []
    for other, ref in enumerate((own_ref, other_ref)):
        for dy in range(4):
            for dx in range(4):
                to_x, to_y = lax.rem(x + dx, 4), lax.rem(y + dy, 4)
                owner = to_x * 4 + (to_y // 2) * 2 + lax.rem(core + other, 2)
                rows = pl.ds(pl.multiple_of(owner * 16, 16), 16)
                started.append(
                    pltpu.make_async_copy(
                        ref.at[dy, dx], out_ref.at[lax.rem(to_y, 2), rows], sems.at[other, dy, dx]
                    )
                )
    for copy in started:
        copy.start()
    for copy in started:
        copy.wait()


def assemble(place, own, other):
    return pl.pallas_call(
        assemble_kernel,
        out_shape=jax.ShapeDtypeStruct((2, PIECE, D), jnp.bfloat16),
        in_specs=[scalars()] + [anywhere()] * 2,
        out_specs=full(),
        scratch_shapes=[pltpu.SemaphoreType.DMA((2, 4, 4))],
        cost_estimate=pl.CostEstimate(flops=1 << 10, bytes_accessed=8 << 20, transcendentals=0),
        name="assemble",
    )(place, own, other)


def output_kernel(side, place_ref, residual_ref, w_ref, gated_ref, out_ref, scratch, total, sems):
    core, y_low = place_ref[2], place_ref[3]
    started = []
    for z in range(8):
        for owner in range(2):
            lanes = pl.ds((z * 2 + owner) * PIECE, PIECE)
            source = gated_ref.at[z * 2 + owner, lax.rem(core + owner, 2)]
            started.append(
                pltpu.make_async_copy(source, scratch.at[:, lanes], sems.at[z, owner])
            )
    for copy in started:
        copy.start()
    for copy in started:
        copy.wait()
    column = lax.rem(y_low + side, 2)
    total[...] = residual_ref[...].astype(jnp.float32)

    def step(i, carry):
        lanes = pl.ds(pl.multiple_of(i * 1024, 1024), 1024)
        total[...] += lax.dot_general(
            scratch[:, lanes], w_ref[column, :, lanes], (((1,), (1,)), ((), ())),
            preferred_element_type=jnp.float32,
        )
        return carry

    lax.fori_loop(0, 4, step, 0)
    out_ref[...] = total[...].astype(jnp.bfloat16)


def output(side, place, residual, weights, gated):
    return pl.pallas_call(
        functools.partial(output_kernel, side),
        out_shape=jax.ShapeDtypeStruct((HALF, PIECE), jnp.bfloat16),
        in_specs=[scalars()] + [full()] * 2 + [anywhere()],
        out_specs=full(),
        scratch_shapes=[
            pltpu.VMEM((HALF, D), jnp.bfloat16),
            pltpu.VMEM((HALF, PIECE), jnp.float32),
            pltpu.SemaphoreType.DMA((8, 2)),
        ],
        compiler_params=pltpu.CompilerParams(vmem_limit_bytes=32 << 20),
        cost_estimate=pl.CostEstimate(
            flops=2 * HALF * D * PIECE, bytes_accessed=6 << 20, transcendentals=0
        ),
        name="output",
    )(place, residual, weights, gated)


def block(
    tokens,
    norm_gain,
    in_weight,
    short_filter,
    medium_filter,
    out_weight,
    genome_lengths,
    block_at_slot,
):
    seq, fsdp = lax.axis_index("seq"), lax.axis_index("fsdp")
    x, core, y_low, z = seq // 4, seq % 2, fsdp // 8, fsdp % 8
    y = ((seq // 2) % 2) * 2 + y_low

    values = tokens.astype(jnp.float32)
    gain = lax.dynamic_index_in_dim(norm_gain.reshape(16, 1, PIECE), fsdp, 0, keepdims=False)
    scaled = (values * gain.astype(jnp.float32)).astype(jnp.bfloat16)
    square = jnp.sum(values * values, axis=1)
    parts = []
    for _ in range(3):
        part = lax.reduce_precision(square, exponent_bits=8, mantissa_bits=7)
        parts.append(part.astype(jnp.bfloat16).reshape(2, 2, PIECE))
        square = square - part
    parts.append(jnp.zeros((2, 2, PIECE), jnp.bfloat16))
    packed = jnp.concatenate([scaled.reshape(2, HALF, PIECE)] + parts, axis=1)
    mine = jnp.where(y_low == 0, packed[0], packed[1])
    theirs = send(jnp.where(y_low == 0, packed[1], packed[0]), swap_y)
    pair = jnp.stack([mine, theirs])
    line = gather_line(pair)

    halves = in_weight.reshape(3, PIECE, 2, LANES)
    keep = jnp.where(core == 0, halves[:, :, 0], halves[:, :, 1])
    give = jnp.where(core == 0, halves[:, :, 1], halves[:, :, 0])
    other = send(give, swap_core)
    first = axis_of(keep, along_x)
    weights = axis_of(jnp.stack(first), along_y)
    weights += axis_of(jnp.stack(axis_of(other, along_y)), along_x)

    place = jnp.stack([x, y, core, y_low, z]).astype(jnp.int32)

    columns = out_weight.reshape(2, 8, 2, LANES, 16).transpose(4, 1, 2, 0, 3).reshape(16, D)
    columns = jnp.stack(axis_of(columns, along_x))
    place, columns = lax.optimization_barrier((place, columns))
    proj = project(place, line, weights)

    both = jnp.concatenate([short_filter.reshape(SHORT * 3, PIECE), medium_filter], axis=0)
    both = jnp.where(core == 0, both[:, :LANES], both[:, LANES:])
    theirs = send(both, swap_y)
    both = jnp.concatenate(
        [jnp.where(y_low == 0, both, theirs), jnp.where(y_low == 0, theirs, both)], axis=1
    )
    taps = both[: SHORT * 3].reshape(SHORT, 3, 2 * LANES)
    medium = both[SHORT * 3 :].astype(jnp.float32)

    ahead = jnp.arange(4, dtype=jnp.int32).reshape(4, 1, 1)
    group = jnp.arange(2, dtype=jnp.int32).reshape(1, 2, 1)
    index = jnp.arange(2, dtype=jnp.int32).reshape(1, 1, 2)
    to_y = (y + ahead) % 4
    slots = (x * 4 + (to_y // 2) * 2 + (core + group) % 2) * 4 + (to_y % 2) * 2 + index
    slots = slots.reshape(16)
    all_slots = jnp.arange(block_at_slot.shape[0], dtype=jnp.int32)
    ids = jnp.sum(jnp.where(all_slots == slots[:, None], block_at_slot, 0), axis=1)
    previous = jnp.maximum(ids - 1, 0)
    before = jnp.sum(jnp.where(block_at_slot == previous[:, None], all_slots, 0), axis=1)
    before = before.reshape(4, 4)
    from_x, from_y = before // 16, ((before // 8) % 2) * 2 + (before // 2) % 2
    local = ((before // 4 + core) % 2) * 2 + before % 2
    dx, dy = (from_x - x) % 4, (from_y - y) % 4
    table = (jnp.where(dy == 0, dx * 4, 0) + local).astype(jnp.int32)
    picks = dy[0].astype(jnp.int32)
    starts = (ids[:4] * BLK).astype(jnp.int32)
    ends = jnp.cumsum(genome_lengths).astype(jnp.int32)

    product, tail = products(starts, ends, proj, taps)
    tails = axis_of(tail, along_x)
    partials = [inner(i, starts, ends, product, medium) for i in range(2)]
    table, partials[0] = lax.optimization_barrier((table, partials[0]))
    routed = route(table, tails)
    halos = [routed[0]] + [send(routed[4 - d], along_y(4 - d)) for d in range(1, 4)]

    rows = tokens.reshape(2, HALF, PIECE)
    residual = send(jnp.where(y_low == 0, rows[1], rows[0]), swap_y)
    mine = jnp.where(y_low == 0, rows[0], rows[1])
    gated = edges(starts, ends, picks, proj, partials, taps, medium, halos)
    columns = lax.optimization_barrier((columns, gated))[0]
    gathered = gather_line(gated.reshape(2, HALF, 2 * LANES))
    columns = jnp.stack(axis_of(columns, along_y))
    columns = assemble(place, columns, send(columns, swap_core))
    theirs = output(1, place, residual, columns, gathered)
    place, theirs = lax.optimization_barrier((place, theirs))
    theirs = send(theirs, swap_y)
    ours = output(0, place, mine, columns, gathered)
    first = jnp.where(y_low == 0, ours, theirs)
    second = jnp.where(y_low == 0, theirs, ours)
    return jnp.concatenate([first, second], axis=0)


def solution(mesh):
    in_specs = (
        P("seq", "fsdp"),
        P(),
        P(None, "seq", "fsdp"),
        P(None, None, "fsdp"),
        P(None, "fsdp"),
        P(None, ("fsdp", "seq")),
        P(),
        P(),
    )
    out_specs = P("seq", "fsdp")
    return jax.shard_map(block, mesh=mesh, in_specs=in_specs, out_specs=out_specs, check_vma=False)
```

```python
import functools

import jax
import jax.numpy as jnp
from jax import lax
from jax.experimental import pallas as pl
from jax.experimental.pallas import tpu as pltpu
from jax.sharding import PartitionSpec as P


BLK = 256
SHORT = 7
MED = 128
LANES = 128
TAIL = 8
HALF = 512
PIECE = 256
D = 4096
HALO = MED + 3 * TAIL
AXES = ("seq", "fsdp")
epsilon = 1e-06


def linear(x, y, z, core):
    return (x * 4 + (y // 2) * 2 + core) * 16 + (y % 2) * 8 + z


def permutation(move):
    pairs = []
    for x in range(4):
        for y in range(4):
            for z in range(8):
                for core in range(2):
                    pairs.append((linear(x, y, z, core), linear(*move(x, y, z, core))))
    return pairs


def send(value, move):
    return lax.ppermute(value, AXES, permutation(move))


def along_x(step):
    return lambda x, y, z, core: ((x + step) % 4, y, z, core)


def along_y(step):
    return lambda x, y, z, core: (x, (y + step) % 4, z, core)


def swap_y(x, y, z, core):
    return (x, y ^ 1, z, core)


def swap_core(x, y, z, core):
    return (x, y, z, core ^ 1)


def gather_line(value):
    groups = [
        [linear(x, y, z, core) for z in range(8) for core in range(2)]
        for x in range(4)
        for y in range(4)
    ]
    return lax.all_gather(value, AXES, axis=0, axis_index_groups=groups)


def axis_of(chunk, along):
    return [chunk] + [send(chunk, along(-d)) for d in range(1, 4)]


def anywhere():
    return pl.BlockSpec(memory_space=pl.ANY)


def full():
    return pl.BlockSpec(memory_space=pltpu.VMEM)


def scalars():
    return pl.BlockSpec(memory_space=pltpu.SMEM)


def project_kernel(place_ref, line_ref, *refs):
    weights = refs[:8]
    out_ref, x_scratch, s_scratch, w_scratch, total, x_sems, s_sems, w_sems = refs[8:]
    x, y, core, y_low = place_ref[0], place_ref[1], place_ref[2], place_ref[3]

    def copies(i):
        made = []
        z, group = i // 2, lax.rem(i, 2)
        source = z * 2 + lax.rem(core + group, 2)
        rows = pl.ds(pl.multiple_of(group * HALF, HALF), HALF)
        for p in range(2):
            lanes = pl.ds(pl.multiple_of((z * 2 + p) * PIECE, PIECE), PIECE)
            made.append(
                pltpu.make_async_copy(
                    line_ref.at[source, p, pl.ds(0, HALF)], x_scratch.at[rows, lanes], x_sems.at[p, i]
                )
            )
            made.append(
                pltpu.make_async_copy(
                    line_ref.at[source, p, pl.ds(HALF, TAIL)], s_scratch.at[group, z * 2 + p],
                    s_sems.at[p, i],
                )
            )
        return made

    def start(i, carry):
        for copy in copies(i):
            copy.start()
        return carry

    def finish(i, carry):
        for copy in copies(i):
            copy.wait()
        return carry

    started = []
    for other in range(2):
        for a in range(4):
            for b in range(4):
                dx, dy = (b, a) if other == 0 else (a, b)
                to_x, to_y = lax.rem(x + dx, 4), lax.rem(y + dy, 4)
                owner = to_x * 4 + (to_y // 2) * 2 + lax.rem(core + other, 2)
                turn = lax.rem(owner, 8) * 2 + lax.rem(owner // 8 + y_low, 2)
                rows = pl.ds(pl.multiple_of(turn * PIECE, PIECE), PIECE)
                lanes = pl.ds(pl.multiple_of(lax.rem(to_y, 2) * LANES, LANES), LANES)
                started.append(
                    pltpu.make_async_copy(
                        weights[other * 4 + a].at[b],
                        w_scratch.at[:, rows, lanes],
                        w_sems.at[other, a, b],
                    )
                )
    for copy in started:
        copy.start()
    lax.fori_loop(0, 16, start, 0)
    for copy in started:
        copy.wait()

    def half(part, carry):
        lax.fori_loop(part * 8, part * 8 + 8, finish, 0)
        depth = pl.ds(pl.multiple_of(part * (D // 2), D // 2), D // 2)

        def step(i, carry):
            branch, group = i // 2, lax.rem(i, 2)
            rows = pl.ds(pl.multiple_of(group * HALF, HALF), HALF)
            product = jnp.dot(
                x_scratch[rows, depth], w_scratch[branch, depth, :],
                preferred_element_type=jnp.float32,
            )

            @pl.when(part == 0)
            def _():
                total[branch, rows, :] = product

            @pl.when(part == 1)
            def _():
                total[branch, rows, :] += product

            return carry

        return lax.fori_loop(0, 6, step, carry)

    lax.fori_loop(0, 2, half, 0)
    for group in range(2):
        square = jnp.sum(s_scratch[group].astype(jnp.float32), axis=0)
        for i in range(2):
            row = square[i : i + 1] + square[i + 2 : i + 3] + square[i + 4 : i + 5]
            scale = lax.rsqrt(row / D + epsilon)
            scale = jnp.transpose(jnp.broadcast_to(scale, (LANES, PIECE)))
            scale = jnp.concatenate([scale, scale], axis=1)
            block = group * 2 + i

            def write(branch, carry, block=block, scale=scale):
                value = total[branch, block * BLK : (block + 1) * BLK, :]
                out_ref[branch, block] = (value * scale).astype(jnp.bfloat16)
                return carry

            lax.fori_loop(0, 3, write, 0)


def project(place, line, weights):
    return pl.pallas_call(
        project_kernel,
        out_shape=jax.ShapeDtypeStruct((3, 4, BLK, 2 * LANES), jnp.bfloat16),
        in_specs=[scalars()] + [anywhere()] * 9,
        out_specs=full(),
        scratch_shapes=[
            pltpu.VMEM((2 * HALF, D), jnp.bfloat16),
            pltpu.VMEM((2, 16, TAIL, PIECE), jnp.bfloat16),
            pltpu.VMEM((3, D, 2 * LANES), jnp.bfloat16),
            pltpu.VMEM((3, 2 * HALF, 2 * LANES), jnp.float32),
            pltpu.SemaphoreType.DMA((2, 16)),
            pltpu.SemaphoreType.DMA((2, 16)),
            pltpu.SemaphoreType.DMA((2, 4, 4)),
        ],
        cost_estimate=pl.CostEstimate(
            flops=2 * 1024 * D * 768, bytes_accessed=16 << 20, transcendentals=0
        ),
        name="project",
    )(place, line, *weights)


def reach_of(start, rows, ends_ref):
    position = start + lax.broadcasted_iota(jnp.int32, (rows, LANES), 0)
    first = jnp.zeros((rows, LANES), jnp.int32)
    for g in range(3):
        end = ends_ref[g]
        first = jnp.maximum(first, jnp.where(position >= end, end, 0))
    return position - first


def split_by_genome(start, ends_ref):
    cut = False
    for g in range(3):
        cut = cut | ((ends_ref[g] > start) & (ends_ref[g] < start + BLK))
    return cut


def short_mix(window_ref, reach, taps_ref, branch, rows, lanes):
    total = jnp.zeros((rows, LANES), jnp.float32)
    for j in range(SHORT):
        part = window_ref[TAIL - j : TAIL - j + rows, :]
        if reach is not None:
            part = jnp.where(reach >= j, part, 0.0)
        total = total + part * taps_ref[j, branch : branch + 1, lanes].astype(jnp.float32)
    return total


def product_kernel(start_ref, ends_ref, proj_ref, taps_ref, out_ref, low_ref, high_ref, k, v):
    start = start_ref[pl.program_id(0)]
    cut = split_by_genome(start, ends_ref)
    for part, tail_ref in enumerate((low_ref, high_ref)):
        lanes = pl.ds(part * LANES, LANES)
        k[:TAIL, :] = jnp.zeros((TAIL, LANES), jnp.float32)
        v[:TAIL, :] = jnp.zeros((TAIL, LANES), jnp.float32)
        k[TAIL:, :] = proj_ref[1, 0, :, lanes].astype(jnp.float32)
        v[TAIL:, :] = proj_ref[2, 0, :, lanes].astype(jnp.float32)

        def store(reach):
            mixed = short_mix(k, reach, taps_ref, 1, BLK, lanes)
            product = mixed * short_mix(v, reach, taps_ref, 2, BLK, lanes)
            first = lax.broadcasted_iota(jnp.int32, (BLK, LANES), 0) >= SHORT - 1
            out_ref[0, :, lanes] = jnp.where(first, product, 0.0).astype(jnp.bfloat16)

        @pl.when(cut)
        def _():
            store(reach_of(start, BLK, ends_ref))

        @pl.when(jnp.logical_not(cut))
        def _():
            store(None)

        tail_ref[0, :MED, :] = out_ref[0, BLK - MED :, lanes]
        for branch in range(3):
            at = MED + branch * TAIL
            tail_ref[0, at : at + TAIL, :] = proj_ref[branch, 0, BLK - TAIL :, lanes]


def products(starts, ends, proj, taps):
    tail = jax.ShapeDtypeStruct((4, HALO, LANES), jnp.bfloat16)
    tail_spec = pl.BlockSpec((1, HALO, LANES), lambda i, *_: (i, 0, 0))
    return pl.pallas_call(
        product_kernel,
        grid_spec=pltpu.PrefetchScalarGridSpec(
            num_scalar_prefetch=2,
            grid=(4,),
            in_specs=[
                pl.BlockSpec((3, 1, BLK, 2 * LANES), lambda i, *_: (0, i, 0, 0)),
                pl.BlockSpec((SHORT, 3, 2 * LANES), lambda i, *_: (0, 0, 0)),
            ],
            out_specs=(
                pl.BlockSpec((1, BLK, 2 * LANES), lambda i, *_: (i, 0, 0)), tail_spec, tail_spec,
            ),
            scratch_shapes=[pltpu.VMEM((BLK + TAIL, LANES), jnp.float32)] * 2,
        ),
        out_shape=(jax.ShapeDtypeStruct((4, BLK, 2 * LANES), jnp.bfloat16), tail, tail),
        cost_estimate=pl.CostEstimate(
            flops=60 << 20, bytes_accessed=4 << 20, transcendentals=0
        ),
        name="products",
    )(starts, ends, proj, taps)


def taps_of(shifted, medium_ref, lanes, base, first, last, rows):
    def step(turn, total):
        at = pl.multiple_of(base - turn * TAIL, TAIL)
        weights = medium_ref[pl.ds(pl.multiple_of(turn * TAIL, TAIL), TAIL), lanes]
        for s in range(TAIL):
            total = total + shifted[s, pl.ds(at, rows), :] * weights[s : s + 1, :]
        return total

    return lax.fori_loop(first, last, step, jnp.zeros((rows, LANES), jnp.float32))


GROUP = 64


def inner_kernel(index, start_ref, ends_ref, product_ref, medium_ref, out_ref, shifted):
    start = start_ref[index * 2 + pl.program_id(0)]
    row = start + lax.broadcasted_iota(jnp.int32, (BLK, LANES), 0)
    cut = split_by_genome(start, ends_ref)

    for part in range(2):
        lanes = pl.ds(part * LANES, LANES)

        def run(low, high):
            value = product_ref[0, :, lanes].astype(jnp.float32)
            if low is not None:
                value = jnp.where(row >= low, value, 0.0)
            for s in range(TAIL):
                shifted[s, : GROUP + TAIL, :] = jnp.zeros((GROUP + TAIL, LANES), jnp.float32)
                shifted[s, GROUP + s : GROUP + BLK, :] = value[: BLK - s, :]
            for r in range(BLK // GROUP):
                last = min(MED // TAIL, (r + 1) * GROUP // TAIL)
                total = taps_of(
                    shifted, medium_ref, lanes, GROUP + r * GROUP, 0, last, GROUP
                )
                rows = pl.ds(r * GROUP, GROUP)
                if low is not None:
                    here = row[r * GROUP : (r + 1) * GROUP]
                    total = jnp.where((here >= low) & (here < high), total, out_ref[0, rows, lanes])
                out_ref[0, rows, lanes] = total

        @pl.when(jnp.logical_not(cut))
        def _():
            run(None, None)

        @pl.when(cut)
        def _():
            def genome(g, carry):
                low = jnp.where(g == 0, 0, ends_ref[jnp.maximum(g - 1, 0)])
                high = ends_ref[g]

                @pl.when((low < start + BLK) & (high > start))
                def _():
                    run(low, high)

                return carry

            lax.fori_loop(0, 4, genome, 0)


def inner(index, starts, ends, product, medium):
    return pl.pallas_call(
        functools.partial(inner_kernel, index),
        grid_spec=pltpu.PrefetchScalarGridSpec(
            num_scalar_prefetch=2,
            grid=(2,),
            in_specs=[
                pl.BlockSpec((1, BLK, 2 * LANES), lambda i, *_: (index * 2 + i, 0, 0)),
                pl.BlockSpec((MED, 2 * LANES), lambda i, *_: (0, 0)),
            ],
            out_specs=pl.BlockSpec((1, BLK, 2 * LANES), lambda i, *_: (i, 0, 0)),
            scratch_shapes=[pltpu.VMEM((TAIL, GROUP + BLK, LANES), jnp.float32)],
        ),
        out_shape=jax.ShapeDtypeStruct((2, BLK, 2 * LANES), jnp.float32),
        cost_estimate=pl.CostEstimate(
            flops=1024 * 256 * 128, bytes_accessed=1 << 20, transcendentals=0
        ),
        name="inner",
    )(starts, ends, product, medium)


def route_kernel(table_ref, *refs):
    ins, outs, every = refs[:8], refs[8:16], refs[16]
    for way in range(2):
        for d in range(4):
            every[d * 4 : (d + 1) * 4] = ins[way * 4 + d][...]
        for d in range(4):
            for j in range(4):
                outs[way * 4 + d][j] = every[table_ref[way, d, j]]


def route(table, ins):
    return pl.pallas_call(
        route_kernel,
        out_shape=(jax.ShapeDtypeStruct((4, HALO, LANES), jnp.bfloat16),) * 8,
        in_specs=[scalars()] + [full()] * 8,
        out_specs=(full(),) * 8,
        scratch_shapes=[pltpu.VMEM((16, HALO, LANES), jnp.bfloat16)],
        cost_estimate=pl.CostEstimate(flops=1 << 10, bytes_accessed=4 << 20, transcendentals=0),
        name="route",
    )(table, *ins)


def edge_kernel(
    start_ref, ends_ref, pick_ref, proj_ref, early_ref, late_ref, taps_ref, medium_ref, *refs
):
    halos, (out_ref, halo, window, small, prior, shifted, filtered) = refs[:8], refs[8:]
    block = pl.program_id(0)
    start = start_ref[block]
    cut = split_by_genome(start, ends_ref)
    near = MED + TAIL
    reach8 = reach_of(start, TAIL, ends_ref)
    row = start - MED + lax.broadcasted_iota(jnp.int32, (near, LANES), 0)
    out_row = start + lax.broadcasted_iota(jnp.int32, (near, LANES), 0)
    for part in range(2):
        lanes = pl.ds(part * LANES, LANES)
        for m in range(4):

            @pl.when(pick_ref[part, block] == m)
            def _(m=m):
                halo[...] = halos[part * 4 + m][0].astype(jnp.float32)

        mixes = []
        for branch in (1, 2):
            at = MED + branch * TAIL
            small[:TAIL, :] = halo[at : at + TAIL, :]
            small[TAIL:, :] = proj_ref[branch, 0, : 2 * TAIL, lanes][:TAIL].astype(jnp.float32)
            mixes.append(short_mix(small, reach8, taps_ref, branch, TAIL, lanes))
        first = lax.broadcasted_iota(jnp.int32, (TAIL, LANES), 0) < SHORT - 1
        early = (mixes[0] * mixes[1]).astype(jnp.bfloat16).astype(jnp.float32)
        prior[:MED, :] = halo[:MED, :]
        prior[MED:, :] = jnp.where(first, early, 0.0)

        @pl.when(block < 2)
        def _():
            filtered[...] = early_ref[0, :, lanes]

        @pl.when(block >= 2)
        def _():
            filtered[...] = late_ref[0, :, lanes]

        def genome(g, carry):
            low = jnp.where(g == 0, 0, ends_ref[jnp.maximum(g - 1, 0)])
            high = ends_ref[g]

            @pl.when((low < start + near) & (high > start))
            def _():
                value = jnp.where(row >= low, prior[...], 0.0)
                for s in range(TAIL):
                    shifted[s, TAIL : TAIL + TAIL, :] = jnp.zeros((TAIL, LANES), jnp.float32)
                    shifted[s, near + TAIL :, :] = jnp.zeros((GROUP, LANES), jnp.float32)
                    shifted[s, TAIL + s : TAIL + s + near, :] = value
                for at, rows, begin in ((0, GROUP, 0), (GROUP, GROUP, 7), (2 * GROUP, TAIL, 15)):
                    total = taps_of(
                        shifted, medium_ref, lanes, TAIL + MED + at, begin, MED // TAIL, rows
                    )
                    here = out_row[at : at + rows]
                    total = jnp.where((here >= low) & (here < high), total, 0.0)
                    filtered[at : at + rows, :] += total

            return carry

        lax.fori_loop(0, 4, genome, 0)
        window[:TAIL, :] = halo[MED : MED + TAIL, :]
        window[TAIL:, :] = proj_ref[0, 0, :, lanes].astype(jnp.float32)

        @pl.when(cut)
        def _():
            mixed = short_mix(window, reach_of(start, BLK, ends_ref), taps_ref, 0, BLK, lanes)
            out_ref[0, :, lanes] = (mixed * filtered[...]).astype(jnp.bfloat16)

        @pl.when(jnp.logical_not(cut))
        def _():
            head = short_mix(window, reach8, taps_ref, 0, TAIL, lanes)
            mixed = short_mix(window, None, taps_ref, 0, BLK, lanes)
            mixed = jnp.concatenate([head, mixed[TAIL:]], axis=0)
            out_ref[0, :, lanes] = (mixed * filtered[...]).astype(jnp.bfloat16)


def edges(starts, ends, picks, proj, partials, taps, medium, halos):
    return pl.pallas_call(
        edge_kernel,
        grid_spec=pltpu.PrefetchScalarGridSpec(
            num_scalar_prefetch=3,
            grid=(4,),
            in_specs=[
                pl.BlockSpec((3, 1, BLK, 2 * LANES), lambda i, *_: (0, i, 0, 0)),
                pl.BlockSpec((1, BLK, 2 * LANES), lambda i, *_: (jnp.minimum(i, 1), 0, 0)),
                pl.BlockSpec((1, BLK, 2 * LANES), lambda i, *_: (jnp.maximum(i - 2, 0), 0, 0)),
                pl.BlockSpec((SHORT, 3, 2 * LANES), lambda i, *_: (0, 0, 0)),
                pl.BlockSpec((MED, 2 * LANES), lambda i, *_: (0, 0)),
            ]
            + [pl.BlockSpec((1, HALO, LANES), lambda i, *_: (i, 0, 0))] * 8,
            out_specs=pl.BlockSpec((1, BLK, 2 * LANES), lambda i, *_: (i, 0, 0)),
            scratch_shapes=[
                pltpu.VMEM((HALO, LANES), jnp.float32),
                pltpu.VMEM((BLK + TAIL, LANES), jnp.float32),
                pltpu.VMEM((2 * TAIL, LANES), jnp.float32),
                pltpu.VMEM((MED + TAIL, LANES), jnp.float32),
                pltpu.VMEM((TAIL, MED + 2 * TAIL + GROUP, LANES), jnp.float32),
                pltpu.VMEM((BLK, LANES), jnp.float32),
            ],
        ),
        out_shape=jax.ShapeDtypeStruct((4, BLK, 2 * LANES), jnp.bfloat16),
        cost_estimate=pl.CostEstimate(
            flops=1024 * 256 * 64, bytes_accessed=3 << 20, transcendentals=0
        ),
        name="edges",
    )(starts, ends, picks, proj, *partials, taps, medium, *halos)


def assemble_kernel(place_ref, own_ref, other_ref, out_ref, sems):
    x, y, core = place_ref[0], place_ref[1], place_ref[2]
    started = []
    for other, ref in enumerate((own_ref, other_ref)):
        for dy in range(4):
            for dx in range(4):
                to_x, to_y = lax.rem(x + dx, 4), lax.rem(y + dy, 4)
                owner = to_x * 4 + (to_y // 2) * 2 + lax.rem(core + other, 2)
                rows = pl.ds(pl.multiple_of(owner * 16, 16), 16)
                started.append(
                    pltpu.make_async_copy(
                        ref.at[dy, dx], out_ref.at[lax.rem(to_y, 2), rows], sems.at[other, dy, dx]
                    )
                )
    for copy in started:
        copy.start()
    for copy in started:
        copy.wait()


def assemble(place, own, other):
    return pl.pallas_call(
        assemble_kernel,
        out_shape=jax.ShapeDtypeStruct((2, PIECE, D), jnp.bfloat16),
        in_specs=[scalars()] + [anywhere()] * 2,
        out_specs=full(),
        scratch_shapes=[pltpu.SemaphoreType.DMA((2, 4, 4))],
        cost_estimate=pl.CostEstimate(flops=1 << 10, bytes_accessed=8 << 20, transcendentals=0),
        name="assemble",
    )(place, own, other)


def output_kernel(side, place_ref, residual_ref, w_ref, gated_ref, out_ref, scratch, weights, total, sems, w_sem):
    core, y_low = place_ref[2], place_ref[3]
    load = pltpu.make_async_copy(w_ref.at[lax.rem(y_low + side, 2)], weights, w_sem)
    load.start()
    started = []
    for z in range(8):
        for owner in range(2):
            lanes = pl.ds((z * 2 + owner) * PIECE, PIECE)
            source = gated_ref.at[z * 2 + owner, lax.rem(core + owner, 2)]
            started.append(
                pltpu.make_async_copy(source, scratch.at[:, lanes], sems.at[z, owner])
            )
    for copy in started:
        copy.start()
    for copy in started:
        copy.wait()
    load.wait()
    total[...] = residual_ref[...].astype(jnp.float32)

    def step(i, carry):
        lanes = pl.ds(pl.multiple_of(i * 1024, 1024), 1024)
        total[...] += lax.dot_general(
            scratch[:, lanes], weights[:, lanes], (((1,), (1,)), ((), ())),
            preferred_element_type=jnp.float32,
        )
        return carry

    lax.fori_loop(0, 4, step, 0)
    out_ref[...] = total[...].astype(jnp.bfloat16)


def output(side, place, residual, weights, gated):
    return pl.pallas_call(
        functools.partial(output_kernel, side),
        out_shape=jax.ShapeDtypeStruct((HALF, PIECE), jnp.bfloat16),
        in_specs=[scalars(), full()] + [anywhere()] * 2,
        out_specs=full(),
        scratch_shapes=[
            pltpu.VMEM((HALF, D), jnp.bfloat16),
            pltpu.VMEM((PIECE, D), jnp.bfloat16),
            pltpu.VMEM((HALF, PIECE), jnp.float32),
            pltpu.SemaphoreType.DMA((8, 2)),
            pltpu.SemaphoreType.DMA,
        ],
        cost_estimate=pl.CostEstimate(
            flops=2 * HALF * D * PIECE, bytes_accessed=6 << 20, transcendentals=0
        ),
        name="output",
    )(place, residual, weights, gated)


def block(
    tokens,
    norm_gain,
    in_weight,
    short_filter,
    medium_filter,
    out_weight,
    genome_lengths,
    block_at_slot,
):
    seq, fsdp = lax.axis_index("seq"), lax.axis_index("fsdp")
    x, core, y_low, z = seq // 4, seq % 2, fsdp // 8, fsdp % 8
    y = ((seq // 2) % 2) * 2 + y_low

    values = tokens.astype(jnp.float32)
    gain = lax.dynamic_index_in_dim(norm_gain.reshape(16, 1, PIECE), fsdp, 0, keepdims=False)
    scaled = (values * gain.astype(jnp.float32)).astype(jnp.bfloat16)
    square = jnp.sum(values * values, axis=1)
    parts = []
    for _ in range(3):
        part = lax.reduce_precision(square, exponent_bits=8, mantissa_bits=7)
        parts.append(part.astype(jnp.bfloat16).reshape(2, 2, PIECE))
        square = square - part
    parts.append(jnp.zeros((2, 2, PIECE), jnp.bfloat16))
    packed = jnp.concatenate([scaled.reshape(2, HALF, PIECE)] + parts, axis=1)
    mine = jnp.where(y_low == 0, packed[0], packed[1])
    theirs = send(jnp.where(y_low == 0, packed[1], packed[0]), swap_y)
    pair = jnp.stack([mine, theirs])
    line = gather_line(pair)

    halves = in_weight.reshape(3, PIECE, 2, LANES)
    keep = jnp.where(core == 0, halves[:, :, 0], halves[:, :, 1])
    give = jnp.where(core == 0, halves[:, :, 1], halves[:, :, 0])
    other = send(give, swap_core)
    first = axis_of(keep, along_x)
    first, other = jnp.stack(first), jnp.stack(axis_of(other, along_y))
    weights = axis_of(first, along_y) + axis_of(other, along_x)

    place = jnp.stack([x, y, core, y_low, z]).astype(jnp.int32)

    columns = out_weight.reshape(2, 8, 2, LANES, 16).transpose(4, 1, 2, 0, 3).reshape(16, D)
    columns = axis_of(columns, along_x)
    columns = jnp.stack(columns)
    place, columns = lax.optimization_barrier((place, columns))
    proj = project(place, line, weights)

    both = jnp.concatenate([short_filter.reshape(SHORT * 3, PIECE), medium_filter], axis=0)
    both = jnp.where(core == 0, both[:, :LANES], both[:, LANES:])
    theirs = send(both, swap_y)
    both = jnp.concatenate(
        [jnp.where(y_low == 0, both, theirs), jnp.where(y_low == 0, theirs, both)], axis=1
    )
    taps = both[: SHORT * 3].reshape(SHORT, 3, 2 * LANES)
    medium = both[SHORT * 3 :].astype(jnp.float32)

    way = jnp.arange(2, dtype=jnp.int32).reshape(2, 1, 1, 1)
    ahead = jnp.arange(4, dtype=jnp.int32).reshape(1, 4, 1, 1)
    group = jnp.arange(2, dtype=jnp.int32).reshape(1, 1, 2, 1)
    index = jnp.arange(2, dtype=jnp.int32).reshape(1, 1, 1, 2)
    to_x, to_y = (x + way * ahead) % 4, (y + (1 - way) * ahead) % 4
    slots = (to_x * 4 + (to_y // 2) * 2 + (core + group) % 2) * 4 + (to_y % 2) * 2 + index
    slots = slots.reshape(32)
    all_slots = jnp.arange(block_at_slot.shape[0], dtype=jnp.int32)
    ids = jnp.sum(jnp.where(all_slots == slots[:, None], block_at_slot, 0), axis=1)
    previous = jnp.maximum(ids - 1, 0)
    before = jnp.sum(jnp.where(block_at_slot == previous[:, None], all_slots, 0), axis=1)
    before = before.reshape(2, 4, 4)
    from_x, from_y = before // 16, ((before // 8) % 2) * 2 + (before // 2) % 2
    local = ((before // 4 + core) % 2) * 2 + before % 2
    dx, dy = (from_x - x) % 4, (from_y - y) % 4
    table = jnp.stack(
        [jnp.where(dy[0] == 0, dx[0] * 4, 0) + local[0],
         jnp.where(dx[1] == 0, dy[1] * 4, 0) + local[1]]
    ).astype(jnp.int32)
    picks = jnp.stack([dy[0, 0], dx[1, 0]]).astype(jnp.int32)
    starts = (ids[:4] * BLK).astype(jnp.int32)
    ends = jnp.cumsum(genome_lengths).astype(jnp.int32)

    product, low, high = products(starts, ends, proj, taps)
    rows_x, rows_y = axis_of(low, along_x), axis_of(high, along_y)
    partials = [inner(i, starts, ends, product, medium) for i in range(2)]
    table, partials[0] = lax.optimization_barrier((table, partials[0]))
    routed = route(table, rows_x + rows_y)
    halos = [routed[0]] + [send(routed[4 - d], along_y(4 - d)) for d in range(1, 4)]
    halos += [routed[4]] + [send(routed[8 - d], along_x(4 - d)) for d in range(1, 4)]

    rows = tokens.reshape(2, HALF, PIECE)
    residual = send(jnp.where(y_low == 0, rows[1], rows[0]), swap_y)
    mine = jnp.where(y_low == 0, rows[0], rows[1])
    gated = edges(starts, ends, picks, proj, partials, taps, medium, halos)
    columns = lax.optimization_barrier((columns, gated))[0]
    gathered = gather_line(gated.reshape(2, HALF, 2 * LANES))
    columns = jnp.stack(axis_of(columns, along_y))
    columns = assemble(place, columns, send(columns, swap_core))
    theirs = output(1, place, residual, columns, gathered)
    place, theirs = lax.optimization_barrier((place, theirs))
    theirs = send(theirs, swap_y)
    ours = output(0, place, mine, columns, gathered)
    first = jnp.where(y_low == 0, ours, theirs)
    second = jnp.where(y_low == 0, theirs, ours)
    return jnp.concatenate([first, second], axis=0)


def solution(mesh):
    in_specs = (
        P("seq", "fsdp"),
        P(),
        P(None, "seq", "fsdp"),
        P(None, None, "fsdp"),
        P(None, "fsdp"),
        P(None, ("fsdp", "seq")),
        P(),
        P(),
    )
    out_specs = P("seq", "fsdp")
    return jax.shard_map(block, mesh=mesh, in_specs=in_specs, out_specs=out_specs, check_vma=False)
```

```python
import functools

import jax
import jax.numpy as jnp
from jax import lax
from jax.experimental import pallas as pl
from jax.experimental.pallas import tpu as pltpu
from jax.sharding import PartitionSpec as P


BLK = 256
SHORT = 7
MED = 128
LANES = 128
TAIL = 8
HALF = 512
PIECE = 256
D = 4096
HALO = MED + 3 * TAIL
AXES = ("seq", "fsdp")
epsilon = 1e-06


def linear(x, y, z, core):
    return (x * 4 + (y // 2) * 2 + core) * 16 + (y % 2) * 8 + z


def permutation(move):
    pairs = []
    for x in range(4):
        for y in range(4):
            for z in range(8):
                for core in range(2):
                    pairs.append((linear(x, y, z, core), linear(*move(x, y, z, core))))
    return pairs


def send(value, move):
    return lax.ppermute(value, AXES, permutation(move))


def along_x(step):
    return lambda x, y, z, core: ((x + step) % 4, y, z, core)


def along_y(step):
    return lambda x, y, z, core: (x, (y + step) % 4, z, core)


def swap_y(x, y, z, core):
    return (x, y ^ 1, z, core)


def swap_core(x, y, z, core):
    return (x, y, z, core ^ 1)


def gather_line(value):
    groups = [
        [linear(x, y, z, core) for z in range(8) for core in range(2)]
        for x in range(4)
        for y in range(4)
    ]
    return lax.all_gather(value, AXES, axis=0, axis_index_groups=groups)


def axis_of(chunk, along):
    return [chunk] + [send(chunk, along(-d)) for d in range(1, 4)]


def anywhere():
    return pl.BlockSpec(memory_space=pl.ANY)


def full():
    return pl.BlockSpec(memory_space=pltpu.VMEM)


def scalars():
    return pl.BlockSpec(memory_space=pltpu.SMEM)


def project_kernel(place_ref, line_ref, *refs):
    weights = refs[:8]
    out_ref, x_scratch, s_scratch, w_scratch, total, x_sems, s_sems, w_sems = refs[8:]
    x, y, core, y_low = place_ref[0], place_ref[1], place_ref[2], place_ref[3]

    def copies(i):
        made = []
        z, group = i // 2, lax.rem(i, 2)
        source = z * 2 + lax.rem(core + group, 2)
        rows = pl.ds(pl.multiple_of(group * HALF, HALF), HALF)
        for p in range(2):
            lanes = pl.ds(pl.multiple_of((z * 2 + p) * PIECE, PIECE), PIECE)
            made.append(
                pltpu.make_async_copy(
                    line_ref.at[source, p, pl.ds(0, HALF)], x_scratch.at[rows, lanes], x_sems.at[p, i]
                )
            )
            made.append(
                pltpu.make_async_copy(
                    line_ref.at[source, p, pl.ds(HALF, TAIL)], s_scratch.at[group, z * 2 + p],
                    s_sems.at[p, i],
                )
            )
        return made

    def start(i, carry):
        for copy in copies(i):
            copy.start()
        return carry

    def finish(i, carry):
        for copy in copies(i):
            copy.wait()
        return carry

    started = []
    for other in range(2):
        for a in range(4):
            for b in range(4):
                dx, dy = (b, a) if other == 0 else (a, b)
                to_x, to_y = lax.rem(x + dx, 4), lax.rem(y + dy, 4)
                owner = to_x * 4 + (to_y // 2) * 2 + lax.rem(core + other, 2)
                turn = lax.rem(owner, 8) * 2 + lax.rem(owner // 8 + y_low, 2)
                rows = pl.ds(pl.multiple_of(turn * PIECE, PIECE), PIECE)
                lanes = pl.ds(pl.multiple_of(lax.rem(to_y, 2) * LANES, LANES), LANES)
                started.append(
                    pltpu.make_async_copy(
                        weights[other * 4 + a].at[b],
                        w_scratch.at[:, rows, lanes],
                        w_sems.at[other, a, b],
                    )
                )
    for copy in started:
        copy.start()
    lax.fori_loop(0, 16, start, 0)
    for copy in started:
        copy.wait()

    def quarter(part, carry):
        lax.fori_loop(part * 4, part * 4 + 4, finish, 0)
        depth = pl.ds(pl.multiple_of(part * 1024, 1024), 1024)

        def step(i, carry):
            branch, group = i // 2, lax.rem(i, 2)
            rows = pl.ds(pl.multiple_of(group * HALF, HALF), HALF)
            product = jnp.dot(
                x_scratch[rows, depth], w_scratch[branch, depth, :],
                preferred_element_type=jnp.float32,
            )

            @pl.when(part == 0)
            def _():
                total[branch, rows, :] = product

            @pl.when(part > 0)
            def _():
                total[branch, rows, :] += product

            return carry

        return lax.fori_loop(0, 6, step, carry)

    lax.fori_loop(0, 4, quarter, 0)
    for group in range(2):
        square = jnp.sum(s_scratch[group].astype(jnp.float32), axis=0)
        for i in range(2):
            row = square[i : i + 1] + square[i + 2 : i + 3] + square[i + 4 : i + 5]
            scale = lax.rsqrt(row / D + epsilon)
            scale = jnp.transpose(jnp.broadcast_to(scale, (LANES, PIECE)))
            scale = jnp.concatenate([scale, scale], axis=1)
            block = group * 2 + i

            def write(branch, carry, block=block, scale=scale):
                value = total[branch, block * BLK : (block + 1) * BLK, :]
                out_ref[branch, block] = (value * scale).astype(jnp.bfloat16)
                return carry

            lax.fori_loop(0, 3, write, 0)


def project(place, line, weights):
    return pl.pallas_call(
        project_kernel,
        out_shape=jax.ShapeDtypeStruct((3, 4, BLK, 2 * LANES), jnp.bfloat16),
        in_specs=[scalars()] + [anywhere()] * 9,
        out_specs=full(),
        scratch_shapes=[
            pltpu.VMEM((2 * HALF, D), jnp.bfloat16),
            pltpu.VMEM((2, 16, TAIL, PIECE), jnp.bfloat16),
            pltpu.VMEM((3, D, 2 * LANES), jnp.bfloat16),
            pltpu.VMEM((3, 2 * HALF, 2 * LANES), jnp.float32),
            pltpu.SemaphoreType.DMA((2, 16)),
            pltpu.SemaphoreType.DMA((2, 16)),
            pltpu.SemaphoreType.DMA((2, 4, 4)),
        ],
        cost_estimate=pl.CostEstimate(
            flops=2 * 1024 * D * 768, bytes_accessed=16 << 20, transcendentals=0
        ),
        name="project",
    )(place, line, *weights)


def reach_of(start, rows, ends_ref):
    position = start + lax.broadcasted_iota(jnp.int32, (rows, LANES), 0)
    first = jnp.zeros((rows, LANES), jnp.int32)
    for g in range(3):
        end = ends_ref[g]
        first = jnp.maximum(first, jnp.where(position >= end, end, 0))
    return position - first


def split_by_genome(start, ends_ref):
    cut = False
    for g in range(3):
        cut = cut | ((ends_ref[g] > start) & (ends_ref[g] < start + BLK))
    return cut


def short_mix(window_ref, reach, taps_ref, branch, rows, lanes):
    total = jnp.zeros((rows, LANES), jnp.float32)
    for j in range(SHORT):
        part = window_ref[TAIL - j : TAIL - j + rows, :]
        if reach is not None:
            part = jnp.where(reach >= j, part, 0.0)
        total = total + part * taps_ref[j, branch : branch + 1, lanes].astype(jnp.float32)
    return total


def product_kernel(start_ref, ends_ref, proj_ref, taps_ref, out_ref, low_ref, high_ref, k, v):
    start = start_ref[pl.program_id(0)]
    cut = split_by_genome(start, ends_ref)
    for part, tail_ref in enumerate((low_ref, high_ref)):
        lanes = pl.ds(part * LANES, LANES)
        k[:TAIL, :] = jnp.zeros((TAIL, LANES), jnp.float32)
        v[:TAIL, :] = jnp.zeros((TAIL, LANES), jnp.float32)
        k[TAIL:, :] = proj_ref[1, 0, :, lanes].astype(jnp.float32)
        v[TAIL:, :] = proj_ref[2, 0, :, lanes].astype(jnp.float32)

        def store(reach):
            mixed = short_mix(k, reach, taps_ref, 1, BLK, lanes)
            product = mixed * short_mix(v, reach, taps_ref, 2, BLK, lanes)
            first = lax.broadcasted_iota(jnp.int32, (BLK, LANES), 0) >= SHORT - 1
            out_ref[0, :, lanes] = jnp.where(first, product, 0.0).astype(jnp.bfloat16)

        @pl.when(cut)
        def _():
            store(reach_of(start, BLK, ends_ref))

        @pl.when(jnp.logical_not(cut))
        def _():
            store(None)

        tail_ref[0, :MED, :] = out_ref[0, BLK - MED :, lanes]
        for branch in range(3):
            at = MED + branch * TAIL
            tail_ref[0, at : at + TAIL, :] = proj_ref[branch, 0, BLK - TAIL :, lanes]


def products(starts, ends, proj, taps):
    tail = jax.ShapeDtypeStruct((4, HALO, LANES), jnp.bfloat16)
    tail_spec = pl.BlockSpec((1, HALO, LANES), lambda i, *_: (i, 0, 0))
    return pl.pallas_call(
        product_kernel,
        grid_spec=pltpu.PrefetchScalarGridSpec(
            num_scalar_prefetch=2,
            grid=(4,),
            in_specs=[
                pl.BlockSpec((3, 1, BLK, 2 * LANES), lambda i, *_: (0, i, 0, 0)),
                pl.BlockSpec((SHORT, 3, 2 * LANES), lambda i, *_: (0, 0, 0)),
            ],
            out_specs=(
                pl.BlockSpec((1, BLK, 2 * LANES), lambda i, *_: (i, 0, 0)), tail_spec, tail_spec,
            ),
            scratch_shapes=[pltpu.VMEM((BLK + TAIL, LANES), jnp.float32)] * 2,
        ),
        out_shape=(jax.ShapeDtypeStruct((4, BLK, 2 * LANES), jnp.bfloat16), tail, tail),
        cost_estimate=pl.CostEstimate(
            flops=60 << 20, bytes_accessed=4 << 20, transcendentals=0
        ),
        name="products",
    )(starts, ends, proj, taps)


def add_turn(total, shifted, weights, turn, at, first, last):
    part = total[first:last]
    for s in range(TAIL):
        tap = turn * TAIL + s
        part = part + shifted[s, at : at + last - first, :] * weights[tap : tap + 1, :]
    pieces = [total[:first]] * (first > 0) + [part] + [total[last:]] * (last < total.shape[0])
    return jnp.concatenate(pieces, axis=0) if len(pieces) > 1 else part


def each_genome(ends_ref, start, rows, body):
    def genome(g, carry):
        low = jnp.where(g == 0, 0, ends_ref[jnp.maximum(g - 1, 0)])
        high = ends_ref[g]

        @pl.when((low < start + rows) & (high > start))
        def _():
            body(low, high)

        return carry

    lax.fori_loop(0, 4, genome, 0)


def lanes_of(part):
    return pl.ds(pl.multiple_of(part * LANES, LANES), LANES)


def inner_kernel(index, start_ref, ends_ref, product_ref, medium_ref, out_ref, shifted):
    start = start_ref[index * 2 + pl.program_id(0)]
    row = start + lax.broadcasted_iota(jnp.int32, (BLK, LANES), 0)

    def segment(part, carry):
        lanes = lanes_of(part)

        def run(low, high):
            value = jnp.where(row >= low, product_ref[0, :, lanes].astype(jnp.float32), 0.0)
            for s in range(TAIL):
                shifted[s, :TAIL, :] = jnp.zeros((TAIL, LANES), jnp.float32)
                shifted[s, s:BLK, :] = value[: BLK - s, :]
            weights = medium_ref.at[:, lanes]
            for begin in (0, MED):
                total = jnp.zeros((MED, LANES), jnp.float32)
                for turn in range(MED // TAIL):
                    first = max(0, turn * TAIL - begin)
                    at = begin + first - turn * TAIL
                    total = add_turn(total, shifted, weights, turn, at, first, MED)
                rows = pl.ds(begin, MED)
                here = row[begin : begin + MED]
                inside = (here >= low) & (here < high)
                out_ref[0, rows, lanes] = jnp.where(inside, total, out_ref[0, rows, lanes])

        each_genome(ends_ref, start, BLK, run)
        return carry

    lax.fori_loop(0, 2, segment, 0)


def inner(index, starts, ends, product, medium):
    return pl.pallas_call(
        functools.partial(inner_kernel, index),
        grid_spec=pltpu.PrefetchScalarGridSpec(
            num_scalar_prefetch=2,
            grid=(2,),
            in_specs=[
                pl.BlockSpec((1, BLK, 2 * LANES), lambda i, *_: (index * 2 + i, 0, 0)),
                pl.BlockSpec((MED, 2 * LANES), lambda i, *_: (0, 0)),
            ],
            out_specs=pl.BlockSpec((1, BLK, 2 * LANES), lambda i, *_: (i, 0, 0)),
            scratch_shapes=[pltpu.VMEM((TAIL, BLK, LANES), jnp.float32)],
        ),
        out_shape=jax.ShapeDtypeStruct((2, BLK, 2 * LANES), jnp.float32),
        cost_estimate=pl.CostEstimate(
            flops=1024 * 256 * 128, bytes_accessed=1 << 20, transcendentals=0
        ),
        name="inner",
    )(starts, ends, product, medium)


def route_kernel(table_ref, *refs):
    ins, outs, every = refs[:8], refs[8:16], refs[16]
    for way in range(2):
        for d in range(4):
            every[d * 4 : (d + 1) * 4] = ins[way * 4 + d][...]
        for d in range(4):
            for j in range(4):
                outs[way * 4 + d][j] = every[table_ref[way, d, j]]


def route(table, ins):
    return pl.pallas_call(
        route_kernel,
        out_shape=(jax.ShapeDtypeStruct((4, HALO, LANES), jnp.bfloat16),) * 8,
        in_specs=[scalars()] + [full()] * 8,
        out_specs=(full(),) * 8,
        scratch_shapes=[pltpu.VMEM((16, HALO, LANES), jnp.bfloat16)],
        cost_estimate=pl.CostEstimate(flops=1 << 10, bytes_accessed=4 << 20, transcendentals=0),
        name="route",
    )(table, *ins)


def edge_kernel(
    start_ref, ends_ref, pick_ref, proj_ref, early_ref, late_ref, taps_ref, medium_ref, *refs
):
    halos, (out_ref, halo, window, small, prior, shifted, filtered) = refs[:8], refs[8:]
    block = pl.program_id(0)
    start = start_ref[block]
    cut = split_by_genome(start, ends_ref)
    near = MED + TAIL
    reach8 = reach_of(start, TAIL, ends_ref)
    row = start - MED + lax.broadcasted_iota(jnp.int32, (near, LANES), 0)
    out_row = start + lax.broadcasted_iota(jnp.int32, (near, LANES), 0)
    for part in range(2):
        for m in range(4):

            @pl.when(pick_ref[part, block] == m)
            def _(part=part, m=m):
                halo[part] = halos[part * 4 + m][0].astype(jnp.float32)

    @pl.when(block < 2)
    def _():
        filtered[...] = early_ref[0]

    @pl.when(block >= 2)
    def _():
        filtered[...] = late_ref[0]

    def segment(part, carry):
        lanes = lanes_of(part)
        taps = taps_ref.at[:, :, lanes]
        mixes = []
        for branch in (1, 2):
            at = MED + branch * TAIL
            small[:TAIL, :] = halo[part, at : at + TAIL, :]
            small[TAIL:, :] = proj_ref[branch, 0, : 2 * TAIL, lanes][:TAIL].astype(jnp.float32)
            mixes.append(short_mix(small, reach8, taps, branch, TAIL, slice(None)))
        first = lax.broadcasted_iota(jnp.int32, (TAIL, LANES), 0) < SHORT - 1
        early = (mixes[0] * mixes[1]).astype(jnp.bfloat16).astype(jnp.float32)
        prior[:MED, :] = halo[part, :MED, :]
        prior[MED:, :] = jnp.where(first, early, 0.0)

        def run(low, high):
            value = jnp.where(row >= low, prior[...], 0.0)
            for s in range(TAIL):
                shifted[s, near : near + TAIL, :] = jnp.zeros((TAIL, LANES), jnp.float32)
                shifted[s, s : s + near, :] = value
            weights = medium_ref.at[:, lanes]
            total = jnp.zeros((near, LANES), jnp.float32)
            for turn in range(MED // TAIL):
                last = min((turn + 2) * TAIL, near)
                at = MED - turn * TAIL
                total = add_turn(total, shifted, weights, turn, at, 0, last)
            inside = (out_row >= low) & (out_row < high)
            filtered[:near, lanes] += jnp.where(inside, total, 0.0)

        each_genome(ends_ref, start, near, run)
        window[:TAIL, :] = halo[part, MED : MED + TAIL, :]
        window[TAIL:, :] = proj_ref[0, 0, :, lanes].astype(jnp.float32)

        @pl.when(cut)
        def _():
            mixed = short_mix(window, reach_of(start, BLK, ends_ref), taps, 0, BLK, slice(None))
            out_ref[0, :, lanes] = (mixed * filtered[:, lanes]).astype(jnp.bfloat16)

        @pl.when(jnp.logical_not(cut))
        def _():
            head = short_mix(window, reach8, taps, 0, TAIL, slice(None))
            mixed = short_mix(window, None, taps, 0, BLK, slice(None))
            mixed = jnp.concatenate([head, mixed[TAIL:]], axis=0)
            out_ref[0, :, lanes] = (mixed * filtered[:, lanes]).astype(jnp.bfloat16)

        return carry

    lax.fori_loop(0, 2, segment, 0)


def edges(starts, ends, picks, proj, partials, taps, medium, halos):
    return pl.pallas_call(
        edge_kernel,
        grid_spec=pltpu.PrefetchScalarGridSpec(
            num_scalar_prefetch=3,
            grid=(4,),
            in_specs=[
                pl.BlockSpec((3, 1, BLK, 2 * LANES), lambda i, *_: (0, i, 0, 0)),
                pl.BlockSpec((1, BLK, 2 * LANES), lambda i, *_: (jnp.minimum(i, 1), 0, 0)),
                pl.BlockSpec((1, BLK, 2 * LANES), lambda i, *_: (jnp.maximum(i - 2, 0), 0, 0)),
                pl.BlockSpec((SHORT, 3, 2 * LANES), lambda i, *_: (0, 0, 0)),
                pl.BlockSpec((MED, 2 * LANES), lambda i, *_: (0, 0)),
            ]
            + [pl.BlockSpec((1, HALO, LANES), lambda i, *_: (i, 0, 0))] * 8,
            out_specs=pl.BlockSpec((1, BLK, 2 * LANES), lambda i, *_: (i, 0, 0)),
            scratch_shapes=[
                pltpu.VMEM((2, HALO, LANES), jnp.float32),
                pltpu.VMEM((BLK + TAIL, LANES), jnp.float32),
                pltpu.VMEM((2 * TAIL, LANES), jnp.float32),
                pltpu.VMEM((MED + TAIL, LANES), jnp.float32),
                pltpu.VMEM((TAIL, MED + 2 * TAIL, LANES), jnp.float32),
                pltpu.VMEM((BLK, 2 * LANES), jnp.float32),
            ],
        ),
        out_shape=jax.ShapeDtypeStruct((4, BLK, 2 * LANES), jnp.bfloat16),
        cost_estimate=pl.CostEstimate(
            flops=1024 * 256 * 64, bytes_accessed=3 << 20, transcendentals=0
        ),
        name="edges",
    )(starts, ends, picks, proj, *partials, taps, medium, *halos)


def assemble_kernel(place_ref, own_ref, other_ref, out_ref, sems):
    x, y, core = place_ref[0], place_ref[1], place_ref[2]
    started = []
    for other, ref in enumerate((own_ref, other_ref)):
        for dy in range(4):
            for dx in range(4):
                to_x, to_y = lax.rem(x + dx, 4), lax.rem(y + dy, 4)
                owner = to_x * 4 + (to_y // 2) * 2 + lax.rem(core + other, 2)
                rows = pl.ds(pl.multiple_of(owner * 16, 16), 16)
                started.append(
                    pltpu.make_async_copy(
                        ref.at[dy, dx], out_ref.at[lax.rem(to_y, 2), rows], sems.at[other, dy, dx]
                    )
                )
    for copy in started:
        copy.start()
    for copy in started:
        copy.wait()


def assemble(place, own, other):
    return pl.pallas_call(
        assemble_kernel,
        out_shape=jax.ShapeDtypeStruct((2, PIECE, D), jnp.bfloat16),
        in_specs=[scalars()] + [anywhere()] * 2,
        out_specs=full(),
        scratch_shapes=[pltpu.SemaphoreType.DMA((2, 4, 4))],
        cost_estimate=pl.CostEstimate(flops=1 << 10, bytes_accessed=8 << 20, transcendentals=0),
        name="assemble",
    )(place, own, other)


def output_kernel(
    side, place_ref, residual_ref, w_ref, gated_ref, out_ref, scratch, weights, total, sems, w_sems
):
    core, y_low = place_ref[2], place_ref[3]
    column = lax.rem(y_low + side, 2)

    def copies(i):
        lanes = pl.ds(pl.multiple_of(i * 1024, 1024), 1024)
        made = [pltpu.make_async_copy(w_ref.at[column, :, lanes], weights.at[:, lanes], w_sems.at[i])]
        for k in range(4):
            lanes = pl.ds(pl.multiple_of((i * 4 + k) * PIECE, PIECE), PIECE)
            source = gated_ref.at[i * 4 + k, lax.rem(core + k, 2)]
            made.append(pltpu.make_async_copy(source, scratch.at[:, lanes], sems.at[i, k]))
        return made

    def start(i, carry):
        for copy in copies(i):
            copy.start()
        return carry

    lax.fori_loop(0, 4, start, 0)
    total[...] = residual_ref[...].astype(jnp.float32)

    def step(i, carry):
        for copy in copies(i):
            copy.wait()
        lanes = pl.ds(pl.multiple_of(i * 1024, 1024), 1024)
        total[...] += lax.dot_general(
            scratch[:, lanes], weights[:, lanes], (((1,), (1,)), ((), ())),
            preferred_element_type=jnp.float32,
        )
        return carry

    lax.fori_loop(0, 4, step, 0)
    out_ref[...] = total[...].astype(jnp.bfloat16)


def output(side, place, residual, weights, gated):
    return pl.pallas_call(
        functools.partial(output_kernel, side),
        out_shape=jax.ShapeDtypeStruct((HALF, PIECE), jnp.bfloat16),
        in_specs=[scalars(), full()] + [anywhere()] * 2,
        out_specs=full(),
        scratch_shapes=[
            pltpu.VMEM((HALF, D), jnp.bfloat16),
            pltpu.VMEM((PIECE, D), jnp.bfloat16),
            pltpu.VMEM((HALF, PIECE), jnp.float32),
            pltpu.SemaphoreType.DMA((4, 4)),
            pltpu.SemaphoreType.DMA((4,)),
        ],
        cost_estimate=pl.CostEstimate(
            flops=2 * HALF * D * PIECE, bytes_accessed=6 << 20, transcendentals=0
        ),
        name="output",
    )(place, residual, weights, gated)


def block(
    tokens,
    norm_gain,
    in_weight,
    short_filter,
    medium_filter,
    out_weight,
    genome_lengths,
    block_at_slot,
):
    seq, fsdp = lax.axis_index("seq"), lax.axis_index("fsdp")
    x, core, y_low, z = seq // 4, seq % 2, fsdp // 8, fsdp % 8
    y = ((seq // 2) % 2) * 2 + y_low

    values = tokens.astype(jnp.float32)
    gain = lax.dynamic_index_in_dim(norm_gain.reshape(16, 1, PIECE), fsdp, 0, keepdims=False)
    scaled = (values * gain.astype(jnp.float32)).astype(jnp.bfloat16)
    square = jnp.sum(values * values, axis=1)
    parts = []
    for _ in range(3):
        part = lax.reduce_precision(square, exponent_bits=8, mantissa_bits=7)
        parts.append(part.astype(jnp.bfloat16).reshape(2, 2, PIECE))
        square = square - part
    parts.append(jnp.zeros((2, 2, PIECE), jnp.bfloat16))
    packed = jnp.concatenate([scaled.reshape(2, HALF, PIECE)] + parts, axis=1)
    mine = jnp.where(y_low == 0, packed[0], packed[1])
    theirs = send(jnp.where(y_low == 0, packed[1], packed[0]), swap_y)
    pair = jnp.stack([mine, theirs])
    line = gather_line(pair)

    halves = in_weight.reshape(3, PIECE, 2, LANES)
    keep = jnp.where(core == 0, halves[:, :, 0], halves[:, :, 1])
    give = jnp.where(core == 0, halves[:, :, 1], halves[:, :, 0])
    other = send(give, swap_core)
    first = axis_of(keep, along_x)
    first, other = jnp.stack(first), jnp.stack(axis_of(other, along_y))
    weights = axis_of(first, along_y) + axis_of(other, along_x)

    place = jnp.stack([x, y, core, y_low, z]).astype(jnp.int32)

    columns = out_weight.reshape(2, 8, 2, LANES, 16).transpose(4, 1, 2, 0, 3).reshape(16, D)
    columns = axis_of(columns, along_x)
    columns = jnp.stack(columns)
    proj = project(place, line, weights)

    both = jnp.concatenate([short_filter.reshape(SHORT * 3, PIECE), medium_filter], axis=0)
    both = jnp.where(core == 0, both[:, :LANES], both[:, LANES:])
    theirs = send(both, swap_y)
    both = jnp.concatenate(
        [jnp.where(y_low == 0, both, theirs), jnp.where(y_low == 0, theirs, both)], axis=1
    )
    taps = both[: SHORT * 3].reshape(SHORT, 3, 2 * LANES)
    medium = both[SHORT * 3 :].astype(jnp.float32)

    way = jnp.arange(2, dtype=jnp.int32).reshape(2, 1, 1, 1)
    ahead = jnp.arange(4, dtype=jnp.int32).reshape(1, 4, 1, 1)
    group = jnp.arange(2, dtype=jnp.int32).reshape(1, 1, 2, 1)
    index = jnp.arange(2, dtype=jnp.int32).reshape(1, 1, 1, 2)
    to_x, to_y = (x + way * ahead) % 4, (y + (1 - way) * ahead) % 4
    slots = (to_x * 4 + (to_y // 2) * 2 + (core + group) % 2) * 4 + (to_y % 2) * 2 + index
    slots = slots.reshape(32)
    all_slots = jnp.arange(block_at_slot.shape[0], dtype=jnp.int32)
    ids = jnp.sum(jnp.where(all_slots == slots[:, None], block_at_slot, 0), axis=1)
    previous = jnp.maximum(ids - 1, 0)
    before = jnp.sum(jnp.where(block_at_slot == previous[:, None], all_slots, 0), axis=1)
    before = before.reshape(2, 4, 4)
    from_x, from_y = before // 16, ((before // 8) % 2) * 2 + (before // 2) % 2
    local = ((before // 4 + core) % 2) * 2 + before % 2
    dx, dy = (from_x - x) % 4, (from_y - y) % 4
    table = jnp.stack(
        [jnp.where(dy[0] == 0, dx[0] * 4, 0) + local[0],
         jnp.where(dx[1] == 0, dy[1] * 4, 0) + local[1]]
    ).astype(jnp.int32)
    picks = jnp.stack([dy[0, 0], dx[1, 0]]).astype(jnp.int32)
    starts = (ids[:4] * BLK).astype(jnp.int32)
    ends = jnp.cumsum(genome_lengths).astype(jnp.int32)

    starts, columns = lax.optimization_barrier((starts, columns))
    product, low, high = products(starts, ends, proj, taps)
    rows_x, rows_y = axis_of(low, along_x), axis_of(high, along_y)
    partials = [inner(i, starts, ends, product, medium) for i in range(2)]
    table, partials[0] = lax.optimization_barrier((table, partials[0]))
    routed = route(table, rows_x + rows_y)
    halos = [routed[0]] + [send(routed[4 - d], along_y(4 - d)) for d in range(1, 4)]
    halos += [routed[4]] + [send(routed[8 - d], along_x(4 - d)) for d in range(1, 4)]

    rows = tokens.reshape(2, HALF, PIECE)
    residual = send(jnp.where(y_low == 0, rows[1], rows[0]), swap_y)
    mine = jnp.where(y_low == 0, rows[0], rows[1])
    gated = edges(starts, ends, picks, proj, partials, taps, medium, halos)
    columns = lax.optimization_barrier((columns, gated))[0]
    gathered = gather_line(gated.reshape(2, HALF, 2 * LANES))
    columns = jnp.stack(axis_of(columns, along_y))
    columns = assemble(place, columns, send(columns, swap_core))
    theirs = output(1, place, residual, columns, gathered)
    place, theirs = lax.optimization_barrier((place, theirs))
    theirs = send(theirs, swap_y)
    ours = output(0, place, mine, columns, gathered)
    first = jnp.where(y_low == 0, ours, theirs)
    second = jnp.where(y_low == 0, theirs, ours)
    return jnp.concatenate([first, second], axis=0)


def solution(mesh):
    in_specs = (
        P("seq", "fsdp"),
        P(),
        P(None, "seq", "fsdp"),
        P(None, None, "fsdp"),
        P(None, "fsdp"),
        P(None, ("fsdp", "seq")),
        P(),
        P(),
    )
    out_specs = P("seq", "fsdp")
    return jax.shard_map(block, mesh=mesh, in_specs=in_specs, out_specs=out_specs, check_vma=False)
```

```python
import functools

import jax
import jax.numpy as jnp
from jax import lax
from jax.experimental import pallas as pl
from jax.experimental.pallas import tpu as pltpu
from jax.sharding import PartitionSpec as P


BLK = 256
SHORT = 7
MED = 128
LANES = 128
TAIL = 8
HALF = 512
PIECE = 256
D = 4096
HALO = MED + 3 * TAIL
AXES = ("seq", "fsdp")
epsilon = 1e-06


def linear(x, y, z, core):
    return (x * 4 + (y // 2) * 2 + core) * 16 + (y % 2) * 8 + z


def permutation(move):
    pairs = []
    for x in range(4):
        for y in range(4):
            for z in range(8):
                for core in range(2):
                    pairs.append((linear(x, y, z, core), linear(*move(x, y, z, core))))
    return pairs


def send(value, move):
    return lax.ppermute(value, AXES, permutation(move))


def along_x(step):
    return lambda x, y, z, core: ((x + step) % 4, y, z, core)


def along_y(step):
    return lambda x, y, z, core: (x, (y + step) % 4, z, core)


def swap_y(x, y, z, core):
    return (x, y ^ 1, z, core)


def swap_core(x, y, z, core):
    return (x, y, z, core ^ 1)


def gather_line(value):
    groups = [
        [linear(x, y, z, core) for z in range(8) for core in range(2)]
        for x in range(4)
        for y in range(4)
    ]
    return lax.all_gather(value, AXES, axis=0, axis_index_groups=groups)


def axis_of(chunk, along):
    return [chunk] + [send(chunk, along(-d)) for d in range(1, 4)]


def anywhere():
    return pl.BlockSpec(memory_space=pl.ANY)


def full():
    return pl.BlockSpec(memory_space=pltpu.VMEM)


def scalars():
    return pl.BlockSpec(memory_space=pltpu.SMEM)


def project_kernel(place_ref, line_ref, *refs):
    weights = refs[:8]
    out_ref, x_scratch, s_scratch, w_scratch, total, x_sems, s_sems, w_sems = refs[8:]
    x, y, core, y_low = place_ref[0], place_ref[1], place_ref[2], place_ref[3]

    def row_copies(i):
        made = []
        group, z = i // 8, lax.rem(i, 8)
        source = z * 2 + lax.rem(core + group, 2)
        rows = pl.ds(pl.multiple_of(group * HALF, HALF), HALF)
        for p in range(2):
            lanes = pl.ds(pl.multiple_of((z * 2 + p) * PIECE, PIECE), PIECE)
            made.append(
                pltpu.make_async_copy(
                    line_ref.at[source, p, pl.ds(0, HALF)], x_scratch.at[rows, lanes],
                    x_sems.at[p, i],
                )
            )
            made.append(
                pltpu.make_async_copy(
                    line_ref.at[source, p, pl.ds(HALF, TAIL)], s_scratch.at[group, z * 2 + p],
                    s_sems.at[p, i],
                )
            )
        return made

    def weight_copies(i):
        made = []
        branch, b = i // 4, lax.rem(i, 4)
        for other in range(2):
            for a in range(4):
                dx, dy = (b, a) if other == 0 else (a, b)
                to_x, to_y = lax.rem(x + dx, 4), lax.rem(y + dy, 4)
                owner = to_x * 4 + (to_y // 2) * 2 + lax.rem(core + other, 2)
                turn = lax.rem(owner, 8) * 2 + lax.rem(owner // 8 + y_low, 2)
                rows = pl.ds(pl.multiple_of(turn * PIECE, PIECE), PIECE)
                lanes = pl.ds(pl.multiple_of(lax.rem(to_y, 2) * LANES, LANES), LANES)
                made.append(
                    pltpu.make_async_copy(
                        weights[other * 4 + a].at[b, branch],
                        w_scratch.at[branch, rows, lanes],
                        w_sems.at[other * 4 + a, i],
                    )
                )
        return made

    def start(copies, first, last):
        def one(i, carry):
            for copy in copies(i):
                copy.start()
            return carry

        lax.fori_loop(first, last, one, 0)

    def finish(copies, first, last):
        def one(i, carry):
            for copy in copies(i):
                copy.wait()
            return carry

        lax.fori_loop(first, last, one, 0)

    start(row_copies, 0, 8)
    start(weight_copies, 0, 4)
    start(row_copies, 8, 16)
    start(weight_copies, 4, 12)

    def step(i, carry):
        branch, group = i // 2, lax.rem(i, 2)

        @pl.when(i < 2)
        def _():
            finish(row_copies, i * 8, i * 8 + 8)

        @pl.when(group == 0)
        def _():
            finish(weight_copies, branch * 4, branch * 4 + 4)

        rows = pl.ds(pl.multiple_of(group * HALF, HALF), HALF)
        total[branch, rows, :] = jnp.dot(
            x_scratch[rows, :], w_scratch[branch], preferred_element_type=jnp.float32
        )
        return carry

    lax.fori_loop(0, 6, step, 0)
    for group in range(2):
        square = jnp.sum(s_scratch[group].astype(jnp.float32), axis=0)
        for i in range(2):
            row = square[i : i + 1] + square[i + 2 : i + 3] + square[i + 4 : i + 5]
            scale = lax.rsqrt(row / D + epsilon)
            scale = jnp.transpose(jnp.broadcast_to(scale, (LANES, PIECE)))
            scale = jnp.concatenate([scale, scale], axis=1)
            block = group * 2 + i

            def write(branch, carry, block=block, scale=scale):
                value = total[branch, block * BLK : (block + 1) * BLK, :]
                out_ref[branch, block] = (value * scale).astype(jnp.bfloat16)
                return carry

            lax.fori_loop(0, 3, write, 0)


def project(place, line, weights):
    return pl.pallas_call(
        project_kernel,
        out_shape=jax.ShapeDtypeStruct((3, 4, BLK, 2 * LANES), jnp.bfloat16),
        in_specs=[scalars()] + [anywhere()] * 9,
        out_specs=full(),
        scratch_shapes=[
            pltpu.VMEM((2 * HALF, D), jnp.bfloat16),
            pltpu.VMEM((2, 16, TAIL, PIECE), jnp.bfloat16),
            pltpu.VMEM((3, D, 2 * LANES), jnp.bfloat16),
            pltpu.VMEM((3, 2 * HALF, 2 * LANES), jnp.float32),
            pltpu.SemaphoreType.DMA((2, 16)),
            pltpu.SemaphoreType.DMA((2, 16)),
            pltpu.SemaphoreType.DMA((8, 12)),
        ],
        cost_estimate=pl.CostEstimate(
            flops=2 * 1024 * D * 768, bytes_accessed=16 << 20, transcendentals=0
        ),
        name="project",
    )(place, line, *weights)


def reach_of(start, rows, ends_ref):
    position = start + lax.broadcasted_iota(jnp.int32, (rows, LANES), 0)
    first = jnp.zeros((rows, LANES), jnp.int32)
    for g in range(3):
        end = ends_ref[g]
        first = jnp.maximum(first, jnp.where(position >= end, end, 0))
    return position - first


def split_by_genome(start, ends_ref):
    cut = False
    for g in range(3):
        cut = cut | ((ends_ref[g] > start) & (ends_ref[g] < start + BLK))
    return cut


def short_mix(window_ref, reach, taps_ref, branch, rows, lanes):
    total = jnp.zeros((rows, LANES), jnp.float32)
    for j in range(SHORT):
        part = window_ref[TAIL - j : TAIL - j + rows, :]
        if reach is not None:
            part = jnp.where(reach >= j, part, 0.0)
        total = total + part * taps_ref[j, branch : branch + 1, lanes].astype(jnp.float32)
    return total


def product_kernel(start_ref, ends_ref, proj_ref, taps_ref, out_ref, low_ref, high_ref, k, v):
    start = start_ref[pl.program_id(0)]
    cut = split_by_genome(start, ends_ref)
    for part, tail_ref in enumerate((low_ref, high_ref)):
        lanes = pl.ds(part * LANES, LANES)
        k[:TAIL, :] = jnp.zeros((TAIL, LANES), jnp.float32)
        v[:TAIL, :] = jnp.zeros((TAIL, LANES), jnp.float32)
        k[TAIL:, :] = proj_ref[1, 0, :, lanes].astype(jnp.float32)
        v[TAIL:, :] = proj_ref[2, 0, :, lanes].astype(jnp.float32)

        def store(reach):
            mixed = short_mix(k, reach, taps_ref, 1, BLK, lanes)
            product = mixed * short_mix(v, reach, taps_ref, 2, BLK, lanes)
            first = lax.broadcasted_iota(jnp.int32, (BLK, LANES), 0) >= SHORT - 1
            out_ref[0, :, lanes] = jnp.where(first, product, 0.0).astype(jnp.bfloat16)

        @pl.when(cut)
        def _():
            store(reach_of(start, BLK, ends_ref))

        @pl.when(jnp.logical_not(cut))
        def _():
            store(None)

        tail_ref[0, :MED, :] = out_ref[0, BLK - MED :, lanes]
        for branch in range(3):
            at = MED + branch * TAIL
            tail_ref[0, at : at + TAIL, :] = proj_ref[branch, 0, BLK - TAIL :, lanes]


def products(starts, ends, proj, taps):
    tail = jax.ShapeDtypeStruct((4, HALO, LANES), jnp.bfloat16)
    tail_spec = pl.BlockSpec((1, HALO, LANES), lambda i, *_: (i, 0, 0))
    return pl.pallas_call(
        product_kernel,
        grid_spec=pltpu.PrefetchScalarGridSpec(
            num_scalar_prefetch=2,
            grid=(4,),
            in_specs=[
                pl.BlockSpec((3, 1, BLK, 2 * LANES), lambda i, *_: (0, i, 0, 0)),
                pl.BlockSpec((SHORT, 3, 2 * LANES), lambda i, *_: (0, 0, 0)),
            ],
            out_specs=(
                pl.BlockSpec((1, BLK, 2 * LANES), lambda i, *_: (i, 0, 0)), tail_spec, tail_spec,
            ),
            scratch_shapes=[pltpu.VMEM((BLK + TAIL, LANES), jnp.float32)] * 2,
        ),
        out_shape=(jax.ShapeDtypeStruct((4, BLK, 2 * LANES), jnp.bfloat16), tail, tail),
        cost_estimate=pl.CostEstimate(
            flops=60 << 20, bytes_accessed=4 << 20, transcendentals=0
        ),
        name="products",
    )(starts, ends, proj, taps)


def add_turn(total, shifted, weights, turn, at, first, last):
    part = total[first:last]
    for s in range(TAIL):
        tap = turn * TAIL + s
        part = part + shifted[s, at : at + last - first, :] * weights[tap : tap + 1, :]
    pieces = [total[:first]] * (first > 0) + [part] + [total[last:]] * (last < total.shape[0])
    return jnp.concatenate(pieces, axis=0) if len(pieces) > 1 else part


def each_genome(ends_ref, start, rows, body):
    def genome(g, carry):
        low = jnp.where(g == 0, 0, ends_ref[jnp.maximum(g - 1, 0)])
        high = ends_ref[g]

        @pl.when((low < start + rows) & (high > start))
        def _():
            body(low, high)

        return carry

    lax.fori_loop(0, 4, genome, 0)


def lanes_of(part):
    return pl.ds(pl.multiple_of(part * LANES, LANES), LANES)


def inner_kernel(index, start_ref, ends_ref, product_ref, medium_ref, out_ref, shifted):
    start = start_ref[index * 2 + pl.program_id(0)]
    row = start + lax.broadcasted_iota(jnp.int32, (BLK, LANES), 0)

    def segment(part, carry):
        lanes = lanes_of(part)

        def run(low, high):
            value = jnp.where(row >= low, product_ref[0, :, lanes].astype(jnp.float32), 0.0)
            for s in range(TAIL):
                shifted[s, :TAIL, :] = jnp.zeros((TAIL, LANES), jnp.float32)
                shifted[s, s:BLK, :] = value[: BLK - s, :]
            weights = medium_ref.at[:, lanes]
            for begin in (0, MED):
                total = jnp.zeros((MED, LANES), jnp.float32)
                for turn in range(MED // TAIL):
                    first = max(0, turn * TAIL - begin)
                    at = begin + first - turn * TAIL
                    total = add_turn(total, shifted, weights, turn, at, first, MED)
                rows = pl.ds(begin, MED)
                here = row[begin : begin + MED]
                inside = (here >= low) & (here < high)
                out_ref[0, rows, lanes] = jnp.where(inside, total, out_ref[0, rows, lanes])

        each_genome(ends_ref, start, BLK, run)
        return carry

    lax.fori_loop(0, 2, segment, 0)


def inner(index, starts, ends, product, medium):
    return pl.pallas_call(
        functools.partial(inner_kernel, index),
        grid_spec=pltpu.PrefetchScalarGridSpec(
            num_scalar_prefetch=2,
            grid=(2,),
            in_specs=[
                pl.BlockSpec((1, BLK, 2 * LANES), lambda i, *_: (index * 2 + i, 0, 0)),
                pl.BlockSpec((MED, 2 * LANES), lambda i, *_: (0, 0)),
            ],
            out_specs=pl.BlockSpec((1, BLK, 2 * LANES), lambda i, *_: (i, 0, 0)),
            scratch_shapes=[pltpu.VMEM((TAIL, BLK, LANES), jnp.float32)],
        ),
        out_shape=jax.ShapeDtypeStruct((2, BLK, 2 * LANES), jnp.float32),
        cost_estimate=pl.CostEstimate(
            flops=1024 * 256 * 128, bytes_accessed=1 << 20, transcendentals=0
        ),
        name="inner",
    )(starts, ends, product, medium)


def route_kernel(table_ref, *refs):
    ins, outs, every = refs[:8], refs[8:16], refs[16]
    for way in range(2):
        for d in range(4):
            every[d * 4 : (d + 1) * 4] = ins[way * 4 + d][...]
        for d in range(4):
            for j in range(4):
                outs[way * 4 + d][j] = every[table_ref[way, d, j]]


def route(table, ins):
    return pl.pallas_call(
        route_kernel,
        out_shape=(jax.ShapeDtypeStruct((4, HALO, LANES), jnp.bfloat16),) * 8,
        in_specs=[scalars()] + [full()] * 8,
        out_specs=(full(),) * 8,
        scratch_shapes=[pltpu.VMEM((16, HALO, LANES), jnp.bfloat16)],
        cost_estimate=pl.CostEstimate(flops=1 << 10, bytes_accessed=4 << 20, transcendentals=0),
        name="route",
    )(table, *ins)


def edge_kernel(
    start_ref, ends_ref, pick_ref, proj_ref, early_ref, late_ref, taps_ref, medium_ref, *refs
):
    halos, (out_ref, halo, window, small, prior, shifted, filtered) = refs[:8], refs[8:]
    block = pl.program_id(0)
    start = start_ref[block]
    cut = split_by_genome(start, ends_ref)
    near = MED + TAIL
    reach8 = reach_of(start, TAIL, ends_ref)
    row = start - MED + lax.broadcasted_iota(jnp.int32, (near, LANES), 0)
    out_row = start + lax.broadcasted_iota(jnp.int32, (near, LANES), 0)
    for part in range(2):
        for m in range(4):

            @pl.when(pick_ref[part, block] == m)
            def _(part=part, m=m):
                halo[part] = halos[part * 4 + m][0].astype(jnp.float32)

    @pl.when(block < 2)
    def _():
        filtered[...] = early_ref[0]

    @pl.when(block >= 2)
    def _():
        filtered[...] = late_ref[0]

    def segment(part, carry):
        lanes = lanes_of(part)
        taps = taps_ref.at[:, :, lanes]
        mixes = []
        for branch in (1, 2):
            at = MED + branch * TAIL
            small[:TAIL, :] = halo[part, at : at + TAIL, :]
            small[TAIL:, :] = proj_ref[branch, 0, : 2 * TAIL, lanes][:TAIL].astype(jnp.float32)
            mixes.append(short_mix(small, reach8, taps, branch, TAIL, slice(None)))
        first = lax.broadcasted_iota(jnp.int32, (TAIL, LANES), 0) < SHORT - 1
        early = (mixes[0] * mixes[1]).astype(jnp.bfloat16).astype(jnp.float32)
        prior[:MED, :] = halo[part, :MED, :]
        prior[MED:, :] = jnp.where(first, early, 0.0)

        def run(low, high):
            value = jnp.where(row >= low, prior[...], 0.0)
            for s in range(TAIL):
                shifted[s, near : near + TAIL, :] = jnp.zeros((TAIL, LANES), jnp.float32)
                shifted[s, s : s + near, :] = value
            weights = medium_ref.at[:, lanes]
            total = jnp.zeros((near, LANES), jnp.float32)
            for turn in range(MED // TAIL):
                last = min((turn + 2) * TAIL, near)
                at = MED - turn * TAIL
                total = add_turn(total, shifted, weights, turn, at, 0, last)
            inside = (out_row >= low) & (out_row < high)
            filtered[:near, lanes] += jnp.where(inside, total, 0.0)

        each_genome(ends_ref, start, near, run)
        window[:TAIL, :] = halo[part, MED : MED + TAIL, :]
        window[TAIL:, :] = proj_ref[0, 0, :, lanes].astype(jnp.float32)

        @pl.when(cut)
        def _():
            mixed = short_mix(window, reach_of(start, BLK, ends_ref), taps, 0, BLK, slice(None))
            out_ref[0, :, lanes] = (mixed * filtered[:, lanes]).astype(jnp.bfloat16)

        @pl.when(jnp.logical_not(cut))
        def _():
            head = short_mix(window, reach8, taps, 0, TAIL, slice(None))
            mixed = short_mix(window, None, taps, 0, BLK, slice(None))
            mixed = jnp.concatenate([head, mixed[TAIL:]], axis=0)
            out_ref[0, :, lanes] = (mixed * filtered[:, lanes]).astype(jnp.bfloat16)

        return carry

    lax.fori_loop(0, 2, segment, 0)


def edges(starts, ends, picks, proj, partials, taps, medium, halos):
    return pl.pallas_call(
        edge_kernel,
        grid_spec=pltpu.PrefetchScalarGridSpec(
            num_scalar_prefetch=3,
            grid=(4,),
            in_specs=[
                pl.BlockSpec((3, 1, BLK, 2 * LANES), lambda i, *_: (0, i, 0, 0)),
                pl.BlockSpec((1, BLK, 2 * LANES), lambda i, *_: (jnp.minimum(i, 1), 0, 0)),
                pl.BlockSpec((1, BLK, 2 * LANES), lambda i, *_: (jnp.maximum(i - 2, 0), 0, 0)),
                pl.BlockSpec((SHORT, 3, 2 * LANES), lambda i, *_: (0, 0, 0)),
                pl.BlockSpec((MED, 2 * LANES), lambda i, *_: (0, 0)),
            ]
            + [pl.BlockSpec((1, HALO, LANES), lambda i, *_: (i, 0, 0))] * 8,
            out_specs=pl.BlockSpec((1, BLK, 2 * LANES), lambda i, *_: (i, 0, 0)),
            scratch_shapes=[
                pltpu.VMEM((2, HALO, LANES), jnp.float32),
                pltpu.VMEM((BLK + TAIL, LANES), jnp.float32),
                pltpu.VMEM((2 * TAIL, LANES), jnp.float32),
                pltpu.VMEM((MED + TAIL, LANES), jnp.float32),
                pltpu.VMEM((TAIL, MED + 2 * TAIL, LANES), jnp.float32),
                pltpu.VMEM((BLK, 2 * LANES), jnp.float32),
            ],
        ),
        out_shape=jax.ShapeDtypeStruct((4, BLK, 2 * LANES), jnp.bfloat16),
        cost_estimate=pl.CostEstimate(
            flops=1024 * 256 * 64, bytes_accessed=3 << 20, transcendentals=0
        ),
        name="edges",
    )(starts, ends, picks, proj, *partials, taps, medium, *halos)


def assemble_kernel(place_ref, own_ref, other_ref, out_ref, sems):
    x, y, core = place_ref[0], place_ref[1], place_ref[2]
    started = []
    for other, ref in enumerate((own_ref, other_ref)):
        for dy in range(4):
            for dx in range(4):
                to_x, to_y = lax.rem(x + dx, 4), lax.rem(y + dy, 4)
                owner = to_x * 4 + (to_y // 2) * 2 + lax.rem(core + other, 2)
                rows = pl.ds(pl.multiple_of(owner * 16, 16), 16)
                started.append(
                    pltpu.make_async_copy(
                        ref.at[dy, dx], out_ref.at[lax.rem(to_y, 2), rows], sems.at[other, dy, dx]
                    )
                )
    for copy in started:
        copy.start()
    for copy in started:
        copy.wait()


def assemble(place, own, other):
    return pl.pallas_call(
        assemble_kernel,
        out_shape=jax.ShapeDtypeStruct((2, PIECE, D), jnp.bfloat16),
        in_specs=[scalars()] + [anywhere()] * 2,
        out_specs=full(),
        scratch_shapes=[pltpu.SemaphoreType.DMA((2, 4, 4))],
        cost_estimate=pl.CostEstimate(flops=1 << 10, bytes_accessed=8 << 20, transcendentals=0),
        name="assemble",
    )(place, own, other)


def output_kernel(
    side, place_ref, residual_ref, w_ref, gated_ref, out_ref, scratch, weights, sems, w_sem
):
    core, y_low = place_ref[2], place_ref[3]
    load = pltpu.make_async_copy(w_ref.at[lax.rem(y_low + side, 2)], weights, w_sem)
    load.start()

    def copies(i):
        made = []
        rows = pl.ds(pl.multiple_of(i * BLK, BLK), BLK)
        for k in range(16):
            source = gated_ref.at[k, lax.rem(core + k, 2), rows]
            target = scratch.at[rows, pl.ds(k * PIECE, PIECE)]
            made.append(pltpu.make_async_copy(source, target, sems.at[i, k]))
        return made

    def start(i, carry):
        for copy in copies(i):
            copy.start()
        return carry

    def step(i, carry):
        for copy in copies(i):
            copy.wait()
        rows = pl.ds(pl.multiple_of(i * BLK, BLK), BLK)
        summed = lax.dot_general(
            scratch[rows, :], weights[...], (((1,), (1,)), ((), ())),
            preferred_element_type=jnp.float32,
        )
        out_ref[rows, :] = (residual_ref[rows, :].astype(jnp.float32) + summed).astype(jnp.bfloat16)
        return carry

    lax.fori_loop(0, 2, start, 0)
    load.wait()
    lax.fori_loop(0, 2, step, 0)


def output(side, place, residual, weights, gated):
    return pl.pallas_call(
        functools.partial(output_kernel, side),
        out_shape=jax.ShapeDtypeStruct((HALF, PIECE), jnp.bfloat16),
        in_specs=[scalars(), full()] + [anywhere()] * 2,
        out_specs=full(),
        scratch_shapes=[
            pltpu.VMEM((HALF, D), jnp.bfloat16),
            pltpu.VMEM((PIECE, D), jnp.bfloat16),
            pltpu.SemaphoreType.DMA((2, 16)),
            pltpu.SemaphoreType.DMA,
        ],
        cost_estimate=pl.CostEstimate(
            flops=2 * HALF * D * PIECE, bytes_accessed=6 << 20, transcendentals=0
        ),
        name="output",
    )(place, residual, weights, gated)


def block(
    tokens,
    norm_gain,
    in_weight,
    short_filter,
    medium_filter,
    out_weight,
    genome_lengths,
    block_at_slot,
):
    seq, fsdp = lax.axis_index("seq"), lax.axis_index("fsdp")
    x, core, y_low, z = seq // 4, seq % 2, fsdp // 8, fsdp % 8
    y = ((seq // 2) % 2) * 2 + y_low

    values = tokens.astype(jnp.float32)
    gain = lax.dynamic_index_in_dim(norm_gain.reshape(16, 1, PIECE), fsdp, 0, keepdims=False)
    scaled = (values * gain.astype(jnp.float32)).astype(jnp.bfloat16)
    square = jnp.sum(values * values, axis=1)
    parts = []
    for _ in range(3):
        part = lax.reduce_precision(square, exponent_bits=8, mantissa_bits=7)
        parts.append(part.astype(jnp.bfloat16).reshape(2, 2, PIECE))
        square = square - part
    parts.append(jnp.zeros((2, 2, PIECE), jnp.bfloat16))
    packed = jnp.concatenate([scaled.reshape(2, HALF, PIECE)] + parts, axis=1)
    mine = jnp.where(y_low == 0, packed[0], packed[1])
    theirs = send(jnp.where(y_low == 0, packed[1], packed[0]), swap_y)
    pair = jnp.stack([mine, theirs])
    line = gather_line(pair)

    halves = in_weight.reshape(3, PIECE, 2, LANES)
    keep = jnp.where(core == 0, halves[:, :, 0], halves[:, :, 1])
    give = jnp.where(core == 0, halves[:, :, 1], halves[:, :, 0])
    other = send(give, swap_core)
    first = axis_of(keep, along_x)
    first, other = jnp.stack(first), jnp.stack(axis_of(other, along_y))
    weights = axis_of(first, along_y) + axis_of(other, along_x)

    place = jnp.stack([x, y, core, y_low, z]).astype(jnp.int32)

    proj = project(place, line, weights)

    both = jnp.concatenate([short_filter.reshape(SHORT * 3, PIECE), medium_filter], axis=0)
    both = jnp.where(core == 0, both[:, :LANES], both[:, LANES:])
    theirs = send(both, swap_y)
    both = jnp.concatenate(
        [jnp.where(y_low == 0, both, theirs), jnp.where(y_low == 0, theirs, both)], axis=1
    )
    taps = both[: SHORT * 3].reshape(SHORT, 3, 2 * LANES)
    medium = both[SHORT * 3 :].astype(jnp.float32)

    way = jnp.arange(2, dtype=jnp.int32).reshape(2, 1, 1, 1)
    ahead = jnp.arange(4, dtype=jnp.int32).reshape(1, 4, 1, 1)
    group = jnp.arange(2, dtype=jnp.int32).reshape(1, 1, 2, 1)
    index = jnp.arange(2, dtype=jnp.int32).reshape(1, 1, 1, 2)
    to_x, to_y = (x + way * ahead) % 4, (y + (1 - way) * ahead) % 4
    slots = (to_x * 4 + (to_y // 2) * 2 + (core + group) % 2) * 4 + (to_y % 2) * 2 + index
    slots = slots.reshape(32)
    all_slots = jnp.arange(block_at_slot.shape[0], dtype=jnp.int32)
    ids = jnp.sum(jnp.where(all_slots == slots[:, None], block_at_slot, 0), axis=1)
    previous = jnp.maximum(ids - 1, 0)
    before = jnp.sum(jnp.where(block_at_slot == previous[:, None], all_slots, 0), axis=1)
    before = before.reshape(2, 4, 4)
    from_x, from_y = before // 16, ((before // 8) % 2) * 2 + (before // 2) % 2
    local = ((before // 4 + core) % 2) * 2 + before % 2
    dx, dy = (from_x - x) % 4, (from_y - y) % 4
    table = jnp.stack(
        [jnp.where(dy[0] == 0, dx[0] * 4, 0) + local[0],
         jnp.where(dx[1] == 0, dy[1] * 4, 0) + local[1]]
    ).astype(jnp.int32)
    picks = jnp.stack([dy[0, 0], dx[1, 0]]).astype(jnp.int32)
    starts = (ids[:4] * BLK).astype(jnp.int32)
    ends = jnp.cumsum(genome_lengths).astype(jnp.int32)

    product, low, high = products(starts, ends, proj, taps)
    rows_x, rows_y = axis_of(low, along_x), axis_of(high, along_y)
    partials = [inner(i, starts, ends, product, medium) for i in range(2)]
    table, partials[0] = lax.optimization_barrier((table, partials[0]))
    routed = route(table, rows_x + rows_y)
    halos = [routed[0]] + [send(routed[4 - d], along_y(4 - d)) for d in range(1, 4)]
    halos += [routed[4]] + [send(routed[8 - d], along_x(4 - d)) for d in range(1, 4)]

    rows = tokens.reshape(2, HALF, PIECE)
    residual = send(jnp.where(y_low == 0, rows[1], rows[0]), swap_y)
    mine = jnp.where(y_low == 0, rows[0], rows[1])
    gated = edges(starts, ends, picks, proj, partials, taps, medium, halos)
    columns = out_weight.reshape(2, 8, 2, LANES, 16).transpose(4, 1, 2, 0, 3).reshape(16, D)
    columns = lax.optimization_barrier((columns, gated))[0]
    columns = jnp.stack(axis_of(columns, along_x))
    gathered = gather_line(gated.reshape(2, HALF, 2 * LANES))
    columns = jnp.stack(axis_of(columns, along_y))
    columns = assemble(place, columns, send(columns, swap_core))
    theirs = output(1, place, residual, columns, gathered)
    place, theirs = lax.optimization_barrier((place, theirs))
    theirs = send(theirs, swap_y)
    ours = output(0, place, mine, columns, gathered)
    first = jnp.where(y_low == 0, ours, theirs)
    second = jnp.where(y_low == 0, theirs, ours)
    return jnp.concatenate([first, second], axis=0)


def solution(mesh):
    in_specs = (
        P("seq", "fsdp"),
        P(),
        P(None, "seq", "fsdp"),
        P(None, None, "fsdp"),
        P(None, "fsdp"),
        P(None, ("fsdp", "seq")),
        P(),
        P(),
    )
    out_specs = P("seq", "fsdp")
    return jax.shard_map(block, mesh=mesh, in_specs=in_specs, out_specs=out_specs, check_vma=False)
```

```python
import functools

import jax
import jax.numpy as jnp
from jax import lax
from jax.experimental import pallas as pl
from jax.experimental.pallas import tpu as pltpu
from jax.sharding import PartitionSpec as P


BLK = 256
SHORT = 7
MED = 128
LANES = 128
TAIL = 8
HALF = 512
PIECE = 256
D = 4096
HALO = MED + 3 * TAIL
AXES = ("seq", "fsdp")
epsilon = 1e-06


def linear(x, y, z, core):
    return (x * 4 + (y // 2) * 2 + core) * 16 + (y % 2) * 8 + z


def permutation(move):
    pairs = []
    for x in range(4):
        for y in range(4):
            for z in range(8):
                for core in range(2):
                    pairs.append((linear(x, y, z, core), linear(*move(x, y, z, core))))
    return pairs


def send(value, move):
    return lax.ppermute(value, AXES, permutation(move))


def along_x(step):
    return lambda x, y, z, core: ((x + step) % 4, y, z, core)


def along_y(step):
    return lambda x, y, z, core: (x, (y + step) % 4, z, core)


def swap_y(x, y, z, core):
    return (x, y ^ 1, z, core)


def swap_core(x, y, z, core):
    return (x, y, z, core ^ 1)


def gather_line(value):
    groups = [
        [linear(x, y, z, core) for z in range(8) for core in range(2)]
        for x in range(4)
        for y in range(4)
    ]
    return lax.all_gather(value, AXES, axis=0, axis_index_groups=groups)


def axis_of(chunk, along):
    return [chunk] + [send(chunk, along(-d)) for d in range(1, 4)]


def anywhere():
    return pl.BlockSpec(memory_space=pl.ANY)


def full():
    return pl.BlockSpec(memory_space=pltpu.VMEM)


def scalars():
    return pl.BlockSpec(memory_space=pltpu.SMEM)


def project_kernel(place_ref, line_ref, *refs):
    weights = refs[:8]
    out_ref, x_scratch, s_scratch, w_scratch, total, x_sems, s_sems, w_sems = refs[8:]
    x, y, core, y_low = place_ref[0], place_ref[1], place_ref[2], place_ref[3]

    def row_copies(i):
        made = []
        group, z = i // 8, lax.rem(i, 8)
        source = z * 2 + lax.rem(core + group, 2)
        rows = pl.ds(pl.multiple_of(group * HALF, HALF), HALF)
        for p in range(2):
            lanes = pl.ds(pl.multiple_of((z * 2 + p) * PIECE, PIECE), PIECE)
            made.append(
                pltpu.make_async_copy(
                    line_ref.at[source, p, pl.ds(0, HALF)], x_scratch.at[rows, lanes],
                    x_sems.at[p, i],
                )
            )
            made.append(
                pltpu.make_async_copy(
                    line_ref.at[source, p, pl.ds(HALF, TAIL)], s_scratch.at[group, z * 2 + p],
                    s_sems.at[p, i],
                )
            )
        return made

    def weight_copies(i):
        made = []
        branch, b = i // 4, lax.rem(i, 4)
        for other in range(2):
            for a in range(4):
                dx, dy = (b, a) if other == 0 else (a, b)
                to_x, to_y = lax.rem(x + dx, 4), lax.rem(y + dy, 4)
                owner = to_x * 4 + (to_y // 2) * 2 + lax.rem(core + other, 2)
                turn = lax.rem(owner, 8) * 2 + lax.rem(owner // 8 + y_low, 2)
                rows = pl.ds(pl.multiple_of(turn * PIECE, PIECE), PIECE)
                lanes = pl.ds(pl.multiple_of(lax.rem(to_y, 2) * LANES, LANES), LANES)
                made.append(
                    pltpu.make_async_copy(
                        weights[other * 4 + a].at[b, branch],
                        w_scratch.at[branch, rows, lanes],
                        w_sems.at[other * 4 + a, i],
                    )
                )
        return made

    def start(copies, first, last):
        def one(i, carry):
            for copy in copies(i):
                copy.start()
            return carry

        lax.fori_loop(first, last, one, 0)

    def finish(copies, first, last):
        def one(i, carry):
            for copy in copies(i):
                copy.wait()
            return carry

        lax.fori_loop(first, last, one, 0)

    start(row_copies, 0, 8)
    start(weight_copies, 0, 4)
    start(row_copies, 8, 16)
    start(weight_copies, 4, 12)

    def step(i, carry):
        branch, group = i // 2, lax.rem(i, 2)

        @pl.when(i < 2)
        def _():
            finish(row_copies, i * 8, i * 8 + 8)

        @pl.when(group == 0)
        def _():
            finish(weight_copies, branch * 4, branch * 4 + 4)

        rows = pl.ds(pl.multiple_of(group * HALF, HALF), HALF)
        total[branch, rows, :] = jnp.dot(
            x_scratch[rows, :], w_scratch[branch], preferred_element_type=jnp.float32
        )
        return carry

    lax.fori_loop(0, 6, step, 0)
    for group in range(2):
        square = jnp.sum(s_scratch[group].astype(jnp.float32), axis=0)
        for i in range(2):
            row = square[i : i + 1] + square[i + 2 : i + 3] + square[i + 4 : i + 5]
            scale = lax.rsqrt(row / D + epsilon)
            scale = jnp.transpose(jnp.broadcast_to(scale, (LANES, PIECE)))
            scale = jnp.concatenate([scale, scale], axis=1)
            block = group * 2 + i

            def write(branch, carry, block=block, scale=scale):
                value = total[branch, block * BLK : (block + 1) * BLK, :]
                out_ref[branch, block] = (value * scale).astype(jnp.bfloat16)
                return carry

            lax.fori_loop(0, 3, write, 0)


def project(place, line, weights):
    return pl.pallas_call(
        project_kernel,
        out_shape=jax.ShapeDtypeStruct((3, 4, BLK, 2 * LANES), jnp.bfloat16),
        in_specs=[scalars()] + [anywhere()] * 9,
        out_specs=full(),
        scratch_shapes=[
            pltpu.VMEM((2 * HALF, D), jnp.bfloat16),
            pltpu.VMEM((2, 16, TAIL, PIECE), jnp.bfloat16),
            pltpu.VMEM((3, D, 2 * LANES), jnp.bfloat16),
            pltpu.VMEM((3, 2 * HALF, 2 * LANES), jnp.float32),
            pltpu.SemaphoreType.DMA((2, 16)),
            pltpu.SemaphoreType.DMA((2, 16)),
            pltpu.SemaphoreType.DMA((8, 12)),
        ],
        cost_estimate=pl.CostEstimate(
            flops=2 * 1024 * D * 768, bytes_accessed=16 << 20, transcendentals=0
        ),
        name="project",
    )(place, line, *weights)


def reach_of(start, rows, ends_ref):
    position = start + lax.broadcasted_iota(jnp.int32, (rows, LANES), 0)
    first = jnp.zeros((rows, LANES), jnp.int32)
    for g in range(3):
        end = ends_ref[g]
        first = jnp.maximum(first, jnp.where(position >= end, end, 0))
    return position - first


def split_by_genome(start, ends_ref):
    cut = False
    for g in range(3):
        cut = cut | ((ends_ref[g] > start) & (ends_ref[g] < start + BLK))
    return cut


def short_mix(window_ref, reach, taps_ref, branch, rows, lanes):
    total = jnp.zeros((rows, LANES), jnp.float32)
    for j in range(SHORT):
        part = window_ref[TAIL - j : TAIL - j + rows, :]
        if reach is not None:
            part = jnp.where(reach >= j, part, 0.0)
        total = total + part * taps_ref[j, branch : branch + 1, lanes].astype(jnp.float32)
    return total


def product_kernel(start_ref, ends_ref, proj_ref, taps_ref, out_ref, low_ref, high_ref, k, v):
    start = start_ref[pl.program_id(0)]
    cut = split_by_genome(start, ends_ref)
    for part, tail_ref in enumerate((low_ref, high_ref)):
        lanes = pl.ds(part * LANES, LANES)
        k[:TAIL, :] = jnp.zeros((TAIL, LANES), jnp.float32)
        v[:TAIL, :] = jnp.zeros((TAIL, LANES), jnp.float32)
        k[TAIL:, :] = proj_ref[1, 0, :, lanes].astype(jnp.float32)
        v[TAIL:, :] = proj_ref[2, 0, :, lanes].astype(jnp.float32)

        def store(reach):
            mixed = short_mix(k, reach, taps_ref, 1, BLK, lanes)
            product = mixed * short_mix(v, reach, taps_ref, 2, BLK, lanes)
            first = lax.broadcasted_iota(jnp.int32, (BLK, LANES), 0) >= SHORT - 1
            out_ref[0, :, lanes] = jnp.where(first, product, 0.0).astype(jnp.bfloat16)

        @pl.when(cut)
        def _():
            store(reach_of(start, BLK, ends_ref))

        @pl.when(jnp.logical_not(cut))
        def _():
            store(None)

        tail_ref[0, :MED, :] = out_ref[0, BLK - MED :, lanes]
        for branch in range(3):
            at = MED + branch * TAIL
            tail_ref[0, at : at + TAIL, :] = proj_ref[branch, 0, BLK - TAIL :, lanes]


def products(starts, ends, proj, taps):
    tail = jax.ShapeDtypeStruct((4, HALO, LANES), jnp.bfloat16)
    tail_spec = pl.BlockSpec((1, HALO, LANES), lambda i, *_: (i, 0, 0))
    return pl.pallas_call(
        product_kernel,
        grid_spec=pltpu.PrefetchScalarGridSpec(
            num_scalar_prefetch=2,
            grid=(4,),
            in_specs=[
                pl.BlockSpec((3, 1, BLK, 2 * LANES), lambda i, *_: (0, i, 0, 0)),
                pl.BlockSpec((SHORT, 3, 2 * LANES), lambda i, *_: (0, 0, 0)),
            ],
            out_specs=(
                pl.BlockSpec((1, BLK, 2 * LANES), lambda i, *_: (i, 0, 0)), tail_spec, tail_spec,
            ),
            scratch_shapes=[pltpu.VMEM((BLK + TAIL, LANES), jnp.float32)] * 2,
        ),
        out_shape=(jax.ShapeDtypeStruct((4, BLK, 2 * LANES), jnp.bfloat16), tail, tail),
        cost_estimate=pl.CostEstimate(
            flops=60 << 20, bytes_accessed=4 << 20, transcendentals=0
        ),
        name="products",
    )(starts, ends, proj, taps)


def add_turn(total, shifted, weights, turn, at, first, last):
    part = total[first:last]
    for s in range(TAIL):
        tap = turn * TAIL + s
        part = part + shifted[s, at : at + last - first, :] * weights[tap : tap + 1, :]
    pieces = [total[:first]] * (first > 0) + [part] + [total[last:]] * (last < total.shape[0])
    return jnp.concatenate(pieces, axis=0) if len(pieces) > 1 else part


def each_genome(ends_ref, start, rows, body):
    def genome(g, carry):
        low = jnp.where(g == 0, 0, ends_ref[jnp.maximum(g - 1, 0)])
        high = ends_ref[g]

        @pl.when((low < start + rows) & (high > start))
        def _():
            body(low, high)

        return carry

    lax.fori_loop(0, 4, genome, 0)


def lanes_of(part):
    return pl.ds(pl.multiple_of(part * LANES, LANES), LANES)


def inner_kernel(index, start_ref, ends_ref, product_ref, medium_ref, out_ref, shifted):
    start = start_ref[index * 2 + pl.program_id(0)]
    row = start + lax.broadcasted_iota(jnp.int32, (BLK, LANES), 0)

    def segment(part, carry):
        lanes = lanes_of(part)

        def run(low, high):
            value = jnp.where(row >= low, product_ref[0, :, lanes].astype(jnp.float32), 0.0)
            for s in range(TAIL):
                shifted[s, :TAIL, :] = jnp.zeros((TAIL, LANES), jnp.float32)
                shifted[s, s:BLK, :] = value[: BLK - s, :]
            weights = medium_ref.at[:, lanes]
            for begin in (0, MED):
                total = jnp.zeros((MED, LANES), jnp.float32)
                for turn in range(MED // TAIL):
                    first = max(0, turn * TAIL - begin)
                    at = begin + first - turn * TAIL
                    total = add_turn(total, shifted, weights, turn, at, first, MED)
                rows = pl.ds(begin, MED)
                here = row[begin : begin + MED]
                inside = (here >= low) & (here < high)
                out_ref[0, rows, lanes] = jnp.where(inside, total, out_ref[0, rows, lanes])

        each_genome(ends_ref, start, BLK, run)
        return carry

    lax.fori_loop(0, 2, segment, 0)


def inner(index, starts, ends, product, medium):
    return pl.pallas_call(
        functools.partial(inner_kernel, index),
        grid_spec=pltpu.PrefetchScalarGridSpec(
            num_scalar_prefetch=2,
            grid=(2,),
            in_specs=[
                pl.BlockSpec((1, BLK, 2 * LANES), lambda i, *_: (index * 2 + i, 0, 0)),
                pl.BlockSpec((MED, 2 * LANES), lambda i, *_: (0, 0)),
            ],
            out_specs=pl.BlockSpec((1, BLK, 2 * LANES), lambda i, *_: (i, 0, 0)),
            scratch_shapes=[pltpu.VMEM((TAIL, BLK, LANES), jnp.float32)],
        ),
        out_shape=jax.ShapeDtypeStruct((2, BLK, 2 * LANES), jnp.float32),
        cost_estimate=pl.CostEstimate(
            flops=1024 * 256 * 128, bytes_accessed=1 << 20, transcendentals=0
        ),
        name="inner",
    )(starts, ends, product, medium)


def route_kernel(table_ref, *refs):
    ins, outs, every = refs[:8], refs[8:16], refs[16]
    for way in range(2):
        for d in range(4):
            every[d * 4 : (d + 1) * 4] = ins[way * 4 + d][...]
        for d in range(4):
            for j in range(4):
                outs[way * 4 + d][j] = every[table_ref[way, d, j]]


def route(table, ins):
    return pl.pallas_call(
        route_kernel,
        out_shape=(jax.ShapeDtypeStruct((4, HALO, LANES), jnp.bfloat16),) * 8,
        in_specs=[scalars()] + [full()] * 8,
        out_specs=(full(),) * 8,
        scratch_shapes=[pltpu.VMEM((16, HALO, LANES), jnp.bfloat16)],
        cost_estimate=pl.CostEstimate(flops=1 << 10, bytes_accessed=4 << 20, transcendentals=0),
        name="route",
    )(table, *ins)


def edge_kernel(
    start_ref, ends_ref, pick_ref, proj_ref, early_ref, late_ref, taps_ref, medium_ref, *refs
):
    halos, (out_ref, halo, window, small, prior, shifted, filtered) = refs[:8], refs[8:]
    block = pl.program_id(0)
    start = start_ref[block]
    cut = split_by_genome(start, ends_ref)
    near = MED + TAIL
    reach8 = reach_of(start, TAIL, ends_ref)
    row = start - MED + lax.broadcasted_iota(jnp.int32, (near, LANES), 0)
    out_row = start + lax.broadcasted_iota(jnp.int32, (near, LANES), 0)
    for part in range(2):
        for m in range(4):

            @pl.when(pick_ref[part, block] == m)
            def _(part=part, m=m):
                halo[part] = halos[part * 4 + m][0].astype(jnp.float32)

    @pl.when(block < 2)
    def _():
        filtered[...] = early_ref[0]

    @pl.when(block >= 2)
    def _():
        filtered[...] = late_ref[0]

    def segment(part, carry):
        lanes = lanes_of(part)
        taps = taps_ref.at[:, :, lanes]
        mixes = []
        for branch in (1, 2):
            at = MED + branch * TAIL
            small[:TAIL, :] = halo[part, at : at + TAIL, :]
            small[TAIL:, :] = proj_ref[branch, 0, : 2 * TAIL, lanes][:TAIL].astype(jnp.float32)
            mixes.append(short_mix(small, reach8, taps, branch, TAIL, slice(None)))
        first = lax.broadcasted_iota(jnp.int32, (TAIL, LANES), 0) < SHORT - 1
        early = (mixes[0] * mixes[1]).astype(jnp.bfloat16).astype(jnp.float32)
        prior[:MED, :] = halo[part, :MED, :]
        prior[MED:, :] = jnp.where(first, early, 0.0)

        def run(low, high):
            value = jnp.where(row >= low, prior[...], 0.0)
            for s in range(TAIL):
                shifted[s, near : near + TAIL, :] = jnp.zeros((TAIL, LANES), jnp.float32)
                shifted[s, s : s + near, :] = value
            weights = medium_ref.at[:, lanes]
            total = jnp.zeros((near, LANES), jnp.float32)
            for turn in range(MED // TAIL):
                last = min((turn + 2) * TAIL, near)
                at = MED - turn * TAIL
                total = add_turn(total, shifted, weights, turn, at, 0, last)
            inside = (out_row >= low) & (out_row < high)
            filtered[:near, lanes] += jnp.where(inside, total, 0.0)

        each_genome(ends_ref, start, near, run)
        window[:TAIL, :] = halo[part, MED : MED + TAIL, :]
        window[TAIL:, :] = proj_ref[0, 0, :, lanes].astype(jnp.float32)

        @pl.when(cut)
        def _():
            mixed = short_mix(window, reach_of(start, BLK, ends_ref), taps, 0, BLK, slice(None))
            out_ref[0, :, lanes] = (mixed * filtered[:, lanes]).astype(jnp.bfloat16)

        @pl.when(jnp.logical_not(cut))
        def _():
            head = short_mix(window, reach8, taps, 0, TAIL, slice(None))
            mixed = short_mix(window, None, taps, 0, BLK, slice(None))
            mixed = jnp.concatenate([head, mixed[TAIL:]], axis=0)
            out_ref[0, :, lanes] = (mixed * filtered[:, lanes]).astype(jnp.bfloat16)

        return carry

    lax.fori_loop(0, 2, segment, 0)


def edges(starts, ends, picks, proj, partials, taps, medium, halos):
    return pl.pallas_call(
        edge_kernel,
        grid_spec=pltpu.PrefetchScalarGridSpec(
            num_scalar_prefetch=3,
            grid=(4,),
            in_specs=[
                pl.BlockSpec((3, 1, BLK, 2 * LANES), lambda i, *_: (0, i, 0, 0)),
                pl.BlockSpec((1, BLK, 2 * LANES), lambda i, *_: (jnp.minimum(i, 1), 0, 0)),
                pl.BlockSpec((1, BLK, 2 * LANES), lambda i, *_: (jnp.maximum(i - 2, 0), 0, 0)),
                pl.BlockSpec((SHORT, 3, 2 * LANES), lambda i, *_: (0, 0, 0)),
                pl.BlockSpec((MED, 2 * LANES), lambda i, *_: (0, 0)),
            ]
            + [pl.BlockSpec((1, HALO, LANES), lambda i, *_: (i, 0, 0))] * 8,
            out_specs=pl.BlockSpec((1, BLK, 2 * LANES), lambda i, *_: (i, 0, 0)),
            scratch_shapes=[
                pltpu.VMEM((2, HALO, LANES), jnp.float32),
                pltpu.VMEM((BLK + TAIL, LANES), jnp.float32),
                pltpu.VMEM((2 * TAIL, LANES), jnp.float32),
                pltpu.VMEM((MED + TAIL, LANES), jnp.float32),
                pltpu.VMEM((TAIL, MED + 2 * TAIL, LANES), jnp.float32),
                pltpu.VMEM((BLK, 2 * LANES), jnp.float32),
            ],
        ),
        out_shape=jax.ShapeDtypeStruct((4, BLK, 2 * LANES), jnp.bfloat16),
        cost_estimate=pl.CostEstimate(
            flops=1024 * 256 * 64, bytes_accessed=3 << 20, transcendentals=0
        ),
        name="edges",
    )(starts, ends, picks, proj, *partials, taps, medium, *halos)


def assemble_kernel(place_ref, own_ref, other_ref, out_ref, scratch, sems):
    x, y, core = place_ref[0], place_ref[1], place_ref[2]
    started = []
    for other, ref in enumerate((own_ref, other_ref)):
        for dy in range(4):
            for dx in range(4):
                to_x, to_y = lax.rem(x + dx, 4), lax.rem(y + dy, 4)
                owner = to_x * 4 + (to_y // 2) * 2 + lax.rem(core + other, 2)
                rows = pl.ds(pl.multiple_of(owner * 16, 16), 16)
                started.append(
                    pltpu.make_async_copy(
                        ref.at[dy, dx], scratch.at[lax.rem(to_y, 2), rows], sems.at[other, dy, dx]
                    )
                )
    for copy in started:
        copy.start()
    for copy in started:
        copy.wait()

    def turn(i, carry):
        lanes = pl.ds(pl.multiple_of(i * PIECE, PIECE), PIECE)
        for column in range(2):
            value = scratch[column, :, lanes].astype(jnp.float32)
            out_ref[column, lanes, :] = jnp.transpose(value).astype(jnp.bfloat16)
        return carry

    lax.fori_loop(0, D // PIECE, turn, 0)


def assemble(place, own, other):
    return pl.pallas_call(
        assemble_kernel,
        out_shape=jax.ShapeDtypeStruct((2, D, PIECE), jnp.bfloat16),
        in_specs=[scalars()] + [anywhere()] * 2,
        out_specs=full(),
        scratch_shapes=[
            pltpu.VMEM((2, PIECE, D), jnp.bfloat16), pltpu.SemaphoreType.DMA((2, 4, 4)),
        ],
        cost_estimate=pl.CostEstimate(flops=1 << 10, bytes_accessed=8 << 20, transcendentals=0),
        name="assemble",
    )(place, own, other)


def output_kernel(
    side, place_ref, residual_ref, w_ref, gated_ref, out_ref, scratch, weights, sems, w_sem
):
    core, y_low = place_ref[2], place_ref[3]
    load = pltpu.make_async_copy(w_ref.at[lax.rem(y_low + side, 2)], weights, w_sem)
    load.start()

    def copies(i):
        made = []
        rows = pl.ds(pl.multiple_of(i * BLK, BLK), BLK)
        for k in range(16):
            source = gated_ref.at[k, lax.rem(core + k, 2), rows]
            target = scratch.at[rows, pl.ds(k * PIECE, PIECE)]
            made.append(pltpu.make_async_copy(source, target, sems.at[i, k]))
        return made

    def start(i, carry):
        for copy in copies(i):
            copy.start()
        return carry

    def step(i, carry):
        for copy in copies(i):
            copy.wait()
        rows = pl.ds(pl.multiple_of(i * BLK, BLK), BLK)
        summed = jnp.dot(scratch[rows, :], weights[...], preferred_element_type=jnp.float32)
        value = (residual_ref[rows, :].astype(jnp.float32) + summed).astype(jnp.bfloat16)
        if side == 0:
            out_ref[y_low, rows, :] = value
        else:
            out_ref[rows, :] = value
        return carry

    lax.fori_loop(0, 2, start, 0)
    load.wait()
    lax.fori_loop(0, 2, step, 0)


def output(side, place, residual, weights, gated):
    return pl.pallas_call(
        functools.partial(output_kernel, side),
        out_shape=jax.ShapeDtypeStruct(
            (2, HALF, PIECE) if side == 0 else (HALF, PIECE), jnp.bfloat16
        ),
        in_specs=[scalars(), full()] + [anywhere()] * 2,
        out_specs=full(),
        scratch_shapes=[
            pltpu.VMEM((HALF, D), jnp.bfloat16),
            pltpu.VMEM((D, PIECE), jnp.bfloat16),
            pltpu.SemaphoreType.DMA((2, 16)),
            pltpu.SemaphoreType.DMA,
        ],
        cost_estimate=pl.CostEstimate(
            flops=2 * HALF * D * PIECE, bytes_accessed=6 << 20, transcendentals=0
        ),
        name="output",
    )(place, residual, weights, gated)


def block(
    tokens,
    norm_gain,
    in_weight,
    short_filter,
    medium_filter,
    out_weight,
    genome_lengths,
    block_at_slot,
):
    seq, fsdp = lax.axis_index("seq"), lax.axis_index("fsdp")
    x, core, y_low, z = seq // 4, seq % 2, fsdp // 8, fsdp % 8
    y = ((seq // 2) % 2) * 2 + y_low

    values = tokens.astype(jnp.float32)
    gain = lax.dynamic_index_in_dim(norm_gain.reshape(16, 1, PIECE), fsdp, 0, keepdims=False)
    scaled = (values * gain.astype(jnp.float32)).astype(jnp.bfloat16)
    square = jnp.sum(values * values, axis=1)
    parts = []
    for _ in range(3):
        part = lax.reduce_precision(square, exponent_bits=8, mantissa_bits=7)
        parts.append(part.astype(jnp.bfloat16).reshape(2, 2, PIECE))
        square = square - part
    parts.append(jnp.zeros((2, 2, PIECE), jnp.bfloat16))
    packed = jnp.concatenate([scaled.reshape(2, HALF, PIECE)] + parts, axis=1)
    mine = jnp.where(y_low == 0, packed[0], packed[1])
    theirs = send(jnp.where(y_low == 0, packed[1], packed[0]), swap_y)
    pair = jnp.stack([mine, theirs])
    line = gather_line(pair)

    halves = in_weight.reshape(3, PIECE, 2, LANES)
    keep = jnp.where(core == 0, halves[:, :, 0], halves[:, :, 1])
    give = jnp.where(core == 0, halves[:, :, 1], halves[:, :, 0])
    other = send(give, swap_core)
    first = axis_of(keep, along_x)
    first, other = jnp.stack(first), jnp.stack(axis_of(other, along_y))
    weights = axis_of(first, along_y) + axis_of(other, along_x)

    place = jnp.stack([x, y, core, y_low, z]).astype(jnp.int32)

    proj = project(place, line, weights)

    both = jnp.concatenate([short_filter.reshape(SHORT * 3, PIECE), medium_filter], axis=0)
    both = jnp.where(core == 0, both[:, :LANES], both[:, LANES:])
    theirs = send(both, swap_y)
    both = jnp.concatenate(
        [jnp.where(y_low == 0, both, theirs), jnp.where(y_low == 0, theirs, both)], axis=1
    )
    taps = both[: SHORT * 3].reshape(SHORT, 3, 2 * LANES)
    medium = both[SHORT * 3 :].astype(jnp.float32)

    way = jnp.arange(2, dtype=jnp.int32).reshape(2, 1, 1, 1)
    ahead = jnp.arange(4, dtype=jnp.int32).reshape(1, 4, 1, 1)
    group = jnp.arange(2, dtype=jnp.int32).reshape(1, 1, 2, 1)
    index = jnp.arange(2, dtype=jnp.int32).reshape(1, 1, 1, 2)
    to_x, to_y = (x + way * ahead) % 4, (y + (1 - way) * ahead) % 4
    slots = (to_x * 4 + (to_y // 2) * 2 + (core + group) % 2) * 4 + (to_y % 2) * 2 + index
    slots = slots.reshape(32)
    all_slots = jnp.arange(block_at_slot.shape[0], dtype=jnp.int32)
    ids = jnp.sum(jnp.where(all_slots == slots[:, None], block_at_slot, 0), axis=1)
    previous = jnp.maximum(ids - 1, 0)
    before = jnp.sum(jnp.where(block_at_slot == previous[:, None], all_slots, 0), axis=1)
    before = before.reshape(2, 4, 4)
    from_x, from_y = before // 16, ((before // 8) % 2) * 2 + (before // 2) % 2
    local = ((before // 4 + core) % 2) * 2 + before % 2
    dx, dy = (from_x - x) % 4, (from_y - y) % 4
    table = jnp.stack(
        [jnp.where(dy[0] == 0, dx[0] * 4, 0) + local[0],
         jnp.where(dx[1] == 0, dy[1] * 4, 0) + local[1]]
    ).astype(jnp.int32)
    picks = jnp.stack([dy[0, 0], dx[1, 0]]).astype(jnp.int32)
    starts = (ids[:4] * BLK).astype(jnp.int32)
    ends = jnp.cumsum(genome_lengths).astype(jnp.int32)

    product, low, high = products(starts, ends, proj, taps)
    rows_x, rows_y = axis_of(low, along_x), axis_of(high, along_y)
    partials = [inner(i, starts, ends, product, medium) for i in range(2)]
    table, partials[0] = lax.optimization_barrier((table, partials[0]))
    routed = route(table, rows_x + rows_y)
    halos = [routed[0]] + [send(routed[4 - d], along_y(4 - d)) for d in range(1, 4)]
    halos += [routed[4]] + [send(routed[8 - d], along_x(4 - d)) for d in range(1, 4)]

    rows = tokens.reshape(2, HALF, PIECE)
    residual = send(jnp.where(y_low == 0, rows[1], rows[0]), swap_y)
    mine = jnp.where(y_low == 0, rows[0], rows[1])
    gated = edges(starts, ends, picks, proj, partials, taps, medium, halos)
    columns = out_weight.reshape(2, 8, 2, LANES, 16).transpose(4, 1, 2, 0, 3).reshape(16, D)
    columns = lax.optimization_barrier((columns, gated))[0]
    columns = jnp.stack(axis_of(columns, along_x))
    gathered = gather_line(gated.reshape(2, HALF, 2 * LANES))
    columns = jnp.stack(axis_of(columns, along_y))
    columns = assemble(place, columns, send(columns, swap_core))
    theirs = output(1, place, residual, columns, gathered)
    place, theirs = lax.optimization_barrier((place, theirs))
    theirs = send(theirs, swap_y)
    ours = output(0, place, mine, columns, gathered)
    ours = lax.dynamic_update_index_in_dim(ours, theirs, 1 - y_low, 0)
    return ours.reshape(2 * HALF, PIECE)


def solution(mesh):
    in_specs = (
        P("seq", "fsdp"),
        P(),
        P(None, "seq", "fsdp"),
        P(None, None, "fsdp"),
        P(None, "fsdp"),
        P(None, ("fsdp", "seq")),
        P(),
        P(),
    )
    out_specs = P("seq", "fsdp")
    return jax.shard_map(block, mesh=mesh, in_specs=in_specs, out_specs=out_specs, check_vma=False)
```
